512 devices in a mesh: ctx: 64 (over y, z), tp: 8 (over x, core).
Axes of the slice: x: 4, y: 4, z: 16, core: 2. Of those that a mesh axis runs over, the one named last changes fastest.
Arguments:
- inputs: bfloat16 [3, 16384, 8192], P(None, 'ctx', 'tp'), may hold values from -6 to 6
- cotangent: bfloat16 [16384, 8192], P('ctx', 'tp'), may hold values from -140 to 140
- short_filter: float32 [3, 7, 8192], P(None, None, 'tp'), may hold values from -2 to 2
- residue: float32 [16, 8192], P(None, 'tp'), may hold values from -0.22 to 0.22
- decay_rate: float32 [16, 8192], P(None, 'tp'), may hold values from 6.1035156e-06 to 0.04
Outputs:
- grad_inputs: bfloat16 [3, 16384, 8192], P(None, 'ctx', 'tp')
- grad_short: float32 [3, 7, 8192], P(None, None, 'tp')
The draws below stay inside these ranges and needn't reach their ends.
All inputs are finite; a program needn't handle non-finite values.
Results may differ from the reference program's by a relative error of at most 0.0057.
Values may be sent and summed in bfloat16 or wider, within the bound.
No kernel may reach another device: no remote copies, remote signals or barrier semaphores. Data moves between devices by JAX's collectives and lax.ppermute only.
A program may use at most 128 MiB of HBM per device.

```python
import math
import jax
import jax.numpy as jnp
from jax import lax

C = 8192
SHORT = 7
MODES = 16
SEQ = 16384


def mode_pair(key):
    pick_key = jax.random.fold_in(key, 101)
    residue_key = jax.random.fold_in(key, 202)
    lowest = math.log(0.1 / SEQ)
    highest = math.log(0.04)
    uniform_pick = jax.random.uniform(pick_key, (MODES, C), jnp.float32)
    rates = jnp.exp(lowest + uniform_pick * (highest - lowest))
    normals = jnp.clip(jax.random.normal(residue_key, (MODES, C), jnp.float32), -3.0, 3.0)
    residues = normals * jnp.sqrt(2.0 * rates / MODES)
    return (rates, residues)


def draw_decay_rate(key, part):
    return mode_pair(key)[0]


def draw_residue(key, part):
    return mode_pair(key)[1]


def draw_cotangent(key, part):
    column_key = jax.random.fold_in(key, 7)
    value_key = jax.random.fold_in(key, 8)
    columns = jnp.arange(C, dtype=jnp.float32) / C
    spread = jnp.exp(jax.random.uniform(column_key, (C,), jnp.float32) * math.log(10.0)) * jnp.exp2(columns)
    base_draw = jnp.clip(jax.random.normal(value_key, (SEQ, C), jnp.float32), -4.0, 4.0)
    return (base_draw * spread[None, :]).astype(jnp.bfloat16)


def levels(key, extent, cuts, low, largest):
    def one(dim, shards_of):
        heights = jax.random.uniform(jax.random.fold_in(jax.random.fold_in(key, 6), dim), (shards_of,), jnp.float32, low / len(cuts), largest / len(cuts))
        return jnp.repeat(jnp.exp(heights), extent[dim] // shards_of).reshape((-1,) + (1,) * (len(extent) - dim - 1))

    gain = one(*cuts[0])
    for cut in cuts[1:]:
        gain = gain * one(*cut)
    return gain


def scatter_about(rng, dims, width, bound, pieces=(), held_as=jnp.bfloat16):
    entries = jax.random.normal(rng, dims, jnp.float32) * width
    if len(pieces) > 0:
        entries = levels(rng, dims, pieces, -0.22, 0.18) * entries
    return jnp.clip(entries, min=-bound, max=bound).astype(held_as)


def setup_inputs(seed: int = 0) -> dict:
    seeds = jax.random.split(jax.random.key(seed), 6)
    inputs = scatter_about(seeds[0], (3, SEQ, C), 1.0, 6.0, ((1, 64), (2, 8)))
    cotangent = draw_cotangent(jax.random.fold_in(seeds[5], 71), 0)
    short_filter = scatter_about(seeds[2], (3, SHORT, C), SHORT ** -0.5, 2.0, ((2, 8),), jnp.float32)
    residue = draw_residue(jax.random.fold_in(seeds[5], 71), 0)
    decay_rate = draw_decay_rate(jax.random.fold_in(seeds[5], 71), 0)
    return dict(inputs=inputs, cotangent=cotangent, short_filter=short_filter, residue=residue, decay_rate=decay_rate)


def reference(inputs, cotangent, short_filter, residue, decay_rate):
    block_width = math.gcd(C, 256)
    block_starts = jnp.arange(C // block_width, dtype=jnp.int32) * block_width
    frame_len = 2 * SEQ
    offsets = jnp.arange(SEQ, dtype=jnp.float32)

    def one_block(first_chan):
        input_block = lax.dynamic_slice_in_dim(inputs, first_chan, block_width, 2).astype(jnp.float32)
        weights = lax.dynamic_slice_in_dim(short_filter, first_chan, block_width, 2)
        residue_part = lax.dynamic_slice_in_dim(residue, first_chan, block_width, 1)
        rate_part = lax.dynamic_slice_in_dim(decay_rate, first_chan, block_width, 1)
        grad_out = lax.dynamic_slice_in_dim(cotangent, first_chan, block_width, 1).astype(jnp.float32)
        padded = jnp.pad(input_block, ((0, 0), (SHORT - 1, 0), (0, 0)))
        mixed_all = jnp.zeros((3, SEQ, block_width), jnp.float32)
        for offset in range(SHORT):
            mixed_all = mixed_all + weights[:, offset, None, :] * padded[:, SHORT - 1 - offset:SHORT - 1 - offset + SEQ, :]
        gated_kv = lax.optimization_barrier((mixed_all[1] * mixed_all[2]).astype(jnp.bfloat16))
        gated_wide = gated_kv.astype(jnp.float32)
        grad_mixer = lax.optimization_barrier((grad_out * mixed_all[0]).astype(jnp.bfloat16))
        grad_wide = grad_mixer.astype(jnp.float32)
        long_filter = jnp.zeros((SEQ, block_width), jnp.float32)
        for mode_index in range(MODES):
            long_filter = long_filter + residue_part[mode_index][None, :] * jnp.exp(-rate_part[mode_index][None, :] * offsets[:, None])
        filter_spec = jnp.fft.rfft(long_filter, n=frame_len, axis=0)
        gated_spec = jnp.fft.rfft(gated_wide, n=frame_len, axis=0)
        grad_spec = jnp.fft.rfft(grad_wide, n=frame_len, axis=0)
        mixer = jnp.fft.irfft(gated_spec * filter_spec, n=frame_len, axis=0)[:SEQ]
        grad_gated = jnp.fft.irfft(jnp.conj(filter_spec) * grad_spec, n=frame_len, axis=0)[:SEQ]
        grad_query = grad_out * mixer
        grad_key = grad_gated * mixed_all[2]
        grad_value = grad_gated * mixed_all[1]
        grad_mix = lax.optimization_barrier(jnp.stack([grad_query, grad_key, grad_value]).astype(jnp.bfloat16))
        grad_mix_wide = grad_mix.astype(jnp.float32)
        grad_padded = jnp.pad(grad_mix_wide, ((0, 0), (0, SHORT - 1), (0, 0)))
        grad_in = jnp.zeros((3, SEQ, block_width), jnp.float32)
        for offset in range(SHORT):
            grad_in = grad_in + weights[:, offset, None, :] * grad_padded[:, offset:offset + SEQ, :]
        short_grad = jnp.stack([lax.optimization_barrier(jnp.sum(grad_mix_wide * padded[:, SHORT - 1 - offset:SHORT - 1 - offset + SEQ, :], axis=1)) for offset in range(SHORT)], axis=1)
        return (grad_in.astype(jnp.bfloat16), short_grad)
    results = lax.map(one_block, block_starts)
    grad_inputs = jnp.moveaxis(results[0], 0, 2).reshape(3, SEQ, C)
    short_grad = jnp.moveaxis(results[1], 0, 2).reshape(3, SHORT, C)
    squares = jnp.sum(short_grad * short_grad)
    clip_limit = math.sqrt(3 * C * SHORT)
    factor = jnp.minimum(1.0, clip_limit / (jnp.sqrt(squares) + 1e-06))
    return (grad_inputs, short_grad * factor)
```

```python
import functools
import math

import jax
import jax.numpy as jnp
from jax import lax
from jax.experimental import pallas as pl
from jax.experimental.pallas import tpu as pltpu
from jax.sharding import PartitionSpec as P

LANES = 128
SUBS = 8
HALO = 8
F32 = jnp.float32
BF16 = jnp.bfloat16


def sub_index():
    return lax.broadcasted_iota(jnp.int32, (SUBS, LANES), 0)


def step_major(row_count, inverse):
    kept = lax.broadcasted_iota(jnp.int32, (row_count, row_count), 1 if inverse else 0)
    time = lax.broadcasted_iota(jnp.int32, (row_count, row_count), 0 if inverse else 1)
    source = (kept & (SUBS - 1)) * (row_count // SUBS) + (kept >> 3)
    return jnp.where(source == time, 1.0, 0.0).astype(BF16)


def spread(row):
    return jnp.broadcast_to(row, (SUBS, LANES))


def lanes_of(group):
    return pl.ds(group * LANES, LANES)


def load_steps(perm, x_ref, prev_ref, held, part, row_count, lead):
    steps = row_count // SUBS
    held[part, pl.ds(lead * SUBS, row_count), :] = jnp.dot(
        perm, x_ref[part], preferred_element_type=F32
    )
    early = prev_ref[part].astype(F32)
    for group in range(held.shape[2] // LANES):
        for step in range(lead):
            late = held[part, pl.ds((steps + step) * SUBS, SUBS), lanes_of(group)]
            row = HALO - lead + step
            first = early[row : row + 1, group * LANES : (group + 1) * LANES]
            held[part, pl.ds(step * SUBS, SUBS), lanes_of(group)] = jnp.where(
                sub_index() == 0, spread(first), pltpu.roll(late, 1, 0)
            )


def mix_kernel(
    x_ref, prev_ref, cot_ref, filt_ref, rate_ref,
    kv_ref, gated_ref, gradm_ref, state_ref,
    held, cot_held, perm_ref,
):
    row_count = cot_ref.shape[0]
    taps = filt_ref.shape[1]
    modes = rate_ref.shape[0]
    lead = taps - 1
    steps = row_count // SUBS
    groups = cot_ref.shape[1] // LANES

    @pl.when(pl.program_id(0) == 0)
    def _():
        perm_ref[...] = step_major(row_count, False)

    perm = perm_ref[...]
    for part in range(3):
        load_steps(perm, x_ref, prev_ref, held, part, row_count, lead)
    cot_held[...] = jnp.dot(perm, cot_ref[...], preferred_element_type=F32)
    chunk = 4 * SUBS
    for group in range(groups):
        lanes = lanes_of(group)
        taps_of = [
            [filt_ref[part, pl.ds(k, 1), lanes] for k in range(taps)] for part in range(3)
        ]

        def mix_chunk(index, carry):
            base = pl.multiple_of(index * chunk, chunk)
            mixed = []
            for part in range(3):
                total = taps_of[part][0] * held[part, pl.ds(base + lead * SUBS, chunk), lanes]
                for k in range(1, taps):
                    total += (
                        taps_of[part][k]
                        * held[part, pl.ds(base + (lead - k) * SUBS, chunk), lanes]
                    )
                mixed.append(total)
            rows = pl.ds(base, chunk)
            kv_ref[0, rows, lanes] = mixed[1]
            kv_ref[1, rows, lanes] = mixed[2]
            gated_ref[rows, lanes] = (mixed[1] * mixed[2]).astype(BF16).astype(F32)
            gradm_ref[rows, lanes] = (
                (cot_held[rows, lanes] * mixed[0]).astype(BF16).astype(F32)
            )
            return carry

        lax.fori_loop(0, row_count // chunk, mix_chunk, 0)
        decay = [spread(jnp.exp(-rate_ref[pl.ds(n, 1), lanes])) for n in range(modes)]

        def gather_step(step, carry):
            ends, starts = carry
            ahead = gated_ref[pl.ds(pl.multiple_of(step * SUBS, SUBS), SUBS), lanes]
            behind = gradm_ref[
                pl.ds(pl.multiple_of((steps - 1 - step) * SUBS, SUBS), SUBS), lanes
            ]
            return (
                [e * d + ahead for e, d in zip(ends, decay)],
                [s * d + behind for s, d in zip(starts, decay)],
            )

        zero = jnp.zeros((SUBS, LANES), F32)
        ends, starts = lax.fori_loop(
            0, steps, gather_step, ([zero] * modes, [zero] * modes), unroll=4
        )
        place = pl.ds(pl.program_id(0) * groups + group, 1)
        seg = sub_index().astype(F32) * steps
        for n in range(modes):
            rate = spread(rate_ref[pl.ds(n, 1), lanes])
            to_start = jnp.exp(-rate * seg)
            to_end = jnp.exp(-rate * (steps * (SUBS - 1) - seg))
            state_ref[n, place, :] = jnp.sum(ends[n] * to_end, axis=0, keepdims=True)
            state_ref[modes + n, place, :] = jnp.sum(
                starts[n] * to_start, axis=0, keepdims=True
            )


def chain_kernel(row_count, half, first_ref, arrived_ref, rate_ref, out_ref):
    blocks = arrived_ref.shape[0]
    step_decay = jnp.exp(-rate_ref[...] * row_count)

    def run(order):
        def body(index, carry):
            block = order(index)
            out_ref[pl.ds(block, 1)] = carry[None]
            return carry * step_decay + arrived_ref[pl.ds(block, 1)][0]

        lax.fori_loop(0, blocks, body, jnp.zeros(rate_ref.shape, F32), unroll=8)

    @pl.when(first_ref[0] < half)
    def _():
        run(lambda index: index)

    @pl.when(first_ref[0] >= half)
    def _():
        run(lambda index: blocks - 1 - index)


def local_kernel(
    gated_ref, gradm_ref, residue_ref, rate_ref, ahead_ref, behind_ref, seg_ref
):
    row_count = gated_ref.shape[0]
    modes = rate_ref.shape[0]
    steps = row_count // SUBS
    for group in range(gated_ref.shape[1] // LANES):
        lanes = lanes_of(group)
        weight = [spread(residue_ref[pl.ds(n, 1), lanes]) for n in range(modes)]
        rates = [rate_ref[pl.ds(n, 1), lanes] for n in range(modes)]
        decay = [spread(jnp.exp(-r)) for r in rates]
        zero = jnp.zeros((SUBS, LANES), F32)
        for source, target, backward in (
            (gated_ref, ahead_ref, False),
            (gradm_ref, behind_ref, True),
        ):

            def scan_step(step, states):
                at = steps - 1 - step if backward else step
                rows = pl.ds(pl.multiple_of(at * SUBS, SUBS), SUBS)
                value = source[rows, lanes]
                states = [s * d + value for s, d in zip(states, decay)]
                terms = [s * w for s, w in zip(states, weight)]
                while len(terms) > 1:
                    terms = [a + b for a, b in zip(terms[::2], terms[1::2])]
                target[rows, lanes] = terms[0]
                return states

            states = lax.fori_loop(0, steps, scan_step, [zero] * modes, unroll=4)
            sub = sub_index()
            for n in range(modes):
                span = spread(jnp.exp(-rates[n] * steps))
                total = states[n]
                for shift in (1, 2, 4):
                    if backward:
                        moved = jnp.where(
                            sub < SUBS - shift, pltpu.roll(total, SUBS - shift, 0), 0.0
                        )
                    else:
                        moved = jnp.where(sub >= shift, pltpu.roll(total, shift, 0), 0.0)
                    total = total + span * moved
                    span = span * span
                if backward:
                    enters = jnp.where(sub < SUBS - 1, pltpu.roll(total, SUBS - 1, 0), 0.0)
                else:
                    enters = jnp.where(sub >= 1, pltpu.roll(total, 1, 0), 0.0)
                seg_ref[int(backward), n, :, lanes] = enters


def grad_kernel(
    x_ref, prev_ref, cot_ref, kv_ref, ahead_ref, behind_ref, seg_ref, enter_ref,
    residue_ref, rate_ref,
    mix_ref, short_ref,
    held, cot_held, perm_ref,
):
    row_count = cot_ref.shape[0]
    modes = rate_ref.shape[0]
    taps = short_ref.shape[1]
    lead = taps - 1
    steps = row_count // SUBS
    groups = cot_ref.shape[1] // LANES

    @pl.when(pl.program_id(0) == 0)
    def _():
        perm_ref[...] = step_major(row_count, False)

    perm = perm_ref[...]
    for part in range(3):
        load_steps(perm, x_ref, prev_ref, held, part, row_count, lead)
    cot_held[...] = jnp.dot(perm, cot_ref[...], preferred_element_type=F32)
    for group in range(groups):
        lanes = lanes_of(group)
        place = pl.ds(pl.program_id(0) * groups + group, 1)
        rates = [spread(rate_ref[pl.ds(n, 1), lanes]) for n in range(modes)]
        decay = [jnp.exp(-r) for r in rates]
        seg = sub_index().astype(F32) * steps
        for backward in (False, True):
            gap = steps * (SUBS - 1) - seg if backward else seg
            carried = []
            for n in range(modes):
                outer = spread(enter_ref[int(backward) * modes + n, place, :])
                inner = seg_ref[int(backward), n, :, lanes]
                total = inner + jnp.exp(-rates[n] * gap) * outer
                carried.append(
                    total * decay[n] * spread(residue_ref[pl.ds(n, 1), lanes])
                )
            parts = (1, 2) if backward else (0,)

            def grad_pair(index, carry):
                carried, sums = carry
                pair = steps // 2 - 1 - index if backward else index
                base = pl.multiple_of(pair * 2 * SUBS, 2 * SUBS)
                long_rows = [None, None]
                source = behind_ref if backward else ahead_ref
                for which in (1, 0) if backward else (0, 1):
                    terms = list(carried)
                    while len(terms) > 1:
                        terms = [a + b for a, b in zip(terms[::2], terms[1::2])]
                    long_rows[which] = (
                        source[pl.ds(base + which * SUBS, SUBS), lanes] + terms[0]
                    )
                    carried = [c * d for c, d in zip(carried, decay)]
                long_pair = jnp.concatenate(long_rows, axis=0)
                rows = pl.ds(base, 2 * SUBS)
                new_sums = []
                for part, old in zip(parts, sums):
                    if part == 0:
                        factor = cot_held[rows, lanes]
                    else:
                        factor = kv_ref[2 - part, rows, lanes]
                    grad = (long_pair * factor).astype(BF16)
                    mix_ref[part, rows, lanes] = grad
                    wide = grad.astype(F32)
                    taken = []
                    for k in range(taps):
                        term = wide * held[part, pl.ds(base + (lead - k) * SUBS, 2 * SUBS), lanes]
                        taken.append(old[k] + (term[:SUBS] + term[SUBS:]))
                    new_sums.append(taken)
                return carried, new_sums

            zero = jnp.zeros((SUBS, LANES), F32)
            _, sums = lax.fori_loop(
                0, steps // 2, grad_pair, (carried, [[zero] * taps for _ in parts]), unroll=2
            )
            for part, taken in zip(parts, sums):
                for k in range(taps):
                    short_ref[part, k, place, :] = jnp.sum(taken[k], axis=0, keepdims=True)


def back_kernel(mix_ref, next_ref, filt_ref, out_ref, held, made, perm_ref):
    row_count = mix_ref.shape[1]
    taps = filt_ref.shape[1]
    steps = row_count // SUBS

    @pl.when(pl.program_id(0) == 0)
    def _():
        perm_ref[...] = step_major(row_count, True)

    perm = perm_ref[...]
    chunk = 4 * SUBS
    for part in range(3):
        held[pl.ds(0, row_count), :] = mix_ref[part].astype(F32)
        late = next_ref[part].astype(F32)
        for group in range(held.shape[1] // LANES):
            lanes = lanes_of(group)
            for step in range(taps - 1):
                first = held[pl.ds(step * SUBS, SUBS), lanes]
                row = late[step : step + 1, group * LANES : (group + 1) * LANES]
                held[pl.ds((steps + step) * SUBS, SUBS), lanes] = jnp.where(
                    sub_index() == SUBS - 1, spread(row), pltpu.roll(first, SUBS - 1, 0)
                )
            weights = [filt_ref[part, pl.ds(k, 1), lanes] for k in range(taps)]

            def back_chunk(index, carry):
                base = pl.multiple_of(index * chunk, chunk)
                total = weights[0] * held[pl.ds(base, chunk), lanes]
                for k in range(1, taps):
                    total += weights[k] * held[pl.ds(base + k * SUBS, chunk), lanes]
                made[pl.ds(base, chunk), lanes] = total.astype(BF16)
                return carry

            lax.fori_loop(0, row_count // chunk, back_chunk, 0)
        out_ref[part] = jnp.dot(perm, made[...], preferred_element_type=F32).astype(BF16)


def passed_along(shard, by):
    length = lax.axis_size("ctx")
    pairs = [(i, i + by) for i in range(length) if 0 <= i + by < length]
    return lax.ppermute(shard, "ctx", pairs)


def exchange(blocks, axis):
    return lax.all_to_all(blocks, axis, split_axis=0, concat_axis=0, tiled=True)


def cost(flops, bytes_accessed):
    return pl.CostEstimate(flops=flops, bytes_accessed=bytes_accessed, transcendentals=0)


def per_device(inputs, cotangent, short_filter, residue, decay_rate):
    _, row_count, channels = inputs.shape
    taps = short_filter.shape[1]
    modes = residue.shape[0]
    blocks = lax.axis_size("ctx")
    groups = channels // LANES
    wide = min(channels, 2 * LANES)
    grid = (channels // wide,)
    lead = taps - 1

    def columns(*lead_dims):
        zeros = (0,) * len(lead_dims)
        return pl.BlockSpec((*lead_dims, wide), lambda c: (*zeros, c))

    def whole(*dims):
        zeros = (0,) * len(dims)
        return pl.BlockSpec(dims, lambda c: zeros)

    def shaped(dtype, *dims):
        return jax.ShapeDtypeStruct(dims, dtype)

    params = pltpu.CompilerParams(vmem_limit_bytes=32 << 20)
    work = row_count * channels
    step_scratch = [
        pltpu.VMEM((3, row_count + lead * SUBS, wide), F32),
        pltpu.VMEM((row_count, wide), F32),
        pltpu.VMEM((row_count, row_count), BF16),
    ]

    prev = passed_along(inputs[:, row_count - HALO :, :], 1)
    kv, gated, gradm, states = pl.pallas_call(
        mix_kernel,
        grid=grid,
        in_specs=[
            columns(3, row_count),
            columns(3, HALO),
            columns(row_count),
            columns(3, taps),
            columns(modes),
        ],
        out_specs=[
            columns(2, row_count),
            columns(row_count),
            columns(row_count),
            whole(2 * modes, groups, LANES),
        ],
        out_shape=[
            shaped(F32, 2, row_count, channels),
            shaped(F32, row_count, channels),
            shaped(F32, row_count, channels),
            shaped(F32, 2 * modes, groups, LANES),
        ],
        scratch_shapes=step_scratch,
        compiler_params=params,
        cost_estimate=cost(work * 110, work * 24),
        name="mix",
    )(inputs, prev, cotangent, short_filter, decay_rate)

    state_rows = 2 * modes * groups // blocks
    first = lax.axis_index("ctx") * state_rows
    half = modes * groups
    arrived = exchange(states.reshape(blocks, state_rows, LANES), "ctx")
    rate_rows = jnp.tile(decay_rate.reshape(half, LANES), (2, 1))
    entering = pl.pallas_call(
        functools.partial(chain_kernel, row_count, half),
        in_specs=[
            pl.BlockSpec(memory_space=pltpu.SMEM),
            pl.BlockSpec(memory_space=pltpu.VMEM),
            pl.BlockSpec(memory_space=pltpu.VMEM),
        ],
        out_specs=pl.BlockSpec(memory_space=pltpu.VMEM),
        out_shape=shaped(F32, blocks, state_rows, LANES),
        compiler_params=pltpu.CompilerParams(vmem_limit_bytes=4 << 20),
        cost_estimate=cost(blocks * state_rows * LANES * 2, blocks * state_rows * LANES * 8),
        name="chain",
    )(first[None], arrived, lax.dynamic_slice_in_dim(rate_rows, first, state_rows, 0))
    entering = exchange(entering, "ctx").reshape(2 * modes, groups, LANES)

    ahead, behind, seg_states = pl.pallas_call(
        local_kernel,
        grid=grid,
        in_specs=[columns(row_count), columns(row_count), columns(modes), columns(modes)],
        out_specs=[columns(row_count), columns(row_count), columns(2, modes, SUBS)],
        out_shape=[
            shaped(F32, row_count, channels),
            shaped(F32, row_count, channels),
            shaped(F32, 2, modes, SUBS, channels),
        ],
        compiler_params=params,
        cost_estimate=cost(work * 128, work * 18),
        name="local",
    )(gated, gradm, residue, decay_rate)

    grad_mix, short_part = pl.pallas_call(
        grad_kernel,
        grid=grid,
        in_specs=[
            columns(3, row_count),
            columns(3, HALO),
            columns(row_count),
            columns(2, row_count),
            columns(row_count),
            columns(row_count),
            columns(2, modes, SUBS),
            whole(2 * modes, groups, LANES),
            columns(modes),
            columns(modes),
        ],
        out_specs=[columns(3, row_count), whole(3, taps, groups, LANES)],
        out_shape=[
            shaped(BF16, 3, row_count, channels),
            shaped(F32, 3, taps, groups, LANES),
        ],
        scratch_shapes=step_scratch,
        compiler_params=params,
        cost_estimate=cost(work * 110, work * 30),
        name="grad",
    )(
        inputs, prev, cotangent, kv, ahead, behind, seg_states, entering, residue, decay_rate
    )

    short_rows = 3 * taps * groups
    share = -(-short_rows // blocks)
    padded = jnp.pad(
        short_part.reshape(short_rows, LANES), ((0, share * blocks - short_rows), (0, 0))
    )
    gathered = exchange(padded.reshape(blocks, share, LANES), "ctx")
    own_sum = jnp.sum(gathered, axis=0)
    all_sums = exchange(jnp.broadcast_to(own_sum[None], (blocks, share, LANES)), "ctx")
    all_sums = all_sums.reshape(share * blocks, LANES)
    squares = jnp.sum(all_sums * all_sums)
    tp_count = lax.axis_size("tp")
    squares = jnp.sum(exchange(jnp.broadcast_to(squares, (tp_count, LANES)), "tp")[:, 0])
    clip_limit = math.sqrt(3 * channels * tp_count * taps)
    factor = jnp.minimum(1.0, clip_limit / (jnp.sqrt(squares) + 1e-06))
    grad_short = (all_sums[:short_rows] * factor).reshape(3, taps, channels)

    late = passed_along(grad_mix[:, : lead * SUBS : SUBS, :], -1)
    late = jnp.pad(late, ((0, 0), (0, HALO - lead), (0, 0)))
    grad_inputs = pl.pallas_call(
        back_kernel,
        grid=grid,
        in_specs=[columns(3, row_count), columns(3, HALO), columns(3, taps)],
        out_specs=columns(3, row_count),
        out_shape=shaped(BF16, 3, row_count, channels),
        scratch_shapes=[
            pltpu.VMEM((row_count + lead * SUBS, wide), F32),
            pltpu.VMEM((row_count, wide), BF16),
            pltpu.VMEM((row_count, row_count), BF16),
        ],
        compiler_params=params,
        cost_estimate=cost(work * 48, work * 12),
        name="back",
    )(grad_mix, late, short_filter)
    return (grad_inputs, grad_short)


def solution(mesh):
    return jax.shard_map(
        per_device,
        mesh=mesh,
        in_specs=(
            P(None, "ctx", "tp"),
            P("ctx", "tp"),
            P(None, None, "tp"),
            P(None, "tp"),
            P(None, "tp"),
        ),
        out_specs=(P(None, "ctx", "tp"), P(None, None, "tp")),
        check_vma=False,
    )
```

```python
import functools
import math

import jax
import jax.numpy as jnp
from jax import lax
from jax.experimental import pallas as pl
from jax.experimental.pallas import tpu as pltpu
from jax.sharding import PartitionSpec as P

LANES = 128
SUBS = 8
HALO = 8
CHUNK = 8
TAPS = 7
F32 = jnp.float32
BF16 = jnp.bfloat16


def sub_index():
    return lax.broadcasted_iota(jnp.int32, (SUBS, LANES), 0)


def step_major(row_count, inverse):
    kept = lax.broadcasted_iota(jnp.int32, (row_count, row_count), 1 if inverse else 0)
    time = lax.broadcasted_iota(jnp.int32, (row_count, row_count), 0 if inverse else 1)
    source = (kept & (SUBS - 1)) * (row_count // SUBS) + (kept >> 3)
    return jnp.where(source == time, 1.0, 0.0).astype(BF16)


def spread(row):
    return jnp.broadcast_to(row, (SUBS, LANES))


def lanes_of(group):
    return pl.ds(group * LANES, LANES)


def kept(value):
    return value.astype(BF16).astype(F32)


def added(terms):
    while len(terms) > 1:
        odd = terms[-1:] if len(terms) % 2 else []
        terms = [a + b for a, b in zip(terms[::2], terms[1::2])] + odd
    return terms[0]


def tapped(weights, rows):
    return added([w * r for w, r in zip(weights, rows)])


def load_steps(perm, x_ref, prev_ref, held, part, row_count, lead):
    steps = row_count // SUBS
    held[part, pl.ds(lead * SUBS, row_count), :] = jnp.dot(
        perm, x_ref[part], preferred_element_type=F32
    )
    early = prev_ref[part].astype(F32)
    for group in range(held.shape[2] // LANES):
        for step in range(lead):
            late = held[part, pl.ds((steps + step) * SUBS, SUBS), lanes_of(group)]
            row = HALO - lead + step
            first = early[row : row + 1, group * LANES : (group + 1) * LANES]
            held[part, pl.ds(step * SUBS, SUBS), lanes_of(group)] = jnp.where(
                sub_index() == 0, spread(first), pltpu.roll(late, 1, 0)
            )


def mix_kernel(
    x_ref, prev_ref, cot_ref, filt_ref, rate_ref,
    kv_ref, gated_ref, gradm_ref, state_ref,
    held, cot_held, perm_ref,
):
    row_count = cot_ref.shape[0]
    taps = filt_ref.shape[1]
    modes = rate_ref.shape[0]
    lead = taps - 1
    steps = row_count // SUBS
    groups = cot_ref.shape[1] // LANES

    @pl.when(pl.program_id(0) == 0)
    def _():
        perm_ref[...] = step_major(row_count, False)

    perm = perm_ref[...]
    for part in range(3):
        load_steps(perm, x_ref, prev_ref, held, part, row_count, lead)
    cot_held[...] = jnp.dot(perm, cot_ref[...], preferred_element_type=F32)
    for group in range(groups):
        lanes = lanes_of(group)
        weights = [
            [spread(filt_ref[part, pl.ds(k, 1), lanes]) for k in range(taps)] for part in range(3)
        ]

        def mix_chunk(index, carry):
            base = pl.multiple_of(index * (CHUNK * SUBS), CHUNK * SUBS)

            def short(part):
                window = [
                    held[part, pl.ds(base + at * SUBS, SUBS), lanes] for at in range(CHUNK + lead)
                ]
                return [tapped(weights[part], window[at : at + taps][::-1]) for at in range(CHUNK)]

            key_rows = short(1)
            value_rows = short(2)
            for at in range(CHUNK):
                rows = pl.ds(base + at * SUBS, SUBS)
                kv_ref[0, rows, lanes] = key_rows[at]
                kv_ref[1, rows, lanes] = value_rows[at]
                gated_ref[rows, lanes] = kept(key_rows[at] * value_rows[at])
            query_rows = short(0)
            for at in range(CHUNK):
                rows = pl.ds(base + at * SUBS, SUBS)
                gradm_ref[rows, lanes] = kept(cot_held[rows, lanes] * query_rows[at])
            return carry

        lax.fori_loop(0, steps // CHUNK, mix_chunk, 0)
        decay = [spread(jnp.exp(-rate_ref[pl.ds(n, 1), lanes])) for n in range(modes)]

        def gather_step(step, carry):
            ends, starts = carry
            ahead = gated_ref[pl.ds(pl.multiple_of(step * SUBS, SUBS), SUBS), lanes]
            behind = gradm_ref[
                pl.ds(pl.multiple_of((steps - 1 - step) * SUBS, SUBS), SUBS), lanes
            ]
            return (
                [e * d + ahead for e, d in zip(ends, decay)],
                [s * d + behind for s, d in zip(starts, decay)],
            )

        zero = jnp.zeros((SUBS, LANES), F32)
        ends, starts = lax.fori_loop(
            0, steps, gather_step, ([zero] * modes, [zero] * modes), unroll=8
        )
        place = pl.ds(pl.program_id(0) * groups + group, 1)
        seg = sub_index().astype(F32) * steps
        for n in range(modes):
            rate = spread(rate_ref[pl.ds(n, 1), lanes])
            to_start = jnp.exp(-rate * seg)
            to_end = jnp.exp(-rate * (steps * (SUBS - 1) - seg))
            state_ref[n, place, :] = jnp.sum(ends[n] * to_end, axis=0, keepdims=True)
            state_ref[modes + n, place, :] = jnp.sum(
                starts[n] * to_start, axis=0, keepdims=True
            )


def chain_kernel(row_count, half, first_ref, arrived_ref, rate_ref, out_ref):
    blocks = arrived_ref.shape[0]
    step_decay = jnp.exp(-rate_ref[...] * row_count)

    def run(order):
        def body(index, carry):
            block = order(index)
            out_ref[pl.ds(block, 1)] = carry[None]
            return carry * step_decay + arrived_ref[pl.ds(block, 1)][0]

        lax.fori_loop(0, blocks, body, jnp.zeros(rate_ref.shape, F32), unroll=8)

    @pl.when(first_ref[0] < half)
    def _():
        run(lambda index: index)

    @pl.when(first_ref[0] >= half)
    def _():
        run(lambda index: blocks - 1 - index)


def local_kernel(
    gated_ref, gradm_ref, residue_ref, rate_ref, ahead_ref, behind_ref, seg_ref
):
    row_count = gated_ref.shape[0]
    modes = rate_ref.shape[0]
    steps = row_count // SUBS
    for group in range(gated_ref.shape[1] // LANES):
        lanes = lanes_of(group)
        weight = [spread(residue_ref[pl.ds(n, 1), lanes]) for n in range(modes)]
        rates = [rate_ref[pl.ds(n, 1), lanes] for n in range(modes)]
        decay = [spread(jnp.exp(-r)) for r in rates]
        zero = jnp.zeros((SUBS, LANES), F32)
        for source, target, backward in (
            (gated_ref, ahead_ref, False),
            (gradm_ref, behind_ref, True),
        ):

            def scan_step(step, states):
                at = steps - 1 - step if backward else step
                rows = pl.ds(pl.multiple_of(at * SUBS, SUBS), SUBS)
                value = source[rows, lanes]
                states = [s * d + value for s, d in zip(states, decay)]
                target[rows, lanes] = tapped(weight, states)
                return states

            states = lax.fori_loop(0, steps, scan_step, [zero] * modes, unroll=8)
            sub = sub_index()
            for n in range(modes):
                span = spread(jnp.exp(-rates[n] * steps))
                total = states[n]
                for shift in (1, 2, 4):
                    if backward:
                        moved = jnp.where(
                            sub < SUBS - shift, pltpu.roll(total, SUBS - shift, 0), 0.0
                        )
                    else:
                        moved = jnp.where(sub >= shift, pltpu.roll(total, shift, 0), 0.0)
                    total = total + span * moved
                    span = span * span
                if backward:
                    enters = jnp.where(sub < SUBS - 1, pltpu.roll(total, SUBS - 1, 0), 0.0)
                else:
                    enters = jnp.where(sub >= 1, pltpu.roll(total, 1, 0), 0.0)
                seg_ref[int(backward), n, :, lanes] = enters


def grad_kernel(
    x_ref, prev_ref, cot_ref, kv_ref, ahead_ref, behind_ref, seg_ref, enter_ref,
    residue_ref, rate_ref,
    mix_ref, short_ref,
    held, cot_held, perm_ref,
):
    row_count = cot_ref.shape[0]
    modes = rate_ref.shape[0]
    taps = TAPS
    lead = taps - 1
    steps = row_count // SUBS
    groups = cot_ref.shape[1] // LANES

    @pl.when(pl.program_id(0) == 0)
    def _():
        perm_ref[...] = step_major(row_count, False)
        short_ref[...] = jnp.zeros(short_ref.shape, F32)

    perm = perm_ref[...]
    for part in range(3):
        load_steps(perm, x_ref, prev_ref, held, part, row_count, lead)
    cot_held[...] = jnp.dot(perm, cot_ref[...], preferred_element_type=F32)
    for group in range(groups):
        lanes = lanes_of(group)
        place = pl.ds(pl.program_id(0) * groups + group, 1)
        rates = [spread(rate_ref[pl.ds(n, 1), lanes]) for n in range(modes)]
        decay = [jnp.exp(-r) for r in rates]
        seg = sub_index().astype(F32) * steps
        for backward in (False, True):
            gap = steps * (SUBS - 1) - seg if backward else seg
            carried = []
            for n in range(modes):
                outer = spread(enter_ref[int(backward) * modes + n, place, :])
                inner = seg_ref[int(backward), n, :, lanes]
                total = inner + jnp.exp(-rates[n] * gap) * outer
                carried.append(
                    total * decay[n] * spread(residue_ref[pl.ds(n, 1), lanes])
                )
            parts = (1, 2) if backward else (0,)

            def grad_chunk(index, carry):
                carried, sums = carry
                place_of = steps // CHUNK - 1 - index if backward else index
                base = pl.multiple_of(place_of * (CHUNK * SUBS), CHUNK * SUBS)
                source = behind_ref if backward else ahead_ref
                long_rows = [None] * CHUNK
                for at in range(CHUNK)[:: -1 if backward else 1]:
                    long_rows[at] = source[pl.ds(base + at * SUBS, SUBS), lanes] + added(carried)
                    carried = [c * d for c, d in zip(carried, decay)]
                new_sums = []
                for part, old in zip(parts, sums):
                    wide = []
                    for pair in range(CHUNK // 2):
                        rows = pl.ds(base + pair * 2 * SUBS, 2 * SUBS)
                        factor = cot_held[rows, lanes] if part == 0 else kv_ref[2 - part, rows, lanes]
                        grad = jnp.concatenate(long_rows[2 * pair : 2 * pair + 2], axis=0) * factor
                        grad = grad.astype(BF16)
                        mix_ref[part, rows, lanes] = grad
                        grad = grad.astype(F32)
                        wide += [grad[:SUBS], grad[SUBS:]]
                    window = [
                        held[part, pl.ds(base + at * SUBS, SUBS), lanes]
                        for at in range(CHUNK + lead)
                    ]
                    new_sums.append(
                        [
                            old[k] + tapped(wide, window[lead - k : lead - k + CHUNK])
                            for k in range(taps)
                        ]
                    )
                return carried, new_sums

            zero = jnp.zeros((SUBS, LANES), F32)
            _, sums = lax.fori_loop(
                0, steps // CHUNK, grad_chunk, (carried, [[zero] * taps for _ in parts])
            )
            for part, taken in zip(parts, sums):
                for k in range(taps):
                    short_ref[part * taps + k, place, :] = jnp.sum(taken[k], axis=0, keepdims=True)


def back_kernel(mix_ref, next_ref, filt_ref, out_ref, held, made, perm_ref):
    row_count = mix_ref.shape[1]
    taps = filt_ref.shape[1]
    steps = row_count // SUBS

    @pl.when(pl.program_id(0) == 0)
    def _():
        perm_ref[...] = step_major(row_count, True)

    perm = perm_ref[...]
    for part in range(3):
        held[pl.ds(0, row_count), :] = mix_ref[part].astype(F32)
        late = next_ref[part].astype(F32)
        for group in range(held.shape[1] // LANES):
            lanes = lanes_of(group)
            for step in range(taps - 1):
                first = held[pl.ds(step * SUBS, SUBS), lanes]
                row = late[step : step + 1, group * LANES : (group + 1) * LANES]
                held[pl.ds((steps + step) * SUBS, SUBS), lanes] = jnp.where(
                    sub_index() == SUBS - 1, spread(row), pltpu.roll(first, SUBS - 1, 0)
                )
            weights = [spread(filt_ref[part, pl.ds(k, 1), lanes]) for k in range(taps)]

            def back_chunk(index, carry):
                base = pl.multiple_of(index * (CHUNK * SUBS), CHUNK * SUBS)
                window = [
                    held[pl.ds(base + at * SUBS, SUBS), lanes] for at in range(CHUNK + taps - 1)
                ]
                rows = [tapped(weights, window[at : at + taps]) for at in range(CHUNK)]
                made[pl.ds(base, CHUNK * SUBS), lanes] = jnp.concatenate(rows, axis=0).astype(BF16)
                return carry

            lax.fori_loop(0, steps // CHUNK, back_chunk, 0)
        out_ref[part] = jnp.dot(perm, made[...], preferred_element_type=F32).astype(BF16)


def fold_kernel(part_ref, out_ref):
    total = jnp.sum(part_ref[...], axis=0, keepdims=True)
    out_ref[...] = jnp.broadcast_to(total, out_ref.shape)


def square_kernel(sums_ref, out_ref):
    value = sums_ref[...]
    total = jnp.sum(jnp.sum(value * value, axis=0))
    out_ref[...] = jnp.full(out_ref.shape, total, F32)


def scale_kernel(clip_limit, sums_ref, squares_ref, out_ref):
    squares = jnp.sum(squares_ref[...], axis=0, keepdims=True)
    factor = jnp.minimum(1.0, clip_limit / (jnp.sqrt(squares) + 1e-06))
    taps = out_ref.shape[1]
    for part in range(3):
        for k in range(taps):
            rows = sums_ref[part * taps + k] * factor
            for group in range(rows.shape[0]):
                out_ref[part, pl.ds(k, 1), lanes_of(group)] = rows[group : group + 1]


def passed_along(shard, by):
    length = lax.axis_size("ctx")
    pairs = [(i, i + by) for i in range(length) if 0 <= i + by < length]
    return lax.ppermute(shard, "ctx", pairs)


def exchange(blocks, axis):
    return lax.all_to_all(blocks, axis, split_axis=0, concat_axis=0, tiled=True)


def cost(flops, bytes_accessed):
    return pl.CostEstimate(flops=flops, bytes_accessed=bytes_accessed, transcendentals=0)


def per_device(inputs, cotangent, short_filter, residue, decay_rate):
    _, row_count, channels = inputs.shape
    taps = short_filter.shape[1]
    modes = residue.shape[0]
    blocks = lax.axis_size("ctx")
    groups = channels // LANES
    wide = min(channels, 2 * LANES)
    grid = (channels // wide,)
    lead = taps - 1

    def columns(*lead_dims):
        zeros = (0,) * len(lead_dims)
        return pl.BlockSpec((*lead_dims, wide), lambda c: (*zeros, c))

    def whole(*dims):
        zeros = (0,) * len(dims)
        return pl.BlockSpec(dims, lambda c: zeros)

    def shaped(dtype, *dims):
        return jax.ShapeDtypeStruct(dims, dtype)

    params = pltpu.CompilerParams(vmem_limit_bytes=60 << 20)
    small = pltpu.CompilerParams(vmem_limit_bytes=4 << 20)
    in_vmem = pl.BlockSpec(memory_space=pltpu.VMEM)
    work = row_count * channels
    step_scratch = [
        pltpu.VMEM((3, row_count + lead * SUBS, wide), F32),
        pltpu.VMEM((row_count, wide), F32),
        pltpu.VMEM((row_count, row_count), BF16),
    ]

    prev = passed_along(inputs[:, row_count - HALO :, :], 1)
    kv, gated, gradm, states = pl.pallas_call(
        mix_kernel,
        grid=grid,
        in_specs=[
            columns(3, row_count),
            columns(3, HALO),
            columns(row_count),
            columns(3, taps),
            columns(modes),
        ],
        out_specs=[
            columns(2, row_count),
            columns(row_count),
            columns(row_count),
            whole(2 * modes, groups, LANES),
        ],
        out_shape=[
            shaped(F32, 2, row_count, channels),
            shaped(F32, row_count, channels),
            shaped(F32, row_count, channels),
            shaped(F32, 2 * modes, groups, LANES),
        ],
        scratch_shapes=step_scratch,
        compiler_params=params,
        cost_estimate=cost(work * 110, work * 24),
        name="mix",
    )(inputs, prev, cotangent, short_filter, decay_rate)

    state_rows = 2 * modes * groups // blocks
    first = lax.axis_index("ctx") * state_rows
    half = modes * groups
    arrived = exchange(states.reshape(blocks, state_rows, LANES), "ctx")
    ahead, behind, seg_states = pl.pallas_call(
        local_kernel,
        grid=grid,
        in_specs=[columns(row_count), columns(row_count), columns(modes), columns(modes)],
        out_specs=[columns(row_count), columns(row_count), columns(2, modes, SUBS)],
        out_shape=[
            shaped(F32, row_count, channels),
            shaped(F32, row_count, channels),
            shaped(F32, 2, modes, SUBS, channels),
        ],
        compiler_params=params,
        cost_estimate=cost(work * 128, work * 18),
        name="local",
    )(gated, gradm, residue, decay_rate)
    arrived, ahead, behind, seg_states = lax.optimization_barrier(
        (arrived, ahead, behind, seg_states)
    )

    rate_rows = jnp.tile(decay_rate.reshape(half, LANES), (2, 1))
    entering = pl.pallas_call(
        functools.partial(chain_kernel, row_count, half),
        in_specs=[
            pl.BlockSpec(memory_space=pltpu.SMEM),
            in_vmem,
            in_vmem,
        ],
        out_specs=in_vmem,
        out_shape=shaped(F32, blocks, state_rows, LANES),
        compiler_params=small,
        cost_estimate=cost(blocks * state_rows * LANES * 2, blocks * state_rows * LANES * 8),
        name="chain",
    )(first[None], arrived, lax.dynamic_slice_in_dim(rate_rows, first, state_rows, 0))
    entering = exchange(entering, "ctx").reshape(2 * modes, groups, LANES)

    share = -(-3 * taps * groups // blocks)
    share += share % 2
    short_rows = share * blocks // groups
    grad_mix, short_part = pl.pallas_call(
        grad_kernel,
        grid=grid,
        in_specs=[
            columns(3, row_count),
            columns(3, HALO),
            columns(row_count),
            columns(2, row_count),
            columns(row_count),
            columns(row_count),
            columns(2, modes, SUBS),
            whole(2 * modes, groups, LANES),
            columns(modes),
            columns(modes),
        ],
        out_specs=[columns(3, row_count), whole(short_rows, groups, LANES)],
        out_shape=[
            shaped(BF16, 3, row_count, channels),
            shaped(F32, short_rows, groups, LANES),
        ],
        scratch_shapes=step_scratch,
        compiler_params=params,
        cost_estimate=cost(work * 110, work * 30),
        name="grad",
    )(
        inputs, prev, cotangent, kv, ahead, behind, seg_states, entering, residue, decay_rate
    )

    gathered = exchange(short_part.reshape(blocks, share, LANES), "ctx")
    late = passed_along(grad_mix[:, : lead * SUBS : SUBS, :], -1)
    late = jnp.pad(late, ((0, 0), (0, HALO - lead), (0, 0)))
    gathered, late = lax.optimization_barrier((gathered, late))
    own_sum = pl.pallas_call(
        fold_kernel,
        in_specs=[in_vmem],
        out_specs=in_vmem,
        out_shape=shaped(F32, blocks, share, LANES),
        compiler_params=small,
        name="fold",
    )(gathered)
    all_sums = exchange(own_sum, "ctx")
    grad_inputs = pl.pallas_call(
        back_kernel,
        grid=grid,
        in_specs=[columns(3, row_count), columns(3, HALO), columns(3, taps)],
        out_specs=columns(3, row_count),
        out_shape=shaped(BF16, 3, row_count, channels),
        scratch_shapes=[
            pltpu.VMEM((row_count + lead * SUBS, wide), F32),
            pltpu.VMEM((row_count, wide), BF16),
            pltpu.VMEM((row_count, row_count), BF16),
        ],
        compiler_params=params,
        cost_estimate=cost(work * 48, work * 12),
        name="back",
    )(grad_mix, late, short_filter)
    all_sums, grad_inputs = lax.optimization_barrier((all_sums, grad_inputs))
    all_sums = all_sums.reshape(short_rows, groups, LANES)
    tp_count = lax.axis_size("tp")
    squares = pl.pallas_call(
        square_kernel,
        in_specs=[in_vmem],
        out_specs=in_vmem,
        out_shape=shaped(F32, tp_count, LANES),
        compiler_params=small,
        name="square",
    )(all_sums)
    squares = exchange(squares, "tp")
    clip_limit = math.sqrt(3 * channels * tp_count * taps)
    grad_short = pl.pallas_call(
        functools.partial(scale_kernel, clip_limit),
        in_specs=[in_vmem, in_vmem],
        out_specs=in_vmem,
        out_shape=shaped(F32, 3, taps, channels),
        compiler_params=small,
        name="scale",
    )(all_sums, squares)
    return (grad_inputs, grad_short)


def solution(mesh):
    return jax.shard_map(
        per_device,
        mesh=mesh,
        in_specs=(
            P(None, "ctx", "tp"),
            P("ctx", "tp"),
            P(None, None, "tp"),
            P(None, "tp"),
            P(None, "tp"),
        ),
        out_specs=(P(None, "ctx", "tp"), P(None, None, "tp")),
        check_vma=False,
    )
```

```python
import functools
import math

import jax
import jax.numpy as jnp
from jax import lax
from jax.experimental import pallas as pl
from jax.experimental.pallas import tpu as pltpu
from jax.sharding import PartitionSpec as P

LANES = 128
SUBS = 8
HALO = 8
CHUNK = 16
F32 = jnp.float32
BF16 = jnp.bfloat16


def sub_index():
    return lax.broadcasted_iota(jnp.int32, (SUBS, LANES), 0)


def step_major(row_count, inverse):
    kept = lax.broadcasted_iota(jnp.int32, (row_count, row_count), 1 if inverse else 0)
    time = lax.broadcasted_iota(jnp.int32, (row_count, row_count), 0 if inverse else 1)
    source = (kept & (SUBS - 1)) * (row_count // SUBS) + (kept >> 3)
    return jnp.where(source == time, 1.0, 0.0).astype(BF16)


def spread(row):
    return jnp.broadcast_to(row, (SUBS, LANES))


def step_rows(first, count=1):
    return pl.ds(pl.multiple_of(first * SUBS, SUBS), count * SUBS)


def kept(value):
    return value.astype(BF16).astype(F32)


def added(terms):
    while len(terms) > 1:
        odd = terms[-1:] if len(terms) % 2 else []
        terms = [a + b for a, b in zip(terms[::2], terms[1::2])] + odd
    return terms[0]


def tapped(weights, rows):
    return added([w * r for w, r in zip(weights, rows)])


def each_group(groups, body):
    def step(group, carry):
        body(group)
        return carry

    lax.fori_loop(0, groups, step, 0)


def slabs(sems, pairs):
    def of(group):
        return [
            pltpu.make_async_copy(source.at[group], target.at[group], sems.at[index, group])
            for index, (source, target) in enumerate(pairs)
        ]

    return of


def start_all(copies):
    for copy in copies:
        copy.start()


def wait_all(copies):
    for copy in copies:
        copy.wait()


def earlier_rows(held, first_row, early, group, part, lanes, lead):
    steps = (held.shape[2] - first_row) // SUBS
    made = []
    for step in range(lead):
        late = held[group, part, pl.ds(first_row + (steps - lead + step) * SUBS, SUBS), :]
        first = early[part, pl.ds(HALO - lead + step, 1), lanes]
        made.append(jnp.where(sub_index() == 0, spread(first), pltpu.roll(late, 1, 0)))
    return made


def short_weights(filt_ref, lanes):
    return [
        [spread(filt_ref[part, pl.ds(k, 1), lanes]) for k in range(filt_ref.shape[1])]
        for part in range(3)
    ]


def short_chunk(weights, window):
    taps = len(weights)
    return [tapped(weights, window[at : at + taps][::-1]) for at in range(CHUNK)]


def load_rows(x_ref, cot_ref, held, cot_held, wide, sems):
    row_count, channels = cot_ref.shape
    copies = [
        pltpu.make_async_copy(x_ref.at[part] if part < 3 else cot_ref, wide.at[part], sems.at[part])
        for part in range(4)
    ]
    start_all(copies)
    perm = step_major(row_count, False)
    lead_rows = held.shape[2] - row_count
    for part, copy in enumerate(copies):
        copy.wait()
        rows = jnp.dot(perm, wide[part], preferred_element_type=F32)
        for group in range(channels // LANES):
            slab = rows[:, group * LANES : (group + 1) * LANES]
            if part < 3:
                held[group, part, pl.ds(lead_rows, row_count), :] = slab
            else:
                cot_held[group] = slab


def load_kernel(
    x_ref, cot_ref, filt_ref, rate_ref, residue_ref,
    held_ref, cot_held_ref, filt_out, rate_out, residue_out,
    wide, sems, small_sems,
):
    sources = [filt_ref, rate_ref, residue_ref]
    targets = [filt_out, rate_out, residue_out]
    copies = [
        pltpu.make_async_copy(source, target, small_sems.at[index])
        for index, (source, target) in enumerate(zip(sources, targets))
    ]
    start_all(copies)
    load_rows(x_ref, cot_ref, held_ref, cot_held_ref, wide, sems)
    wait_all(copies)


def stage_kernel(
    x_ref, cot_ref, prev_ref, filt_ref, held_out, cot_out, kv_out,
    held, cot_held, kv, early, wide, sems, out_sems,
):
    groups, row_count, _ = cot_out.shape
    lead = filt_ref.shape[1] - 1
    load_rows(x_ref, cot_ref, held, cot_held, wide, sems)
    early[...] = prev_ref[...].astype(F32)
    leaving = slabs(out_sems, [(held, held_out), (cot_held, cot_out), (kv, kv_out)])

    def one_group(group):
        lanes = pl.ds(pl.multiple_of(group * LANES, LANES), LANES)
        for part in range(3):
            rows = earlier_rows(held, lead * SUBS, early, group, part, lanes, lead)
            for step in range(lead):
                held[group, part, step_rows(step), :] = rows[step]
        weights = short_weights(filt_ref, lanes)

        def stage_chunk(index, carry):
            base = index * CHUNK
            for part in (1, 2):
                window = [held[group, part, step_rows(base + at), :] for at in range(CHUNK + lead)]
                rows = short_chunk(weights[part], window)
                for at in range(CHUNK):
                    kv[group, part - 1, step_rows(base + at), :] = rows[at]
            return carry

        lax.fori_loop(0, row_count // SUBS // CHUNK, stage_chunk, 0)
        start_all(leaving(group))

    each_group(groups, one_group)
    each_group(groups, lambda group: wait_all(leaving(group)))


def mix_kernel(
    held, prev_ref, cot_ref, filt_ref, rate_ref, gated, gradm, state_ref, early
):
    groups, row_count, _ = cot_ref.shape
    taps = filt_ref.shape[1]
    modes = rate_ref.shape[0]
    lead = taps - 1
    steps = row_count // SUBS
    early[...] = prev_ref[...].astype(F32)

    def one_group(group):
        lanes = pl.ds(pl.multiple_of(group * LANES, LANES), LANES)
        weights = short_weights(filt_ref, lanes)

        def mix_rows(base, window_of):
            key_rows = short_chunk(weights[1], window_of(1))
            value_rows = short_chunk(weights[2], window_of(2))
            for at in range(CHUNK):
                gated[group, step_rows(base + at), :] = kept(key_rows[at] * value_rows[at])
            query_rows = short_chunk(weights[0], window_of(0))
            for at in range(CHUNK):
                rows = step_rows(base + at)
                gradm[group, rows, :] = kept(cot_ref[group, rows, :] * query_rows[at])

        def inner(base, count):
            return lambda part: [
                held[group, part, step_rows(base + at), :] for at in range(count)
            ]

        def mix_chunk(index, carry):
            base = index * CHUNK
            mix_rows(base, inner(base - lead, CHUNK + lead))
            return carry

        mix_rows(
            0,
            lambda part: earlier_rows(held, 0, early, group, part, lanes, lead)
            + inner(0, CHUNK)(part),
        )
        lax.fori_loop(1, steps // CHUNK, mix_chunk, 0)
        decay = [spread(jnp.exp(-rate_ref[pl.ds(n, 1), lanes])) for n in range(modes)]

        def gather_step(step, carry):
            ends, starts = carry
            ahead = gated[group, step_rows(step), :]
            behind = gradm[group, step_rows(steps - 1 - step), :]
            return (
                [e * d + ahead for e, d in zip(ends, decay)],
                [s * d + behind for s, d in zip(starts, decay)],
            )

        zero = jnp.zeros((SUBS, LANES), F32)
        ends, starts = lax.fori_loop(
            0, steps, gather_step, ([zero] * modes, [zero] * modes), unroll=32
        )
        place = pl.ds(group, 1)
        seg = sub_index().astype(F32) * steps
        for n in range(modes):
            rate = spread(rate_ref[pl.ds(n, 1), lanes])
            to_start = jnp.exp(-rate * seg)
            to_end = jnp.exp(-rate * (steps * (SUBS - 1) - seg))
            state_ref[n, place, :] = jnp.sum(ends[n] * to_end, axis=0, keepdims=True)
            state_ref[modes + n, place, :] = jnp.sum(
                starts[n] * to_start, axis=0, keepdims=True
            )

    each_group(groups, one_group)


def chain_kernel(row_count, half, first_ref, arrived_ref, rate_ref, residue_ref, out_ref):
    blocks = arrived_ref.shape[0]
    step_decay = jnp.exp(-rate_ref[...] * row_count)
    weight = residue_ref[...] * jnp.exp(-rate_ref[...])

    def run(order):
        def body(index, carry):
            block = order(index)
            out_ref[pl.ds(block, 1)] = (carry * weight)[None]
            return carry * step_decay + arrived_ref[pl.ds(block, 1)][0]

        lax.fori_loop(0, blocks, body, jnp.zeros(rate_ref.shape, F32), unroll=32)

    @pl.when(first_ref[0] < half)
    def _():
        run(lambda index: index)

    @pl.when(first_ref[0] >= half)
    def _():
        run(lambda index: blocks - 1 - index)


def local_kernel(
    gated, gradm, residue_ref, rate_ref,
    ahead, behind, seg_out,
    seg_states, sems,
):
    groups, row_count, _ = gated.shape
    modes = rate_ref.shape[0]
    steps = row_count // SUBS
    leaving = slabs(sems, [(seg_states, seg_out)])

    def one_group(group):
        lanes = pl.ds(pl.multiple_of(group * LANES, LANES), LANES)
        weight = [spread(residue_ref[pl.ds(n, 1), lanes]) for n in range(modes)]
        rates = [rate_ref[pl.ds(n, 1), lanes] for n in range(modes)]
        decay = [spread(jnp.exp(-r)) for r in rates]
        zero = jnp.zeros((SUBS, LANES), F32)
        for source, target, backward in ((gated, ahead, False), (gradm, behind, True)):

            def scan_chunk(index, states):
                base = (steps // CHUNK - 1 - index if backward else index) * CHUNK
                values = [source[group, step_rows(base + at), :] for at in range(CHUNK)]
                made = [None] * CHUNK
                for at in range(CHUNK)[:: -1 if backward else 1]:
                    states = [s * d + values[at] for s, d in zip(states, decay)]
                    made[at] = tapped(weight, states)
                for at in range(CHUNK):
                    target[group, step_rows(base + at), :] = made[at]
                return states

            states = lax.fori_loop(0, steps // CHUNK, scan_chunk, [zero] * modes)
            sub = sub_index()
            for n in range(modes):
                span = spread(jnp.exp(-rates[n] * steps))
                total = states[n]
                for shift in (1, 2, 4):
                    if backward:
                        moved = jnp.where(
                            sub < SUBS - shift, pltpu.roll(total, SUBS - shift, 0), 0.0
                        )
                    else:
                        moved = jnp.where(sub >= shift, pltpu.roll(total, shift, 0), 0.0)
                    total = total + span * moved
                    span = span * span
                if backward:
                    enters = jnp.where(sub < SUBS - 1, pltpu.roll(total, SUBS - 1, 0), 0.0)
                else:
                    enters = jnp.where(sub >= 1, pltpu.roll(total, 1, 0), 0.0)
                seg_states[group, int(backward), n] = enters * weight[n] * decay[n]
        start_all(leaving(group))

    each_group(groups, one_group)
    each_group(groups, lambda group: wait_all(leaving(group)))


def grad_kernel(
    held_ref, cot_ref, kv_ref, seg_ref, ahead, behind, enter_ref, rate_ref,
    query_mix, key_mix, value_mix, head_ref, short_ref,
    held, cot, kv, seg_states, sems,
):
    groups, row_count, _ = cot.shape
    arriving = slabs(
        sems, [(seg_ref, seg_states), (cot_ref, cot), (held_ref, held), (kv_ref, kv)]
    )
    each_group(groups, lambda group: start_all(arriving(group)))
    modes = rate_ref.shape[0]
    steps = row_count // SUBS
    lead = held.shape[2] // SUBS - steps
    taps = lead + 1
    mix = (query_mix, key_mix, value_mix)
    short_ref[...] = jnp.zeros(short_ref.shape, F32)
    head_ref[...] = jnp.zeros(head_ref.shape, BF16)

    def one_group(group):
        lanes = pl.ds(pl.multiple_of(group * LANES, LANES), LANES)
        place = pl.ds(group, 1)
        rates = [spread(rate_ref[pl.ds(n, 1), lanes]) for n in range(modes)]
        decay = [jnp.exp(-r) for r in rates]
        seg = sub_index().astype(F32) * steps
        wait_all(arriving(group))
        for backward in (False, True):
            gap = steps * (SUBS - 1) - seg if backward else seg
            carried = []
            for n in range(modes):
                outer = spread(enter_ref[int(backward) * modes + n, place, :])
                inner = seg_states[group, int(backward), n]
                carried.append(inner + jnp.exp(-rates[n] * gap) * outer)
            parts = (1, 2) if backward else (0,)
            def grad_chunk(index, carry):
                carried, sums = carry
                base = (steps // CHUNK - 1 - index if backward else index) * CHUNK
                source = behind if backward else ahead
                long_rows = [None] * CHUNK
                for at in range(CHUNK)[:: -1 if backward else 1]:
                    long_rows[at] = source[group, step_rows(base + at), :] + added(carried)
                    carried = [c * d for c, d in zip(carried, decay)]
                new_sums = []
                for part, old in zip(parts, sums):
                    grads = []
                    for at in range(CHUNK):
                        rows = step_rows(base + at)
                        factor = cot[group, rows, :] if part == 0 else kv[group, 2 - part, rows, :]
                        grads.append(kept(long_rows[at] * factor))
                        mix[part][group, rows, :] = grads[at]
                    window = [
                        held[group, part, step_rows(base + at), :] for at in range(CHUNK + lead)
                    ]
                    new_sums.append(
                        [
                            old[k] + tapped(grads, window[lead - k : lead - k + CHUNK])
                            for k in range(taps)
                        ]
                    )
                return carried, new_sums

            zero = jnp.zeros((SUBS, LANES), F32)
            _, sums = lax.fori_loop(
                0, steps // CHUNK, grad_chunk, (carried, [[zero] * taps for _ in parts])
            )
            for part, taken in zip(parts, sums):
                for k in range(taps):
                    short_ref[part * taps + k, place, :] = jnp.sum(taken[k], axis=0, keepdims=True)
                first = [mix[part][group, pl.ds(step * SUBS, 1), :] for step in range(lead)]
                first += [jnp.zeros((1, LANES), F32)] * (HALO - lead)
                head_ref[part, :, lanes] = jnp.concatenate(first, axis=0).astype(BF16)

    each_group(groups, one_group)


def back_kernel(
    query_mix, key_mix, value_mix, next_ref, filt_ref, out_ref, late, made, wide, sems
):
    mix = (query_mix, key_mix, value_mix)
    taps = filt_ref.shape[1]
    row_count, channels = made.shape
    groups = channels // LANES
    steps = row_count // SUBS
    perm = step_major(row_count, True)
    late[...] = next_ref[...].astype(F32)
    copies = []
    for part in range(3):

        def one_group(group):
            lanes = pl.ds(pl.multiple_of(group * LANES, LANES), LANES)
            weights = [spread(filt_ref[part, pl.ds(k, 1), lanes]) for k in range(taps)]

            def back_rows(base, window):
                rows = [tapped(weights, window[at : at + taps]) for at in range(CHUNK)]
                made[step_rows(base, CHUNK), lanes] = jnp.concatenate(rows, axis=0).astype(BF16)

            def back_chunk(index, carry):
                base = index * CHUNK
                back_rows(
                    base,
                    [mix[part][group, step_rows(base + at), :] for at in range(CHUNK + taps - 1)],
                )
                return carry

            last = steps - CHUNK
            lax.fori_loop(0, last // CHUNK, back_chunk, 0)
            window = [mix[part][group, step_rows(last + at), :] for at in range(CHUNK)]
            for step in range(taps - 1):
                first = mix[part][group, step_rows(step), :]
                row = late[part, pl.ds(step, 1), lanes]
                window.append(
                    jnp.where(sub_index() == SUBS - 1, spread(row), pltpu.roll(first, SUBS - 1, 0))
                )
            back_rows(last, window)

        each_group(groups, one_group)
        wide[part] = jnp.dot(perm, made[...], preferred_element_type=F32).astype(BF16)
        copies.append(pltpu.make_async_copy(wide.at[part], out_ref.at[part], sems.at[part]))
        copies[-1].start()
    wait_all(copies)


def fold_kernel(part_ref, out_ref):
    total = jnp.sum(part_ref[...], axis=0, keepdims=True)
    out_ref[...] = jnp.broadcast_to(total, out_ref.shape)


def square_kernel(sums_ref, out_ref):
    value = sums_ref[...]
    total = jnp.sum(jnp.sum(value * value, axis=0))
    out_ref[...] = jnp.full(out_ref.shape, total, F32)


def scale_kernel(clip_limit, sums_ref, squares_ref, out_ref):
    squares = jnp.sum(squares_ref[...], axis=0, keepdims=True)
    factor = jnp.minimum(1.0, clip_limit / (jnp.sqrt(squares) + 1e-06))
    taps = out_ref.shape[1]
    for part in range(3):
        for k in range(taps):
            rows = sums_ref[part * taps + k] * factor
            for group in range(rows.shape[0]):
                out_ref[part, pl.ds(k, 1), pl.ds(group * LANES, LANES)] = rows[group : group + 1]


def passed_along(shard, by):
    length = lax.axis_size("ctx")
    pairs = [(i, i + by) for i in range(length) if 0 <= i + by < length]
    return lax.ppermute(shard, "ctx", pairs)


def exchange(blocks, axis):
    return lax.all_to_all(blocks, axis, split_axis=0, concat_axis=0, tiled=True)


def cost(flops, bytes_accessed):
    return pl.CostEstimate(flops=flops, bytes_accessed=bytes_accessed, transcendentals=0)


def per_device(inputs, cotangent, short_filter, residue, decay_rate):
    _, row_count, channels = inputs.shape
    taps = short_filter.shape[1]
    modes = residue.shape[0]
    blocks = lax.axis_size("ctx")
    groups = channels // LANES
    lead = taps - 1
    long_rows = row_count + lead * SUBS

    def shaped(dtype, *dims):
        return jax.ShapeDtypeStruct(dims, dtype)

    def near(dtype, *dims):
        return pltpu.VMEM(dims, dtype)

    def far(dtype, *dims):
        return pltpu.HBM(dims, dtype)

    def from_near(*values):
        return [pltpu.with_memory_space_constraint(v, pltpu.VMEM) for v in values]

    def from_far(*values):
        return [pltpu.with_memory_space_constraint(v, pltpu.HBM) for v in values]

    small = pltpu.CompilerParams(vmem_limit_bytes=4 << 20)
    params = pltpu.CompilerParams(vmem_limit_bytes=24 << 20)
    at_vmem = pl.BlockSpec(memory_space=pltpu.VMEM)
    at_hbm = pl.BlockSpec(memory_space=pltpu.HBM)
    sems = pltpu.SemaphoreType.DMA
    work = row_count * channels
    held_dims = (groups, 3, long_rows, LANES)
    part_dims = (groups, 3, row_count, LANES)
    row_dims = (groups, row_count, LANES)
    kv_dims = (groups, 2, row_count, LANES)
    seg_dims = (groups, 2, modes, SUBS, LANES)

    held, cot_held, filt, rate, weight = pl.pallas_call(
        load_kernel,
        in_specs=[at_hbm] * 5,
        out_specs=[at_vmem] * 5,
        out_shape=[
            near(F32, *part_dims),
            near(F32, *row_dims),
            near(F32, 3, taps, channels),
            near(F32, modes, channels),
            near(F32, modes, channels),
        ],
        scratch_shapes=[pltpu.VMEM((4, row_count, channels), BF16), sems((4,)), sems((3,))],
        compiler_params=params,
        cost_estimate=cost(work * 2000, work * 8),
        name="load",
    )(*from_far(inputs, cotangent, short_filter, decay_rate, residue))
    prev = passed_along(inputs[:, row_count - HALO :, :], 1)
    prev, held, cot_held = lax.optimization_barrier((prev, held, cot_held))
    gated, gradm, states = pl.pallas_call(
        mix_kernel,
        in_specs=[at_vmem] * 5,
        out_specs=[at_vmem] * 3,
        out_shape=[
            near(F32, *row_dims),
            near(F32, *row_dims),
            shaped(F32, 2 * modes, groups, LANES),
        ],
        scratch_shapes=[pltpu.VMEM((3, HALO, channels), F32)],
        compiler_params=params,
        cost_estimate=cost(work * 110, work * 24),
        name="mix",
    )(*from_near(held), prev, *from_near(cot_held, filt, rate))

    state_rows = 2 * modes * groups // blocks
    first = lax.axis_index("ctx") * state_rows
    half = modes * groups
    arrived = exchange(states.reshape(blocks, state_rows, LANES), "ctx")
    held, cot_held, kv = pl.pallas_call(
        stage_kernel,
        in_specs=[at_hbm] * 2 + [at_vmem] * 2,
        out_specs=[at_hbm] * 3,
        out_shape=[far(F32, *held_dims), far(F32, *row_dims), far(F32, *kv_dims)],
        scratch_shapes=[
            pltpu.VMEM(held_dims, F32),
            pltpu.VMEM(row_dims, F32),
            pltpu.VMEM(kv_dims, F32),
            pltpu.VMEM((3, HALO, channels), F32),
            pltpu.VMEM((4, row_count, channels), BF16),
            sems((4,)),
            sems((3, groups)),
        ],
        compiler_params=params,
        cost_estimate=cost(work * 2000, work * 18),
        name="stage",
    )(*from_far(inputs, cotangent), prev, filt)
    arrived, held, cot_held, kv = lax.optimization_barrier((arrived, held, cot_held, kv))


    def own_rows(values):
        rows = jnp.tile(values.reshape(half, LANES), (2, 1))
        return lax.dynamic_slice_in_dim(rows, first, state_rows, 0)

    entering = pl.pallas_call(
        functools.partial(chain_kernel, row_count, half),
        in_specs=[
            pl.BlockSpec(memory_space=pltpu.SMEM),
            at_vmem,
            at_vmem,
            at_vmem,
        ],
        out_specs=at_vmem,
        out_shape=shaped(F32, blocks, state_rows, LANES),
        compiler_params=small,
        cost_estimate=cost(blocks * state_rows * LANES * 2, blocks * state_rows * LANES * 8),
        name="chain",
    )(first[None], arrived, own_rows(decay_rate), own_rows(residue))
    entering = exchange(entering, "ctx").reshape(2 * modes, groups, LANES)

    ahead, behind, seg_states = pl.pallas_call(
        local_kernel,
        in_specs=[at_vmem] * 4,
        out_specs=[at_vmem] * 2 + [at_hbm],
        out_shape=[near(F32, *row_dims), near(F32, *row_dims), far(F32, *seg_dims)],
        scratch_shapes=[pltpu.VMEM(seg_dims, F32), sems((1, groups))],
        input_output_aliases={0: 0, 1: 1},
        compiler_params=params,
        cost_estimate=cost(work * 128, work * 18),
        name="local",
    )(*from_near(gated, gradm), weight, rate)
    entering, seg_states = lax.optimization_barrier((entering, seg_states))

    share = -(-3 * taps * groups // blocks)
    share += share % 2
    short_rows = share * blocks // groups
    *grad_mix, head, short_part = pl.pallas_call(
        grad_kernel,
        in_specs=[at_hbm] * 4 + [at_vmem] * 4,
        out_specs=[at_vmem] * 5,
        out_shape=[
            near(F32, *row_dims),
            near(F32, *row_dims),
            near(F32, *row_dims),
            shaped(BF16, 3, HALO, channels),
            far(F32, short_rows, groups, LANES),
        ],
        scratch_shapes=[
            pltpu.VMEM(held_dims, F32),
            pltpu.VMEM(row_dims, F32),
            pltpu.VMEM(kv_dims, F32),
            pltpu.VMEM(seg_dims, F32),
            sems((4, groups)),
        ],
        input_output_aliases={4: 0, 5: 1},
        compiler_params=params,
        cost_estimate=cost(work * 110, work * 30),
        name="grad",
    )(
        *from_far(held, cot_held, kv, seg_states), *from_near(ahead, behind), entering, rate
    )

    gathered = exchange(short_part.reshape(blocks, share, LANES), "ctx")
    late = passed_along(head, -1)
    own_sum = pl.pallas_call(
        fold_kernel,
        in_specs=[at_vmem],
        out_specs=at_vmem,
        out_shape=shaped(F32, blocks, share, LANES),
        compiler_params=small,
        name="fold",
    )(gathered)
    own_sum, late = lax.optimization_barrier((own_sum, late))
    all_sums = exchange(own_sum, "ctx")
    grad_inputs = pl.pallas_call(
        back_kernel,
        in_specs=[at_vmem] * 5,
        out_specs=at_hbm,
        out_shape=far(BF16, 3, row_count, channels),
        scratch_shapes=[
            pltpu.VMEM((3, HALO, channels), F32),
            pltpu.VMEM((row_count, channels), BF16),
            pltpu.VMEM((3, row_count, channels), BF16),
            sems((3,)),
        ],
        compiler_params=params,
        cost_estimate=cost(work * 48, work * 12),
        name="back",
    )(*from_near(*grad_mix), late, filt)
    all_sums, grad_inputs = lax.optimization_barrier((all_sums, grad_inputs))
    all_sums = all_sums.reshape(short_rows, groups, LANES)
    tp_count = lax.axis_size("tp")
    squares = pl.pallas_call(
        square_kernel,
        in_specs=[at_vmem],
        out_specs=at_vmem,
        out_shape=shaped(F32, tp_count, LANES),
        compiler_params=small,
        name="square",
    )(all_sums)
    squares = exchange(squares, "tp")
    clip_limit = math.sqrt(3 * channels * tp_count * taps)
    grad_short = pl.pallas_call(
        functools.partial(scale_kernel, clip_limit),
        in_specs=[at_vmem, at_vmem],
        out_specs=at_vmem,
        out_shape=shaped(F32, 3, taps, channels),
        compiler_params=small,
        name="scale",
    )(all_sums, squares)
    return (grad_inputs, grad_short)


def solution(mesh):
    return jax.shard_map(
        per_device,
        mesh=mesh,
        in_specs=(
            P(None, "ctx", "tp"),
            P("ctx", "tp"),
            P(None, None, "tp"),
            P(None, "tp"),
            P(None, "tp"),
        ),
        out_specs=(P(None, "ctx", "tp"), P(None, None, "tp")),
        check_vma=False,
    )
```

```python
import functools
import math

import jax
import jax.numpy as jnp
from jax import lax
from jax.experimental import pallas as pl
from jax.experimental.pallas import tpu as pltpu
from jax.sharding import PartitionSpec as P

LANES = 128
SUBS = 8
HALO = 8
CHUNK = 16
LINES = 4
F32 = jnp.float32
BF16 = jnp.bfloat16


def sub_index():
    return lax.broadcasted_iota(jnp.int32, (SUBS, LANES), 0)


def step_major(row_count, inverse):
    kept = lax.broadcasted_iota(jnp.int32, (row_count, row_count), 1 if inverse else 0)
    time = lax.broadcasted_iota(jnp.int32, (row_count, row_count), 0 if inverse else 1)
    source = (kept & (SUBS - 1)) * (row_count // SUBS) + (kept >> 3)
    return jnp.where(source == time, 1.0, 0.0).astype(BF16)


def spread(row):
    return jnp.broadcast_to(row, (SUBS, LANES))


def step_rows(first, count=1):
    return pl.ds(pl.multiple_of(first * SUBS, SUBS), count * SUBS)


def kept(value):
    return value.astype(BF16).astype(F32)


def added(terms):
    while len(terms) > 1:
        odd = terms[-1:] if len(terms) % 2 else []
        terms = [a + b for a, b in zip(terms[::2], terms[1::2])] + odd
    return terms[0]


def tapped(weights, rows):
    return added([w * r for w, r in zip(weights, rows)])


def each_group(groups, body):
    def step(group, carry):
        body(group)
        return carry

    lax.fori_loop(0, groups, step, 0)


def slabs(sems, pairs):
    def of(group):
        return [
            pltpu.make_async_copy(source.at[group], target.at[group], sems.at[index, group])
            for index, (source, target) in enumerate(pairs)
        ]

    return of


def start_all(copies):
    for copy in copies:
        copy.start()


def wait_all(copies):
    for copy in copies:
        copy.wait()


def earlier_rows(held, first_row, early, group, part, lanes, lead):
    steps = (held.shape[2] - first_row) // SUBS
    made = []
    for step in range(lead):
        late = held[group, part, pl.ds(first_row + (steps - lead + step) * SUBS, SUBS), :]
        first = early[part, pl.ds(HALO - lead + step, 1), lanes]
        made.append(jnp.where(sub_index() == 0, spread(first), pltpu.roll(late, 1, 0)))
    return made


def short_weights(filt_ref, lanes):
    return [
        [spread(filt_ref[part, pl.ds(k, 1), lanes]) for k in range(filt_ref.shape[1])]
        for part in range(3)
    ]


def short_chunk(weights, window):
    taps = len(weights)
    return [tapped(weights, window[at : at + taps][::-1]) for at in range(CHUNK)]


def load_rows(x_ref, cot_ref, held, cot_held, wide, sems):
    row_count, channels = cot_ref.shape
    copies = [
        pltpu.make_async_copy(x_ref.at[part] if part < 3 else cot_ref, wide.at[part], sems.at[part])
        for part in range(4)
    ]
    start_all(copies)
    perm = step_major(row_count, False)
    lead_rows = held.shape[2] - row_count
    for part, copy in enumerate(copies):
        copy.wait()
        rows = jnp.dot(perm, wide[part], preferred_element_type=F32)
        for group in range(channels // LANES):
            slab = rows[:, group * LANES : (group + 1) * LANES]
            if part < 3:
                held[group, part, pl.ds(lead_rows, row_count), :] = slab
            else:
                cot_held[group] = slab


def load_kernel(
    x_ref, cot_ref, filt_ref, rate_ref, residue_ref,
    held_ref, cot_held_ref, filt_out, rate_out, residue_out,
    wide, sems, small_sems,
):
    sources = [filt_ref, rate_ref, residue_ref]
    targets = [filt_out, rate_out, residue_out]
    copies = [
        pltpu.make_async_copy(source, target, small_sems.at[index])
        for index, (source, target) in enumerate(zip(sources, targets))
    ]
    start_all(copies)
    load_rows(x_ref, cot_ref, held_ref, cot_held_ref, wide, sems)
    wait_all(copies)


def stage_kernel(
    x_ref, cot_ref, prev_ref, filt_ref, held_out, cot_out, kv_out,
    held, cot_held, kv, early, wide, sems, out_sems,
):
    groups, row_count, _ = cot_out.shape
    lead = filt_ref.shape[1] - 1
    load_rows(x_ref, cot_ref, held, cot_held, wide, sems)
    early[...] = prev_ref[...].astype(F32)
    leaving = slabs(out_sems, [(held, held_out), (cot_held, cot_out), (kv, kv_out)])

    def one_group(group):
        lanes = pl.ds(pl.multiple_of(group * LANES, LANES), LANES)
        for part in range(3):
            rows = earlier_rows(held, lead * SUBS, early, group, part, lanes, lead)
            for step in range(lead):
                held[group, part, step_rows(step), :] = rows[step]
        weights = short_weights(filt_ref, lanes)

        def stage_chunk(index, carry):
            base = index * CHUNK
            for part in (1, 2):
                window = [held[group, part, step_rows(base + at), :] for at in range(CHUNK + lead)]
                rows = short_chunk(weights[part], window)
                for at in range(CHUNK):
                    kv[group, part - 1, step_rows(base + at), :] = rows[at]
            return carry

        lax.fori_loop(0, row_count // SUBS // CHUNK, stage_chunk, 0)
        start_all(leaving(group))

    each_group(groups, one_group)
    each_group(groups, lambda group: wait_all(leaving(group)))


def mix_kernel(
    held, prev_ref, cot_ref, filt_ref, rate_ref, gated, gradm, state_ref, early
):
    groups, row_count, _ = cot_ref.shape
    taps = filt_ref.shape[1]
    modes = rate_ref.shape[0]
    lead = taps - 1
    steps = row_count // SUBS
    early[...] = prev_ref[...].astype(F32)

    def one_group(group):
        lanes = pl.ds(pl.multiple_of(group * LANES, LANES), LANES)
        weights = short_weights(filt_ref, lanes)

        def mix_rows(base, window_of):
            key_rows = short_chunk(weights[1], window_of(1))
            value_rows = short_chunk(weights[2], window_of(2))
            for at in range(CHUNK):
                gated[group, step_rows(base + at), :] = kept(key_rows[at] * value_rows[at])
            query_rows = short_chunk(weights[0], window_of(0))
            for at in range(CHUNK):
                rows = step_rows(base + at)
                gradm[group, rows, :] = kept(cot_ref[group, rows, :] * query_rows[at])

        def inner(base, count):
            return lambda part: [
                held[group, part, step_rows(base + at), :] for at in range(count)
            ]

        def mix_chunk(index, carry):
            base = index * CHUNK
            mix_rows(base, inner(base - lead, CHUNK + lead))
            return carry

        mix_rows(
            0,
            lambda part: earlier_rows(held, 0, early, group, part, lanes, lead)
            + inner(0, CHUNK)(part),
        )
        lax.fori_loop(1, steps // CHUNK, mix_chunk, 0)
        decay = [spread(jnp.exp(-rate_ref[pl.ds(n, 1), lanes])) for n in range(modes)]

        def gather_step(step, carry):
            ends, starts = carry
            ahead = gated[group, step_rows(step), :]
            behind = gradm[group, step_rows(steps - 1 - step), :]
            return (
                [e * d + ahead for e, d in zip(ends, decay)],
                [s * d + behind for s, d in zip(starts, decay)],
            )

        zero = jnp.zeros((SUBS, LANES), F32)
        ends, starts = lax.fori_loop(
            0, steps, gather_step, ([zero] * modes, [zero] * modes), unroll=32
        )
        place = pl.ds(group, 1)
        seg = sub_index().astype(F32) * steps
        for n in range(modes):
            rate = spread(rate_ref[pl.ds(n, 1), lanes])
            to_start = jnp.exp(-rate * seg)
            to_end = jnp.exp(-rate * (steps * (SUBS - 1) - seg))
            state_ref[n, place, :] = jnp.sum(ends[n] * to_end, axis=0, keepdims=True)
            state_ref[modes + n, place, :] = jnp.sum(
                starts[n] * to_start, axis=0, keepdims=True
            )

    each_group(groups, one_group)


def chain_kernel(row_count, half, first_ref, arrived_ref, rate_ref, residue_ref, out_ref):
    blocks = arrived_ref.shape[0]
    step_decay = jnp.exp(-rate_ref[...] * row_count)
    weight = residue_ref[...] * jnp.exp(-rate_ref[...])

    def run(order):
        def body(index, carry):
            block = order(index)
            out_ref[pl.ds(block, 1)] = (carry * weight)[None]
            return carry * step_decay + arrived_ref[pl.ds(block, 1)][0]

        lax.fori_loop(0, blocks, body, jnp.zeros(rate_ref.shape, F32), unroll=32)

    @pl.when(first_ref[0] < half)
    def _():
        run(lambda index: index)

    @pl.when(first_ref[0] >= half)
    def _():
        run(lambda index: blocks - 1 - index)


def local_kernel(
    gated, gradm, residue_ref, rate_ref,
    ahead, behind, seg_out,
    seg_states, sems,
):
    groups, row_count, _ = gated.shape
    modes = rate_ref.shape[0]
    steps = row_count // SUBS
    leaving = slabs(sems, [(seg_states, seg_out)])

    def one_group(group):
        lanes = pl.ds(pl.multiple_of(group * LANES, LANES), LANES)
        weight = [spread(residue_ref[pl.ds(n, 1), lanes]) for n in range(modes)]
        rates = [rate_ref[pl.ds(n, 1), lanes] for n in range(modes)]
        decay = [spread(jnp.exp(-r)) for r in rates]
        zero = jnp.zeros((SUBS, LANES), F32)
        for source, target, backward in ((gated, ahead, False), (gradm, behind, True)):

            def scan_chunk(index, states):
                base = (steps // CHUNK - 1 - index if backward else index) * CHUNK
                values = [source[group, step_rows(base + at), :] for at in range(CHUNK)]
                made = [None] * CHUNK
                for at in range(CHUNK)[:: -1 if backward else 1]:
                    states = [s * d + values[at] for s, d in zip(states, decay)]
                    made[at] = tapped(weight, states)
                for at in range(CHUNK):
                    target[group, step_rows(base + at), :] = made[at]
                return states

            states = lax.fori_loop(0, steps // CHUNK, scan_chunk, [zero] * modes)
            sub = sub_index()
            for n in range(modes):
                span = spread(jnp.exp(-rates[n] * steps))
                total = states[n]
                for shift in (1, 2, 4):
                    if backward:
                        moved = jnp.where(
                            sub < SUBS - shift, pltpu.roll(total, SUBS - shift, 0), 0.0
                        )
                    else:
                        moved = jnp.where(sub >= shift, pltpu.roll(total, shift, 0), 0.0)
                    total = total + span * moved
                    span = span * span
                if backward:
                    enters = jnp.where(sub < SUBS - 1, pltpu.roll(total, SUBS - 1, 0), 0.0)
                else:
                    enters = jnp.where(sub >= 1, pltpu.roll(total, 1, 0), 0.0)
                seg_states[group, int(backward), n] = enters * weight[n] * decay[n]
        start_all(leaving(group))

    each_group(groups, one_group)
    each_group(groups, lambda group: wait_all(leaving(group)))


def grad_kernel(
    share, held_ref, cot_ref, kv_ref, seg_ref, ahead, behind, enter_ref, rate_ref,
    query_mix, key_mix, value_mix, head_ref, short_ref,
    held, cot, kv, seg_states, sems,
):
    groups, row_count, _ = cot.shape
    arriving = slabs(
        sems, [(seg_ref, seg_states), (cot_ref, cot), (held_ref, held), (kv_ref, kv)]
    )
    each_group(groups, lambda group: start_all(arriving(group)))
    modes = rate_ref.shape[0]
    steps = row_count // SUBS
    lead = held.shape[2] // SUBS - steps
    taps = lead + 1
    mix = (query_mix, key_mix, value_mix)
    short_ref[...] = jnp.zeros(short_ref.shape, F32)
    head_ref[...] = jnp.zeros(head_ref.shape, BF16)

    def one_group(group):
        lanes = pl.ds(pl.multiple_of(group * LANES, LANES), LANES)
        place = pl.ds(group, 1)
        rates = [spread(rate_ref[pl.ds(n, 1), lanes]) for n in range(modes)]
        decay = [jnp.exp(-r) for r in rates]
        seg = sub_index().astype(F32) * steps
        wait_all(arriving(group))
        for backward in (False, True):
            gap = steps * (SUBS - 1) - seg if backward else seg
            carried = []
            for n in range(modes):
                outer = spread(enter_ref[int(backward) * modes + n, place, :])
                inner = seg_states[group, int(backward), n]
                carried.append(inner + jnp.exp(-rates[n] * gap) * outer)
            parts = (1, 2) if backward else (0,)
            def grad_chunk(index, carry):
                carried, sums = carry
                base = (steps // CHUNK - 1 - index if backward else index) * CHUNK
                source = behind if backward else ahead
                long_rows = [None] * CHUNK
                for at in range(CHUNK)[:: -1 if backward else 1]:
                    long_rows[at] = source[group, step_rows(base + at), :] + added(carried)
                    carried = [c * d for c, d in zip(carried, decay)]
                new_sums = []
                for part, old in zip(parts, sums):
                    grads = []
                    for at in range(CHUNK):
                        rows = step_rows(base + at)
                        factor = cot[group, rows, :] if part == 0 else kv[group, 2 - part, rows, :]
                        grads.append(kept(long_rows[at] * factor))
                        mix[part][group, rows, :] = grads[at]
                    window = [
                        held[group, part, step_rows(base + at), :] for at in range(CHUNK + lead)
                    ]
                    new_sums.append(
                        [
                            old[k] + tapped(grads, window[lead - k : lead - k + CHUNK])
                            for k in range(taps)
                        ]
                    )
                return carried, new_sums

            zero = jnp.zeros((SUBS, LANES), F32)
            _, sums = lax.fori_loop(
                0, steps // CHUNK, grad_chunk, (carried, [[zero] * taps for _ in parts])
            )
            for part, taken in zip(parts, sums):
                for k in range(taps):
                    row = (part * taps + k) * groups + group
                    short_ref[row // share, pl.ds(row % share, 1), :] = jnp.sum(
                        taken[k], axis=0, keepdims=True
                    )
                first = [mix[part][group, pl.ds(step * SUBS, 1), :] for step in range(lead)]
                first += [jnp.zeros((1, LANES), F32)] * (HALO - lead)
                head_ref[part, :, lanes] = jnp.concatenate(first, axis=0).astype(BF16)

    each_group(groups, one_group)


def back_kernel(
    query_mix, key_mix, value_mix, next_ref, filt_ref, out_ref, late, made, wide, sems
):
    mix = (query_mix, key_mix, value_mix)
    taps = filt_ref.shape[1]
    row_count, channels = made.shape
    groups = channels // LANES
    steps = row_count // SUBS
    perm = step_major(row_count, True)
    late[...] = next_ref[...].astype(F32)
    copies = []
    for part in range(3):

        def one_group(group):
            lanes = pl.ds(pl.multiple_of(group * LANES, LANES), LANES)
            weights = [spread(filt_ref[part, pl.ds(k, 1), lanes]) for k in range(taps)]

            def back_rows(base, window):
                rows = [tapped(weights, window[at : at + taps]) for at in range(CHUNK)]
                made[step_rows(base, CHUNK), lanes] = jnp.concatenate(rows, axis=0).astype(BF16)

            def back_chunk(index, carry):
                base = index * CHUNK
                back_rows(
                    base,
                    [mix[part][group, step_rows(base + at), :] for at in range(CHUNK + taps - 1)],
                )
                return carry

            last = steps - CHUNK
            lax.fori_loop(0, last // CHUNK, back_chunk, 0)
            window = [mix[part][group, step_rows(last + at), :] for at in range(CHUNK)]
            for step in range(taps - 1):
                first = mix[part][group, step_rows(step), :]
                row = late[part, pl.ds(step, 1), lanes]
                window.append(
                    jnp.where(sub_index() == SUBS - 1, spread(row), pltpu.roll(first, SUBS - 1, 0))
                )
            back_rows(last, window)

        each_group(groups, one_group)
        wide[part] = jnp.dot(perm, made[...], preferred_element_type=F32).astype(BF16)
        copies.append(pltpu.make_async_copy(wide.at[part], out_ref.at[part], sems.at[part]))
        copies[-1].start()
    wait_all(copies)


def line_kernel(part_ref, out_ref):
    columns = out_ref.shape[1]
    lines = part_ref.shape[0] // columns
    for column in range(columns):
        total = added([part_ref[line * columns + column] for line in range(lines)])
        for plane in range(out_ref.shape[0]):
            out_ref[plane, column] = total.astype(BF16)


def plane_kernel(share, part_ref, out_ref):
    planes, columns, rows, _ = part_ref.shape
    totals = [
        added([part_ref[plane, column].astype(F32) for plane in range(planes)])
        for column in range(columns)
    ]
    squares = jnp.sum(added([total * total for total in totals]))
    at_row = lax.broadcasted_iota(jnp.int32, (rows, LANES), 0)
    for column in range(columns):
        marked = jnp.where(at_row == share, squares, totals[column])
        for line in range(out_ref.shape[0] // columns):
            out_ref[line * columns + column] = marked


def scale_kernel(clip_limit, share, sums_ref, out_ref):
    squares = added([sums_ref[piece, share : share + 1, :] for piece in range(sums_ref.shape[0])])
    factor = jnp.minimum(1.0, clip_limit / (jnp.sqrt(squares) + 1e-06))
    _, taps, channels = out_ref.shape
    groups = channels // LANES
    for part in range(3):
        for k in range(taps):
            for group in range(groups):
                piece, row = divmod((part * taps + k) * groups + group, share)
                out_ref[part, k : k + 1, pl.ds(group * LANES, LANES)] = (
                    sums_ref[piece, row : row + 1, :] * factor
                )


def passed_along(shard, by):
    length = lax.axis_size("ctx")
    pairs = [(i, i + by) for i in range(length) if 0 <= i + by < length]
    return lax.ppermute(shard, "ctx", pairs)


def exchange(blocks, axis, members=None):
    return lax.all_to_all(
        blocks, axis, split_axis=0, concat_axis=0, tiled=True, axis_index_groups=members
    )


def cost(flops, bytes_accessed):
    return pl.CostEstimate(flops=flops, bytes_accessed=bytes_accessed, transcendentals=0)


def per_device(inputs, cotangent, short_filter, residue, decay_rate):
    _, row_count, channels = inputs.shape
    taps = short_filter.shape[1]
    modes = residue.shape[0]
    blocks = lax.axis_size("ctx")
    groups = channels // LANES
    lead = taps - 1
    long_rows = row_count + lead * SUBS

    def shaped(dtype, *dims):
        return jax.ShapeDtypeStruct(dims, dtype)

    def near(dtype, *dims):
        return pltpu.VMEM(dims, dtype)

    def far(dtype, *dims):
        return pltpu.HBM(dims, dtype)

    def from_near(*values):
        return [pltpu.with_memory_space_constraint(v, pltpu.VMEM) for v in values]

    def from_far(*values):
        return [pltpu.with_memory_space_constraint(v, pltpu.HBM) for v in values]

    small = pltpu.CompilerParams(vmem_limit_bytes=4 << 20)
    params = pltpu.CompilerParams(vmem_limit_bytes=24 << 20)
    at_vmem = pl.BlockSpec(memory_space=pltpu.VMEM)
    at_hbm = pl.BlockSpec(memory_space=pltpu.HBM)
    sems = pltpu.SemaphoreType.DMA
    work = row_count * channels
    held_dims = (groups, 3, long_rows, LANES)
    part_dims = (groups, 3, row_count, LANES)
    row_dims = (groups, row_count, LANES)
    kv_dims = (groups, 2, row_count, LANES)
    seg_dims = (groups, 2, modes, SUBS, LANES)

    held, cot_held, filt, rate, weight = pl.pallas_call(
        load_kernel,
        in_specs=[at_hbm] * 5,
        out_specs=[at_vmem] * 5,
        out_shape=[
            near(F32, *part_dims),
            near(F32, *row_dims),
            near(F32, 3, taps, channels),
            near(F32, modes, channels),
            near(F32, modes, channels),
        ],
        scratch_shapes=[pltpu.VMEM((4, row_count, channels), BF16), sems((4,)), sems((3,))],
        compiler_params=params,
        cost_estimate=cost(work * 2000, work * 8),
        name="load",
    )(*from_far(inputs, cotangent, short_filter, decay_rate, residue))
    prev = passed_along(inputs[:, row_count - HALO :, :], 1)
    prev, held, cot_held = lax.optimization_barrier((prev, held, cot_held))
    gated, gradm, states = pl.pallas_call(
        mix_kernel,
        in_specs=[at_vmem] * 5,
        out_specs=[at_vmem] * 3,
        out_shape=[
            near(F32, *row_dims),
            near(F32, *row_dims),
            shaped(F32, 2 * modes, groups, LANES),
        ],
        scratch_shapes=[pltpu.VMEM((3, HALO, channels), F32)],
        compiler_params=params,
        cost_estimate=cost(work * 110, work * 24),
        name="mix",
    )(*from_near(held), prev, *from_near(cot_held, filt, rate))

    state_rows = 2 * modes * groups // blocks
    first = lax.axis_index("ctx") * state_rows
    half = modes * groups
    arrived = exchange(states.reshape(blocks, state_rows, LANES), "ctx")
    held, cot_held, kv = pl.pallas_call(
        stage_kernel,
        in_specs=[at_hbm] * 2 + [at_vmem] * 2,
        out_specs=[at_hbm] * 3,
        out_shape=[far(F32, *held_dims), far(F32, *row_dims), far(F32, *kv_dims)],
        scratch_shapes=[
            pltpu.VMEM(held_dims, F32),
            pltpu.VMEM(row_dims, F32),
            pltpu.VMEM(kv_dims, F32),
            pltpu.VMEM((3, HALO, channels), F32),
            pltpu.VMEM((4, row_count, channels), BF16),
            sems((4,)),
            sems((3, groups)),
        ],
        compiler_params=params,
        cost_estimate=cost(work * 2000, work * 18),
        name="stage",
    )(*from_far(inputs, cotangent), prev, filt)
    arrived, held, cot_held, kv = lax.optimization_barrier((arrived, held, cot_held, kv))


    def own_rows(values):
        rows = jnp.tile(values.reshape(half, LANES), (2, 1))
        return lax.dynamic_slice_in_dim(rows, first, state_rows, 0)

    entering = pl.pallas_call(
        functools.partial(chain_kernel, row_count, half),
        in_specs=[
            pl.BlockSpec(memory_space=pltpu.SMEM),
            at_vmem,
            at_vmem,
            at_vmem,
        ],
        out_specs=at_vmem,
        out_shape=shaped(F32, blocks, state_rows, LANES),
        compiler_params=small,
        cost_estimate=cost(blocks * state_rows * LANES * 2, blocks * state_rows * LANES * 8),
        name="chain",
    )(first[None], arrived, own_rows(decay_rate), own_rows(residue))
    entering = exchange(entering, "ctx").reshape(2 * modes, groups, LANES)

    ahead, behind, seg_states = pl.pallas_call(
        local_kernel,
        in_specs=[at_vmem] * 4,
        out_specs=[at_vmem] * 2 + [at_hbm],
        out_shape=[near(F32, *row_dims), near(F32, *row_dims), far(F32, *seg_dims)],
        scratch_shapes=[pltpu.VMEM(seg_dims, F32), sems((1, groups))],
        input_output_aliases={0: 0, 1: 1},
        compiler_params=params,
        cost_estimate=cost(work * 128, work * 18),
        name="local",
    )(*from_near(gated, gradm), weight, rate)
    entering, seg_states = lax.optimization_barrier((entering, seg_states))

    tp_count = lax.axis_size("tp")
    planes = blocks // LINES
    in_plane = LINES * tp_count
    share = -(-3 * taps * groups // in_plane)
    piece_rows = -(-(share + 1) // SUBS) * SUBS
    plane_members = [
        [(y * planes + z) * tp_count + m for y in range(LINES) for m in range(tp_count)]
        for z in range(planes)
    ]
    line_members = [[y * planes + z for z in range(planes)] for y in range(LINES)]
    *grad_mix, head, short_part = pl.pallas_call(
        functools.partial(grad_kernel, share),
        in_specs=[at_hbm] * 4 + [at_vmem] * 4,
        out_specs=[at_vmem] * 5,
        out_shape=[
            near(F32, *row_dims),
            near(F32, *row_dims),
            near(F32, *row_dims),
            shaped(BF16, 3, HALO, channels),
            far(F32, in_plane, piece_rows, LANES),
        ],
        scratch_shapes=[
            pltpu.VMEM(held_dims, F32),
            pltpu.VMEM(row_dims, F32),
            pltpu.VMEM(kv_dims, F32),
            pltpu.VMEM(seg_dims, F32),
            sems((4, groups)),
        ],
        input_output_aliases={4: 0, 5: 1},
        compiler_params=params,
        cost_estimate=cost(work * 110, work * 30),
        name="grad",
    )(
        *from_far(held, cot_held, kv, seg_states), *from_near(ahead, behind), entering, rate
    )

    gathered = exchange(short_part, ("ctx", "tp"), plane_members)
    late = passed_along(head, -1)
    own_sum = pl.pallas_call(
        line_kernel,
        in_specs=[at_vmem],
        out_specs=at_vmem,
        out_shape=shaped(BF16, planes, tp_count, piece_rows, LANES),
        compiler_params=small,
        name="line",
    )(gathered)
    own_sum, late = lax.optimization_barrier((own_sum, late))
    all_sums = exchange(own_sum, "ctx", line_members)
    grad_inputs = pl.pallas_call(
        back_kernel,
        in_specs=[at_vmem] * 5,
        out_specs=at_hbm,
        out_shape=far(BF16, 3, row_count, channels),
        scratch_shapes=[
            pltpu.VMEM((3, HALO, channels), F32),
            pltpu.VMEM((row_count, channels), BF16),
            pltpu.VMEM((3, row_count, channels), BF16),
            sems((3,)),
        ],
        compiler_params=params,
        cost_estimate=cost(work * 48, work * 12),
        name="back",
    )(*from_near(*grad_mix), late, filt)
    all_sums, grad_inputs = lax.optimization_barrier((all_sums, grad_inputs))
    all_sums = pl.pallas_call(
        functools.partial(plane_kernel, share),
        in_specs=[at_vmem],
        out_specs=at_vmem,
        out_shape=shaped(F32, in_plane, piece_rows, LANES),
        compiler_params=small,
        name="plane",
    )(all_sums)
    all_sums = exchange(all_sums, ("ctx", "tp"), plane_members)
    clip_limit = math.sqrt(3 * channels * tp_count * taps)
    grad_short = pl.pallas_call(
        functools.partial(scale_kernel, clip_limit, share),
        in_specs=[at_vmem],
        out_specs=at_vmem,
        out_shape=shaped(F32, 3, taps, channels),
        compiler_params=small,
        name="scale",
    )(all_sums)
    return (grad_inputs, grad_short)


def solution(mesh):
    return jax.shard_map(
        per_device,
        mesh=mesh,
        in_specs=(
            P(None, "ctx", "tp"),
            P("ctx", "tp"),
            P(None, None, "tp"),
            P(None, "tp"),
            P(None, "tp"),
        ),
        out_specs=(P(None, "ctx", "tp"), P(None, None, "tp")),
        check_vma=False,
    )
```

```python
import functools
import math

import jax
import jax.numpy as jnp
from jax import lax
from jax.experimental import pallas as pl
from jax.experimental.pallas import tpu as pltpu
from jax.sharding import PartitionSpec as P

LANES = 128
SUBS = 8
HALO = 8
CHUNK = 16
LINES = 4
F32 = jnp.float32
BF16 = jnp.bfloat16


def sub_index():
    return lax.broadcasted_iota(jnp.int32, (SUBS, LANES), 0)


def step_major(row_count, inverse):
    kept = lax.broadcasted_iota(jnp.int32, (row_count, row_count), 1 if inverse else 0)
    time = lax.broadcasted_iota(jnp.int32, (row_count, row_count), 0 if inverse else 1)
    source = (kept & (SUBS - 1)) * (row_count // SUBS) + (kept >> 3)
    return jnp.where(source == time, 1.0, 0.0).astype(BF16)


def spread(row):
    return jnp.broadcast_to(row, (SUBS, LANES))


def step_rows(first, count=1):
    return pl.ds(pl.multiple_of(first * SUBS, SUBS), count * SUBS)


def kept(value):
    return value.astype(BF16).astype(F32)


def added(terms):
    while len(terms) > 1:
        odd = terms[-1:] if len(terms) % 2 else []
        terms = [a + b for a, b in zip(terms[::2], terms[1::2])] + odd
    return terms[0]


def tapped(weights, rows):
    return added([w * r for w, r in zip(weights, rows)])


def each_group(groups, body):
    def step(group, carry):
        body(group)
        return carry

    lax.fori_loop(0, groups, step, 0)


def slabs(sems, pairs):
    def of(group):
        return [
            pltpu.make_async_copy(source.at[group], target.at[group], sems.at[index, group])
            for index, (source, target) in enumerate(pairs)
        ]

    return of


def start_all(copies):
    for copy in copies:
        copy.start()


def wait_all(copies):
    for copy in copies:
        copy.wait()


def earlier_rows(held, first_row, early, group, part, lanes, lead):
    steps = (held.shape[2] - first_row) // SUBS
    made = []
    for step in range(lead):
        late = held[group, part, pl.ds(first_row + (steps - lead + step) * SUBS, SUBS), :]
        first = early[part, pl.ds(HALO - lead + step, 1), lanes]
        made.append(jnp.where(sub_index() == 0, spread(first), pltpu.roll(late, 1, 0)))
    return made


def short_weights(filt_ref, lanes):
    return [
        [spread(filt_ref[part, pl.ds(k, 1), lanes]) for k in range(filt_ref.shape[1])]
        for part in range(3)
    ]


def short_chunk(weights, window):
    taps = len(weights)
    return [tapped(weights, window[at : at + taps][::-1]) for at in range(CHUNK)]


def load_rows(sources, targets, wide, sems):
    row_count, channels = sources[0].shape
    copies = [
        pltpu.make_async_copy(source, wide.at[part], sems.at[part])
        for part, source in enumerate(sources)
    ]
    start_all(copies)
    perm = step_major(row_count, False)
    for part, copy in enumerate(copies):
        copy.wait()
        rows = jnp.dot(perm, wide[part], preferred_element_type=F32)
        for group in range(channels // LANES):
            slab = rows[:, group * LANES : (group + 1) * LANES]
            targets[part](group)[...] = slab


def load_kernel(
    x_ref, cot_ref, filt_ref, rate_ref, residue_ref,
    held_ref, cot_held_ref, filt_out, rate_out, residue_out,
    wide, sems, small_sems,
):
    sources = [filt_ref, rate_ref, residue_ref]
    targets = [filt_out, rate_out, residue_out]
    copies = [
        pltpu.make_async_copy(source, target, small_sems.at[index])
        for index, (source, target) in enumerate(zip(sources, targets))
    ]
    start_all(copies)
    load_rows(
        [x_ref.at[part] for part in range(3)] + [cot_ref],
        [lambda group, part=part: held_ref.at[group, part] for part in range(3)]
        + [lambda group: cot_held_ref.at[group]],
        wide,
        sems,
    )
    wait_all(copies)


def stage_kernel(
    x_ref, filt_in, prev_ref, held_out, kv_out,
    held, kv, filt_ref, early, wide, sems, filt_sem, out_sems,
):
    filt_copy = pltpu.make_async_copy(filt_in, filt_ref, filt_sem.at[0])
    filt_copy.start()
    groups, _, row_count, _ = kv_out.shape
    lead = filt_ref.shape[1] - 1
    below = pl.ds(lead * SUBS, row_count)
    load_rows(
        [x_ref.at[part] for part in range(3)],
        [lambda group, part=part: held.at[group, part, below, :] for part in range(3)],
        wide,
        sems,
    )
    early[...] = prev_ref[...].astype(F32)
    leaving = slabs(out_sems, [(held, held_out), (kv, kv_out)])
    filt_copy.wait()

    def one_group(group):
        lanes = pl.ds(pl.multiple_of(group * LANES, LANES), LANES)
        for part in range(3):
            rows = earlier_rows(held, lead * SUBS, early, group, part, lanes, lead)
            for step in range(lead):
                held[group, part, step_rows(step), :] = rows[step]
        weights = short_weights(filt_ref, lanes)

        def stage_chunk(index, carry):
            base = index * CHUNK
            for part in (1, 2):
                window = [held[group, part, step_rows(base + at), :] for at in range(CHUNK + lead)]
                rows = short_chunk(weights[part], window)
                for at in range(CHUNK):
                    kv[group, part - 1, step_rows(base + at), :] = rows[at]
            return carry

        lax.fori_loop(0, row_count // SUBS // CHUNK, stage_chunk, 0)
        start_all(leaving(group))

    each_group(groups, one_group)
    each_group(groups, lambda group: wait_all(leaving(group)))


def mix_kernel(
    held, prev_ref, cot_ref, filt_ref, rate_ref, gated, gradm, state_ref, early
):
    groups, row_count, _ = cot_ref.shape
    taps = filt_ref.shape[1]
    modes = rate_ref.shape[0]
    lead = taps - 1
    steps = row_count // SUBS
    early[...] = prev_ref[...].astype(F32)

    def one_group(group):
        lanes = pl.ds(pl.multiple_of(group * LANES, LANES), LANES)
        weights = short_weights(filt_ref, lanes)

        def mix_rows(base, window_of):
            key_rows = short_chunk(weights[1], window_of(1))
            value_rows = short_chunk(weights[2], window_of(2))
            for at in range(CHUNK):
                gated[group, step_rows(base + at), :] = kept(key_rows[at] * value_rows[at])
            query_rows = short_chunk(weights[0], window_of(0))
            for at in range(CHUNK):
                rows = step_rows(base + at)
                gradm[group, rows, :] = kept(cot_ref[group, rows, :] * query_rows[at])

        def inner(base, count):
            return lambda part: [
                held[group, part, step_rows(base + at), :] for at in range(count)
            ]

        def mix_chunk(index, carry):
            base = index * CHUNK
            mix_rows(base, inner(base - lead, CHUNK + lead))
            return carry

        mix_rows(
            0,
            lambda part: earlier_rows(held, 0, early, group, part, lanes, lead)
            + inner(0, CHUNK)(part),
        )
        lax.fori_loop(1, steps // CHUNK, mix_chunk, 0)
        decay = [spread(jnp.exp(-rate_ref[pl.ds(n, 1), lanes])) for n in range(modes)]

        def gather_step(step, carry):
            ends, starts = carry
            ahead = gated[group, step_rows(step), :]
            behind = gradm[group, step_rows(steps - 1 - step), :]
            return (
                [e * d + ahead for e, d in zip(ends, decay)],
                [s * d + behind for s, d in zip(starts, decay)],
            )

        zero = jnp.zeros((SUBS, LANES), F32)
        ends, starts = lax.fori_loop(
            0, steps, gather_step, ([zero] * modes, [zero] * modes), unroll=32
        )
        place = pl.ds(group, 1)
        seg = sub_index().astype(F32) * steps
        for n in range(modes):
            rate = spread(rate_ref[pl.ds(n, 1), lanes])
            to_start = jnp.exp(-rate * seg)
            to_end = jnp.exp(-rate * (steps * (SUBS - 1) - seg))
            state_ref[n, place, :] = jnp.sum(ends[n] * to_end, axis=0, keepdims=True)
            state_ref[modes + n, place, :] = jnp.sum(
                starts[n] * to_start, axis=0, keepdims=True
            )

    each_group(groups, one_group)


def chain_kernel(row_count, half, first_ref, arrived_ref, rate_ref, residue_ref, out_ref):
    blocks = arrived_ref.shape[0]
    step_decay = jnp.exp(-rate_ref[...] * row_count)
    weight = residue_ref[...] * jnp.exp(-rate_ref[...])

    def run(order):
        def body(index, carry):
            block = order(index)
            out_ref[pl.ds(block, 1)] = (carry * weight)[None]
            return carry * step_decay + arrived_ref[pl.ds(block, 1)][0]

        lax.fori_loop(0, blocks, body, jnp.zeros(rate_ref.shape, F32), unroll=32)

    @pl.when(first_ref[0] < half)
    def _():
        run(lambda index: index)

    @pl.when(first_ref[0] >= half)
    def _():
        run(lambda index: blocks - 1 - index)


def local_kernel(
    gated, gradm, residue_ref, rate_ref,
    ahead, behind, seg_out,
    seg_states, sems,
):
    groups, row_count, _ = gated.shape
    modes = rate_ref.shape[0]
    steps = row_count // SUBS
    leaving = slabs(sems, [(seg_states, seg_out)])

    def one_group(group):
        lanes = pl.ds(pl.multiple_of(group * LANES, LANES), LANES)
        weight = [spread(residue_ref[pl.ds(n, 1), lanes]) for n in range(modes)]
        rates = [rate_ref[pl.ds(n, 1), lanes] for n in range(modes)]
        decay = [spread(jnp.exp(-r)) for r in rates]
        zero = jnp.zeros((SUBS, LANES), F32)
        for source, target, backward in ((gated, ahead, False), (gradm, behind, True)):

            def scan_chunk(index, states):
                base = (steps // CHUNK - 1 - index if backward else index) * CHUNK
                values = [source[group, step_rows(base + at), :] for at in range(CHUNK)]
                made = [None] * CHUNK
                for at in range(CHUNK)[:: -1 if backward else 1]:
                    states = [s * d + values[at] for s, d in zip(states, decay)]
                    made[at] = tapped(weight, states)
                for at in range(CHUNK):
                    target[group, step_rows(base + at), :] = made[at]
                return states

            states = lax.fori_loop(0, steps // CHUNK, scan_chunk, [zero] * modes)
            sub = sub_index()
            for n in range(modes):
                span = spread(jnp.exp(-rates[n] * steps))
                total = states[n]
                for shift in (1, 2, 4):
                    if backward:
                        moved = jnp.where(
                            sub < SUBS - shift, pltpu.roll(total, SUBS - shift, 0), 0.0
                        )
                    else:
                        moved = jnp.where(sub >= shift, pltpu.roll(total, shift, 0), 0.0)
                    total = total + span * moved
                    span = span * span
                if backward:
                    enters = jnp.where(sub < SUBS - 1, pltpu.roll(total, SUBS - 1, 0), 0.0)
                else:
                    enters = jnp.where(sub >= 1, pltpu.roll(total, 1, 0), 0.0)
                seg_states[group, int(backward), n] = enters * weight[n] * decay[n]
        start_all(leaving(group))

    each_group(groups, one_group)
    each_group(groups, lambda group: wait_all(leaving(group)))


def grad_kernel(
    share, held_ref, kv_ref, seg_ref, ahead, behind, cot, enter_ref, rate_ref,
    query_mix, key_mix, value_mix, head_ref, short_ref,
    held, kv, seg_states, short, sems,
):
    groups, row_count, _ = cot.shape
    arriving = slabs(
        sems, [(seg_ref, seg_states), (held_ref, held), (kv_ref, kv)]
    )
    each_group(groups, lambda group: start_all(arriving(group)))
    modes = rate_ref.shape[0]
    steps = row_count // SUBS
    lead = held.shape[2] // SUBS - steps
    taps = lead + 1
    mix = (query_mix, key_mix, value_mix)
    short_ref[...] = jnp.zeros(short_ref.shape, F32)
    head_ref[...] = jnp.zeros(head_ref.shape, BF16)

    def one_group(group):
        lanes = pl.ds(pl.multiple_of(group * LANES, LANES), LANES)
        place = pl.ds(group, 1)
        rates = [spread(rate_ref[pl.ds(n, 1), lanes]) for n in range(modes)]
        decay = [jnp.exp(-r) for r in rates]
        seg = sub_index().astype(F32) * steps
        wait_all(arriving(group))
        for backward in (False, True):
            gap = steps * (SUBS - 1) - seg if backward else seg
            carried = []
            for n in range(modes):
                outer = spread(enter_ref[int(backward) * modes + n, place, :])
                inner = seg_states[group, int(backward), n]
                carried.append(inner + jnp.exp(-rates[n] * gap) * outer)
            parts = (1, 2) if backward else (0,)
            def grad_chunk(index, carry):
                carried, sums = carry
                base = (steps // CHUNK - 1 - index if backward else index) * CHUNK
                source = behind if backward else ahead
                long_rows = [None] * CHUNK
                for at in range(CHUNK)[:: -1 if backward else 1]:
                    long_rows[at] = source[group, step_rows(base + at), :] + added(carried)
                    carried = [c * d for c, d in zip(carried, decay)]
                new_sums = []
                for part, old in zip(parts, sums):
                    grads = []
                    for at in range(CHUNK):
                        rows = step_rows(base + at)
                        factor = cot[group, rows, :] if part == 0 else kv[group, 2 - part, rows, :]
                        grads.append(kept(long_rows[at] * factor))
                        mix[part][group, rows, :] = grads[at]
                    window = [
                        held[group, part, step_rows(base + at), :] for at in range(CHUNK + lead)
                    ]
                    new_sums.append(
                        [
                            old[k] + tapped(grads, window[lead - k : lead - k + CHUNK])
                            for k in range(taps)
                        ]
                    )
                return carried, new_sums

            zero = jnp.zeros((SUBS, LANES), F32)
            _, sums = lax.fori_loop(
                0, steps // CHUNK, grad_chunk, (carried, [[zero] * taps for _ in parts])
            )
            for part, taken in zip(parts, sums):
                for k in range(taps):
                    short[part * taps + k, place, :] = jnp.sum(taken[k], axis=0, keepdims=True)
                first = [mix[part][group, pl.ds(step * SUBS, 1), :] for step in range(lead)]
                first += [jnp.zeros((1, LANES), F32)] * (HALO - lead)
                head_ref[part, :, lanes] = jnp.concatenate(first, axis=0).astype(BF16)

    each_group(groups, one_group)
    for piece in range(short_ref.shape[0]):
        for slot in range(share):
            row, group = divmod(piece * share + slot, groups)
            if row < 3 * taps:
                short_ref[piece, slot : slot + 1, :] = short[row, group : group + 1, :]


def back_kernel(
    query_mix, key_mix, value_mix, next_ref, filt_in, out_ref,
    late, made, wide, filt_ref, sems, filt_sem,
):
    filt_copy = pltpu.make_async_copy(filt_in, filt_ref, filt_sem.at[0])
    filt_copy.start()
    mix = (query_mix, key_mix, value_mix)
    taps = filt_ref.shape[1]
    row_count, channels = made.shape
    groups = channels // LANES
    steps = row_count // SUBS
    perm = step_major(row_count, True)
    late[...] = next_ref[...].astype(F32)
    filt_copy.wait()
    copies = []
    for part in range(3):

        def one_group(group):
            lanes = pl.ds(pl.multiple_of(group * LANES, LANES), LANES)
            weights = [spread(filt_ref[part, pl.ds(k, 1), lanes]) for k in range(taps)]

            def back_rows(base, window):
                rows = [tapped(weights, window[at : at + taps]) for at in range(CHUNK)]
                made[step_rows(base, CHUNK), lanes] = jnp.concatenate(rows, axis=0).astype(BF16)

            def back_chunk(index, carry):
                base = index * CHUNK
                back_rows(
                    base,
                    [mix[part][group, step_rows(base + at), :] for at in range(CHUNK + taps - 1)],
                )
                return carry

            last = steps - CHUNK
            lax.fori_loop(0, last // CHUNK, back_chunk, 0)
            window = [mix[part][group, step_rows(last + at), :] for at in range(CHUNK)]
            for step in range(taps - 1):
                first = mix[part][group, step_rows(step), :]
                row = late[part, pl.ds(step, 1), lanes]
                window.append(
                    jnp.where(sub_index() == SUBS - 1, spread(row), pltpu.roll(first, SUBS - 1, 0))
                )
            back_rows(last, window)

        each_group(groups, one_group)
        wide[part] = jnp.dot(perm, made[...], preferred_element_type=F32).astype(BF16)
        copies.append(pltpu.make_async_copy(wide.at[part], out_ref.at[part], sems.at[part]))
        copies[-1].start()
    wait_all(copies)


def line_kernel(share, columns, part_ref, out_ref):
    lines = part_ref.shape[0] // columns
    totals = [
        added([part_ref[line * columns + column, :share, :] for line in range(lines)])
        for column in range(columns)
    ]
    totals = jnp.concatenate(totals, axis=0).astype(BF16)
    for plane in range(out_ref.shape[0]):
        out_ref[plane] = totals


def plane_kernel(share, part_ref, out_ref):
    planes, rows, _ = part_ref.shape
    piece_rows = out_ref.shape[1]
    totals = added([part_ref[plane].astype(F32) for plane in range(planes)])
    squares = jnp.sum(totals * totals)
    marks = jnp.full((piece_rows - share, LANES), squares, F32)
    columns = rows // share
    for column in range(columns):
        own = totals[column * share : (column + 1) * share]
        piece = jnp.concatenate([own, marks], axis=0)
        for line in range(out_ref.shape[0] // columns):
            out_ref[line * columns + column] = piece


def scale_kernel(clip_limit, share, sums_ref, out_ref):
    squares = added([sums_ref[piece, share : share + 1, :] for piece in range(sums_ref.shape[0])])
    factor = jnp.minimum(1.0, clip_limit / (jnp.sqrt(squares) + 1e-06))
    _, taps, channels = out_ref.shape
    groups = channels // LANES
    for part in range(3):
        for k in range(taps):
            for group in range(groups):
                piece, row = divmod((part * taps + k) * groups + group, share)
                out_ref[part, k : k + 1, pl.ds(group * LANES, LANES)] = (
                    sums_ref[piece, row : row + 1, :] * factor
                )


def passed_along(shard, by):
    length = lax.axis_size("ctx")
    pairs = [(i, i + by) for i in range(length) if 0 <= i + by < length]
    return lax.ppermute(shard, "ctx", pairs)


def exchange(blocks, axis, members=None):
    return lax.all_to_all(
        blocks, axis, split_axis=0, concat_axis=0, tiled=True, axis_index_groups=members
    )


def cost(flops, bytes_accessed):
    return pl.CostEstimate(flops=flops, bytes_accessed=bytes_accessed, transcendentals=0)


def per_device(inputs, cotangent, short_filter, residue, decay_rate):
    _, row_count, channels = inputs.shape
    taps = short_filter.shape[1]
    modes = residue.shape[0]
    blocks = lax.axis_size("ctx")
    groups = channels // LANES
    lead = taps - 1
    long_rows = row_count + lead * SUBS

    def shaped(dtype, *dims):
        return jax.ShapeDtypeStruct(dims, dtype)

    def near(dtype, *dims):
        return pltpu.VMEM(dims, dtype)

    def far(dtype, *dims):
        return pltpu.HBM(dims, dtype)

    def from_near(*values):
        return [pltpu.with_memory_space_constraint(v, pltpu.VMEM) for v in values]

    def from_far(*values):
        return [pltpu.with_memory_space_constraint(v, pltpu.HBM) for v in values]

    small = pltpu.CompilerParams(vmem_limit_bytes=4 << 20)
    params = pltpu.CompilerParams(vmem_limit_bytes=24 << 20)
    at_vmem = pl.BlockSpec(memory_space=pltpu.VMEM)
    at_hbm = pl.BlockSpec(memory_space=pltpu.HBM)
    sems = pltpu.SemaphoreType.DMA
    work = row_count * channels
    held_dims = (groups, 3, long_rows, LANES)
    part_dims = (groups, 3, row_count, LANES)
    row_dims = (groups, row_count, LANES)
    kv_dims = (groups, 2, row_count, LANES)
    seg_dims = (groups, 2, modes, SUBS, LANES)

    held, cot_held, filt, rate, weight = pl.pallas_call(
        load_kernel,
        in_specs=[at_hbm] * 5,
        out_specs=[at_vmem] * 5,
        out_shape=[
            near(F32, *part_dims),
            near(F32, *row_dims),
            near(F32, 3, taps, channels),
            near(F32, modes, channels),
            near(F32, modes, channels),
        ],
        scratch_shapes=[pltpu.VMEM((4, row_count, channels), BF16), sems((4,)), sems((3,))],
        compiler_params=params,
        cost_estimate=cost(work * 2000, work * 8),
        name="load",
    )(*from_far(inputs, cotangent, short_filter, decay_rate, residue))
    prev = passed_along(inputs[:, row_count - HALO :, :], 1)
    prev, held, cot_held = lax.optimization_barrier((prev, held, cot_held))
    gated, gradm, states = pl.pallas_call(
        mix_kernel,
        in_specs=[at_vmem] * 5,
        out_specs=[at_vmem] * 3,
        out_shape=[
            near(F32, *row_dims),
            near(F32, *row_dims),
            far(F32, 2 * modes, groups, LANES),
        ],
        scratch_shapes=[pltpu.VMEM((3, HALO, channels), F32)],
        compiler_params=params,
        cost_estimate=cost(work * 110, work * 24),
        name="mix",
    )(*from_near(held), prev, *from_near(cot_held, filt, rate))

    state_rows = 2 * modes * groups // blocks
    first = lax.axis_index("ctx") * state_rows
    half = modes * groups
    arrived = exchange(states.reshape(blocks, state_rows, LANES), "ctx")
    held, kv = pl.pallas_call(
        stage_kernel,
        in_specs=[at_hbm] * 2 + [at_vmem],
        out_specs=[at_hbm] * 2,
        out_shape=[far(F32, *held_dims), far(F32, *kv_dims)],
        scratch_shapes=[
            pltpu.VMEM(held_dims, F32),
            pltpu.VMEM(kv_dims, F32),
            pltpu.VMEM((3, taps, channels), F32),
            pltpu.VMEM((3, HALO, channels), F32),
            pltpu.VMEM((3, row_count, channels), BF16),
            sems((3,)),
            sems((1,)),
            sems((2, groups)),
        ],
        compiler_params=params,
        cost_estimate=cost(work * 2000, work * 18),
        name="stage",
    )(*from_far(inputs, short_filter), prev)
    arrived, held, kv = lax.optimization_barrier((arrived, held, kv))

    def own_rows(values):
        rows = jnp.tile(values.reshape(half, LANES), (2, 1))
        return lax.dynamic_slice_in_dim(rows, first, state_rows, 0)

    entering = pl.pallas_call(
        functools.partial(chain_kernel, row_count, half),
        in_specs=[
            pl.BlockSpec(memory_space=pltpu.SMEM),
            at_vmem,
            at_vmem,
            at_vmem,
        ],
        out_specs=at_vmem,
        out_shape=shaped(F32, blocks, state_rows, LANES),
        compiler_params=small,
        cost_estimate=cost(blocks * state_rows * LANES * 2, blocks * state_rows * LANES * 8),
        name="chain",
    )(first[None], arrived, own_rows(decay_rate), own_rows(residue))
    entering = exchange(entering, "ctx").reshape(2 * modes, groups, LANES)

    ahead, behind, seg_states = pl.pallas_call(
        local_kernel,
        in_specs=[at_vmem] * 4,
        out_specs=[at_vmem] * 2 + [at_hbm],
        out_shape=[near(F32, *row_dims), near(F32, *row_dims), far(F32, *seg_dims)],
        scratch_shapes=[pltpu.VMEM(seg_dims, F32), sems((1, groups))],
        input_output_aliases={0: 0, 1: 1},
        compiler_params=params,
        cost_estimate=cost(work * 128, work * 18),
        name="local",
    )(*from_near(gated, gradm, weight, rate))
    entering, seg_states = lax.optimization_barrier((entering, seg_states))

    tp_count = lax.axis_size("tp")
    planes = blocks // LINES
    in_plane = LINES * tp_count
    share = -(-3 * taps * groups // in_plane)
    piece_rows = -(-(share + 1) // SUBS) * SUBS
    plane_members = [
        [(y * planes + z) * tp_count + m for y in range(LINES) for m in range(tp_count)]
        for z in range(planes)
    ]
    line_members = [[y * planes + z for z in range(planes)] for y in range(LINES)]
    *grad_mix, head, short_part = pl.pallas_call(
        functools.partial(grad_kernel, share),
        in_specs=[at_hbm] * 3 + [at_vmem] * 5,
        out_specs=[at_vmem] * 5,
        out_shape=[
            near(F32, *row_dims),
            near(F32, *row_dims),
            near(F32, *row_dims),
            shaped(BF16, 3, HALO, channels),
            far(F32, in_plane, piece_rows, LANES),
        ],
        scratch_shapes=[
            pltpu.VMEM(held_dims, F32),
            pltpu.VMEM(kv_dims, F32),
            pltpu.VMEM(seg_dims, F32),
            pltpu.VMEM((3 * taps, groups, LANES), F32),
            sems((3, groups)),
        ],
        input_output_aliases={3: 0, 4: 1, 5: 2},
        compiler_params=params,
        cost_estimate=cost(work * 110, work * 30),
        name="grad",
    )(
        *from_far(held, kv, seg_states), *from_near(ahead, behind, cot_held), entering, rate
    )

    gathered = exchange(short_part, ("ctx", "tp"), plane_members)
    late = passed_along(head, -1)
    own_sum = pl.pallas_call(
        functools.partial(line_kernel, share, tp_count),
        in_specs=[at_vmem],
        out_specs=at_vmem,
        out_shape=shaped(BF16, planes, tp_count * share, LANES),
        compiler_params=small,
        name="line",
    )(gathered)
    own_sum, late = lax.optimization_barrier((own_sum, late))
    all_sums = exchange(own_sum, "ctx", line_members)
    grad_inputs = pl.pallas_call(
        back_kernel,
        in_specs=[at_vmem] * 4 + [at_hbm],
        out_specs=at_hbm,
        out_shape=far(BF16, 3, row_count, channels),
        scratch_shapes=[
            pltpu.VMEM((3, HALO, channels), F32),
            pltpu.VMEM((row_count, channels), BF16),
            pltpu.VMEM((3, row_count, channels), BF16),
            pltpu.VMEM((3, taps, channels), F32),
            sems((3,)),
            sems((1,)),
        ],
        compiler_params=params,
        cost_estimate=cost(work * 48, work * 12),
        name="back",
    )(*from_near(*grad_mix), late, *from_far(short_filter))
    all_sums, grad_inputs = lax.optimization_barrier((all_sums, grad_inputs))
    all_sums = pl.pallas_call(
        functools.partial(plane_kernel, share),
        in_specs=[at_vmem],
        out_specs=at_vmem,
        out_shape=shaped(F32, in_plane, piece_rows, LANES),
        compiler_params=small,
        name="plane",
    )(all_sums)
    all_sums = exchange(all_sums, ("ctx", "tp"), plane_members)
    clip_limit = math.sqrt(3 * channels * tp_count * taps)
    grad_short = pl.pallas_call(
        functools.partial(scale_kernel, clip_limit, share),
        in_specs=[at_vmem],
        out_specs=at_vmem,
        out_shape=shaped(F32, 3, taps, channels),
        compiler_params=small,
        name="scale",
    )(all_sums)
    return (grad_inputs, grad_short)


def solution(mesh):
    return jax.shard_map(
        per_device,
        mesh=mesh,
        in_specs=(
            P(None, "ctx", "tp"),
            P("ctx", "tp"),
            P(None, None, "tp"),
            P(None, "tp"),
            P(None, "tp"),
        ),
        out_specs=(P(None, "ctx", "tp"), P(None, None, "tp")),
        check_vma=False,
    )
```

```python
import functools
import math

import jax
import jax.numpy as jnp
from jax import lax
from jax.experimental import pallas as pl
from jax.experimental.pallas import tpu as pltpu
from jax.sharding import PartitionSpec as P

LANES = 128
SUBS = 8
HALO = 8
CHUNK = 16
LINES = 4
F32 = jnp.float32
BF16 = jnp.bfloat16


def sub_index():
    return lax.broadcasted_iota(jnp.int32, (SUBS, LANES), 0)


def step_major(row_count, inverse):
    kept = lax.broadcasted_iota(jnp.int32, (row_count, row_count), 1 if inverse else 0)
    time = lax.broadcasted_iota(jnp.int32, (row_count, row_count), 0 if inverse else 1)
    source = (kept & (SUBS - 1)) * (row_count // SUBS) + (kept >> 3)
    return jnp.where(source == time, 1.0, 0.0).astype(BF16)


def spread(row):
    return jnp.broadcast_to(row, (SUBS, LANES))


def step_rows(first, count=1):
    return pl.ds(pl.multiple_of(first * SUBS, SUBS), count * SUBS)


def kept(value):
    return value.astype(BF16).astype(F32)


def added(terms):
    while len(terms) > 1:
        odd = terms[-1:] if len(terms) % 2 else []
        terms = [a + b for a, b in zip(terms[::2], terms[1::2])] + odd
    return terms[0]


def tapped(weights, rows):
    return added([w * r for w, r in zip(weights, rows)])


def each_group(groups, body):
    first, last = groups if isinstance(groups, tuple) else (0, groups)

    def step(group, carry):
        body(group)
        return carry

    lax.fori_loop(first, last, step, 0)


def slabs(sems, pairs):
    def of(group):
        return [
            pltpu.make_async_copy(source.at[group], target.at[group], sems.at[index, group])
            for index, (source, target) in enumerate(pairs)
        ]

    return of


def start_all(copies):
    for copy in copies:
        copy.start()


def wait_all(copies):
    for copy in copies:
        copy.wait()


def earlier_rows(held, first_row, early, group, part, lanes, lead):
    steps = (held.shape[2] - first_row) // SUBS
    made = []
    for step in range(lead):
        late = held[group, part, pl.ds(first_row + (steps - lead + step) * SUBS, SUBS), :]
        first = early[part, pl.ds(HALO - lead + step, 1), lanes]
        made.append(jnp.where(sub_index() == 0, spread(first), pltpu.roll(late, 1, 0)))
    return made


def short_weights(filt_ref, lanes):
    return [
        [spread(filt_ref[part, pl.ds(k, 1), lanes]) for k in range(filt_ref.shape[1])]
        for part in range(3)
    ]


def short_chunk(weights, window):
    taps = len(weights)
    return [tapped(weights, window[at : at + taps][::-1]) for at in range(CHUNK)]


def load_rows(sources, targets, wide, sems):
    row_count, channels = sources[0].shape
    copies = [
        pltpu.make_async_copy(source, wide.at[part], sems.at[part])
        for part, source in enumerate(sources)
    ]
    start_all(copies)
    perm = step_major(row_count, False)
    for part, copy in enumerate(copies):
        copy.wait()
        rows = jnp.dot(perm, wide[part], preferred_element_type=F32)
        for group in range(channels // LANES):
            slab = rows[:, group * LANES : (group + 1) * LANES]
            targets[part](group)[...] = slab


def load_kernel(
    x_ref, cot_ref, filt_ref, rate_ref, residue_ref,
    held_ref, cot_held_ref, filt_out, rate_out, residue_out,
    wide, sems, small_sems,
):
    sources = [filt_ref, rate_ref, residue_ref]
    targets = [filt_out, rate_out, residue_out]
    copies = [
        pltpu.make_async_copy(source, target, small_sems.at[index])
        for index, (source, target) in enumerate(zip(sources, targets))
    ]
    start_all(copies)
    load_rows(
        [x_ref.at[part] for part in range(3)] + [cot_ref],
        [lambda group, part=part: held_ref.at[group, part] for part in range(3)]
        + [lambda group: cot_held_ref.at[group]],
        wide,
        sems,
    )
    wait_all(copies)


def stage_kernel(
    x_ref, filt_in, prev_ref, held_out, kv_out,
    held, kv, filt_ref, early, wide, sems, filt_sem, out_sems,
):
    filt_copy = pltpu.make_async_copy(filt_in, filt_ref, filt_sem.at[0])
    filt_copy.start()
    groups, _, row_count, _ = kv_out.shape
    lead = filt_ref.shape[1] - 1
    below = pl.ds(lead * SUBS, row_count)
    load_rows(
        [x_ref.at[part] for part in range(3)],
        [lambda group, part=part: held.at[group, part, below, :] for part in range(3)],
        wide,
        sems,
    )
    early[...] = prev_ref[...].astype(F32)
    leaving = slabs(out_sems, [(held, held_out), (kv, kv_out)])
    filt_copy.wait()

    def one_group(group):
        lanes = pl.ds(pl.multiple_of(group * LANES, LANES), LANES)
        for part in range(3):
            rows = earlier_rows(held, lead * SUBS, early, group, part, lanes, lead)
            for step in range(lead):
                held[group, part, step_rows(step), :] = rows[step]
        weights = short_weights(filt_ref, lanes)

        def stage_chunk(index, carry):
            base = index * CHUNK
            for part in (1, 2):
                window = [held[group, part, step_rows(base + at), :] for at in range(CHUNK + lead)]
                rows = short_chunk(weights[part], window)
                for at in range(CHUNK):
                    kv[group, part - 1, step_rows(base + at), :] = rows[at]
            return carry

        lax.fori_loop(0, row_count // SUBS // CHUNK, stage_chunk, 0)
        start_all(leaving(group))

    each_group(groups, one_group)
    each_group(groups, lambda group: wait_all(leaving(group)))


def mix_kernel(
    held, prev_ref, cot_ref, filt_ref, rate_ref, gated, gradm, state_ref, early
):
    groups, row_count, _ = cot_ref.shape
    taps = filt_ref.shape[1]
    modes = rate_ref.shape[0]
    lead = taps - 1
    steps = row_count // SUBS
    early[...] = prev_ref[...].astype(F32)

    def one_group(group):
        lanes = pl.ds(pl.multiple_of(group * LANES, LANES), LANES)
        weights = short_weights(filt_ref, lanes)

        def mix_rows(base, window_of):
            key_rows = short_chunk(weights[1], window_of(1))
            value_rows = short_chunk(weights[2], window_of(2))
            for at in range(CHUNK):
                gated[group, step_rows(base + at), :] = kept(key_rows[at] * value_rows[at])
            query_rows = short_chunk(weights[0], window_of(0))
            for at in range(CHUNK):
                rows = step_rows(base + at)
                gradm[group, rows, :] = kept(cot_ref[group, rows, :] * query_rows[at])

        def inner(base, count):
            return lambda part: [
                held[group, part, step_rows(base + at), :] for at in range(count)
            ]

        def mix_chunk(index, carry):
            base = index * CHUNK
            mix_rows(base, inner(base - lead, CHUNK + lead))
            return carry

        mix_rows(
            0,
            lambda part: earlier_rows(held, 0, early, group, part, lanes, lead)
            + inner(0, CHUNK)(part),
        )
        lax.fori_loop(1, steps // CHUNK, mix_chunk, 0)
        decay = [spread(jnp.exp(-rate_ref[pl.ds(n, 1), lanes])) for n in range(modes)]

        def gather_step(step, carry):
            ends, starts = carry
            ahead = gated[group, step_rows(step), :]
            behind = gradm[group, step_rows(steps - 1 - step), :]
            return (
                [e * d + ahead for e, d in zip(ends, decay)],
                [s * d + behind for s, d in zip(starts, decay)],
            )

        zero = jnp.zeros((SUBS, LANES), F32)
        ends, starts = lax.fori_loop(
            0, steps, gather_step, ([zero] * modes, [zero] * modes), unroll=32
        )
        place = pl.ds(group, 1)
        seg = sub_index().astype(F32) * steps
        for n in range(modes):
            rate = spread(rate_ref[pl.ds(n, 1), lanes])
            to_start = jnp.exp(-rate * seg)
            to_end = jnp.exp(-rate * (steps * (SUBS - 1) - seg))
            state_ref[n, place, :] = jnp.sum(ends[n] * to_end, axis=0, keepdims=True)
            state_ref[modes + n, place, :] = jnp.sum(
                starts[n] * to_start, axis=0, keepdims=True
            )

    each_group(groups, one_group)


def chain_kernel(row_count, half, first_ref, arrived_ref, rate_ref, residue_ref, out_ref):
    blocks = arrived_ref.shape[0]
    step_decay = jnp.exp(-rate_ref[...] * row_count)
    weight = residue_ref[...] * jnp.exp(-rate_ref[...])

    def run(order):
        def body(index, carry):
            block = order(index)
            out_ref[pl.ds(block, 1)] = (carry * weight)[None]
            return carry * step_decay + arrived_ref[pl.ds(block, 1)][0]

        lax.fori_loop(0, blocks, body, jnp.zeros(rate_ref.shape, F32), unroll=32)

    @pl.when(first_ref[0] < half)
    def _():
        run(lambda index: index)

    @pl.when(first_ref[0] >= half)
    def _():
        run(lambda index: blocks - 1 - index)


def local_kernel(groups, given, gated, gradm, residue_ref, rate_ref, *refs):
    ahead, behind, seg_out, seg_states, sems = refs[given:]
    _, row_count, _ = gated.shape
    modes = rate_ref.shape[0]
    steps = row_count // SUBS
    leaving = slabs(sems, [(seg_states, seg_out)])

    def one_group(group):
        lanes = pl.ds(pl.multiple_of(group * LANES, LANES), LANES)
        weight = [spread(residue_ref[pl.ds(n, 1), lanes]) for n in range(modes)]
        rates = [rate_ref[pl.ds(n, 1), lanes] for n in range(modes)]
        decay = [spread(jnp.exp(-r)) for r in rates]
        zero = jnp.zeros((SUBS, LANES), F32)
        for source, target, backward in ((gated, ahead, False), (gradm, behind, True)):

            def scan_chunk(index, states):
                base = (steps // CHUNK - 1 - index if backward else index) * CHUNK
                values = [source[group, step_rows(base + at), :] for at in range(CHUNK)]
                made = [None] * CHUNK
                for at in range(CHUNK)[:: -1 if backward else 1]:
                    states = [s * d + values[at] for s, d in zip(states, decay)]
                    made[at] = tapped(weight, states)
                for at in range(CHUNK):
                    target[group, step_rows(base + at), :] = made[at]
                return states

            states = lax.fori_loop(0, steps // CHUNK, scan_chunk, [zero] * modes)
            sub = sub_index()
            for n in range(modes):
                span = spread(jnp.exp(-rates[n] * steps))
                total = states[n]
                for shift in (1, 2, 4):
                    if backward:
                        moved = jnp.where(
                            sub < SUBS - shift, pltpu.roll(total, SUBS - shift, 0), 0.0
                        )
                    else:
                        moved = jnp.where(sub >= shift, pltpu.roll(total, shift, 0), 0.0)
                    total = total + span * moved
                    span = span * span
                if backward:
                    enters = jnp.where(sub < SUBS - 1, pltpu.roll(total, SUBS - 1, 0), 0.0)
                else:
                    enters = jnp.where(sub >= 1, pltpu.roll(total, 1, 0), 0.0)
                seg_states[group, int(backward), n] = enters * weight[n] * decay[n]
        start_all(leaving(group))

    each_group(groups, one_group)
    each_group(groups, lambda group: wait_all(leaving(group)))


def grad_kernel(
    share, held_ref, kv_ref, seg_ref, ahead, behind, cot, enter_ref, rate_ref,
    query_mix, key_mix, value_mix, head_ref, short_ref,
    held, kv, seg_states, short, sems,
):
    groups, row_count, _ = cot.shape
    arriving = slabs(
        sems, [(seg_ref, seg_states), (held_ref, held), (kv_ref, kv)]
    )
    each_group(groups, lambda group: start_all(arriving(group)))
    modes = rate_ref.shape[0]
    steps = row_count // SUBS
    lead = held.shape[2] // SUBS - steps
    taps = lead + 1
    mix = (query_mix, key_mix, value_mix)
    short_ref[...] = jnp.zeros(short_ref.shape, F32)
    head_ref[...] = jnp.zeros(head_ref.shape, BF16)

    def one_group(group):
        lanes = pl.ds(pl.multiple_of(group * LANES, LANES), LANES)
        place = pl.ds(group, 1)
        rates = [spread(rate_ref[pl.ds(n, 1), lanes]) for n in range(modes)]
        decay = [jnp.exp(-r) for r in rates]
        seg = sub_index().astype(F32) * steps
        wait_all(arriving(group))
        for backward in (False, True):
            gap = steps * (SUBS - 1) - seg if backward else seg
            carried = []
            for n in range(modes):
                outer = spread(enter_ref[int(backward) * modes + n, place, :])
                inner = seg_states[group, int(backward), n]
                carried.append(inner + jnp.exp(-rates[n] * gap) * outer)
            parts = (1, 2) if backward else (0,)
            def grad_chunk(index, carry):
                carried, sums = carry
                base = (steps // CHUNK - 1 - index if backward else index) * CHUNK
                source = behind if backward else ahead
                long_rows = [None] * CHUNK
                for at in range(CHUNK)[:: -1 if backward else 1]:
                    long_rows[at] = source[group, step_rows(base + at), :] + added(carried)
                    carried = [c * d for c, d in zip(carried, decay)]
                new_sums = []
                for part, old in zip(parts, sums):
                    grads = []
                    for at in range(CHUNK):
                        rows = step_rows(base + at)
                        factor = cot[group, rows, :] if part == 0 else kv[group, 2 - part, rows, :]
                        grads.append(kept(long_rows[at] * factor))
                        mix[part][group, rows, :] = grads[at]
                    window = [
                        held[group, part, step_rows(base + at), :] for at in range(CHUNK + lead)
                    ]
                    new_sums.append(
                        [
                            old[k] + tapped(grads, window[lead - k : lead - k + CHUNK])
                            for k in range(taps)
                        ]
                    )
                return carried, new_sums

            zero = jnp.zeros((SUBS, LANES), F32)
            _, sums = lax.fori_loop(
                0, steps // CHUNK, grad_chunk, (carried, [[zero] * taps for _ in parts])
            )
            for part, taken in zip(parts, sums):
                for k in range(taps):
                    short[part * taps + k, place, :] = jnp.sum(taken[k], axis=0, keepdims=True)
                first = [mix[part][group, pl.ds(step * SUBS, 1), :] for step in range(lead)]
                first += [jnp.zeros((1, LANES), F32)] * (HALO - lead)
                head_ref[part, :, lanes] = jnp.concatenate(first, axis=0).astype(BF16)

    each_group(groups, one_group)
    for piece in range(short_ref.shape[0]):
        for slot in range(share):
            row, group = divmod(piece * share + slot, groups)
            if row < 3 * taps:
                short_ref[piece, slot : slot + 1, :] = short[row, group : group + 1, :]


def back_kernel(
    query_mix, key_mix, value_mix, next_ref, filt_in, out_ref,
    late, made, wide, filt_ref, sems, filt_sem,
):
    filt_copy = pltpu.make_async_copy(filt_in, filt_ref, filt_sem.at[0])
    filt_copy.start()
    mix = (query_mix, key_mix, value_mix)
    taps = filt_ref.shape[1]
    row_count, channels = made.shape
    groups = channels // LANES
    steps = row_count // SUBS
    perm = step_major(row_count, True)
    late[...] = next_ref[...].astype(F32)
    filt_copy.wait()
    copies = []
    for part in range(3):

        def one_group(group):
            lanes = pl.ds(pl.multiple_of(group * LANES, LANES), LANES)
            weights = [spread(filt_ref[part, pl.ds(k, 1), lanes]) for k in range(taps)]

            def back_rows(base, window):
                rows = [tapped(weights, window[at : at + taps]) for at in range(CHUNK)]
                made[step_rows(base, CHUNK), lanes] = jnp.concatenate(rows, axis=0).astype(BF16)

            def back_chunk(index, carry):
                base = index * CHUNK
                back_rows(
                    base,
                    [mix[part][group, step_rows(base + at), :] for at in range(CHUNK + taps - 1)],
                )
                return carry

            last = steps - CHUNK
            lax.fori_loop(0, last // CHUNK, back_chunk, 0)
            window = [mix[part][group, step_rows(last + at), :] for at in range(CHUNK)]
            for step in range(taps - 1):
                first = mix[part][group, step_rows(step), :]
                row = late[part, pl.ds(step, 1), lanes]
                window.append(
                    jnp.where(sub_index() == SUBS - 1, spread(row), pltpu.roll(first, SUBS - 1, 0))
                )
            back_rows(last, window)

        each_group(groups, one_group)
        wide[part] = jnp.dot(perm, made[...], preferred_element_type=F32).astype(BF16)
        copies.append(pltpu.make_async_copy(wide.at[part], out_ref.at[part], sems.at[part]))
        copies[-1].start()
    wait_all(copies)


def line_kernel(share, columns, part_ref, out_ref):
    lines = part_ref.shape[0] // columns
    totals = [
        added([part_ref[line * columns + column, :share, :] for line in range(lines)])
        for column in range(columns)
    ]
    totals = jnp.concatenate(totals, axis=0).astype(BF16)
    for plane in range(out_ref.shape[0]):
        out_ref[plane] = totals


def plane_kernel(share, part_ref, out_ref):
    planes, rows, _ = part_ref.shape
    piece_rows = out_ref.shape[1]
    totals = added([part_ref[plane].astype(F32) for plane in range(planes)])
    squares = jnp.sum(totals * totals)
    marks = jnp.full((piece_rows - share, LANES), squares, F32)
    columns = rows // share
    for column in range(columns):
        own = totals[column * share : (column + 1) * share]
        piece = jnp.concatenate([own, marks], axis=0)
        for line in range(out_ref.shape[0] // columns):
            out_ref[line * columns + column] = piece


def scale_kernel(clip_limit, share, sums_ref, out_ref):
    squares = added([sums_ref[piece, share : share + 1, :] for piece in range(sums_ref.shape[0])])
    factor = jnp.minimum(1.0, clip_limit / (jnp.sqrt(squares) + 1e-06))
    _, taps, channels = out_ref.shape
    groups = channels // LANES
    for part in range(3):
        for k in range(taps):
            for group in range(groups):
                piece, row = divmod((part * taps + k) * groups + group, share)
                out_ref[part, k : k + 1, pl.ds(group * LANES, LANES)] = (
                    sums_ref[piece, row : row + 1, :] * factor
                )


def passed_along(shard, by):
    length = lax.axis_size("ctx")
    pairs = [(i, i + by) for i in range(length) if 0 <= i + by < length]
    return lax.ppermute(shard, "ctx", pairs)


def exchange(blocks, axis, members=None):
    return lax.all_to_all(
        blocks, axis, split_axis=0, concat_axis=0, tiled=True, axis_index_groups=members
    )


def cost(flops, bytes_accessed):
    return pl.CostEstimate(flops=flops, bytes_accessed=bytes_accessed, transcendentals=0)


def per_device(inputs, cotangent, short_filter, residue, decay_rate):
    _, row_count, channels = inputs.shape
    taps = short_filter.shape[1]
    modes = residue.shape[0]
    blocks = lax.axis_size("ctx")
    groups = channels // LANES
    lead = taps - 1
    long_rows = row_count + lead * SUBS

    def shaped(dtype, *dims):
        return jax.ShapeDtypeStruct(dims, dtype)

    def near(dtype, *dims):
        return pltpu.VMEM(dims, dtype)

    def far(dtype, *dims):
        return pltpu.HBM(dims, dtype)

    def from_near(*values):
        return [pltpu.with_memory_space_constraint(v, pltpu.VMEM) for v in values]

    def from_far(*values):
        return [pltpu.with_memory_space_constraint(v, pltpu.HBM) for v in values]

    small = pltpu.CompilerParams(vmem_limit_bytes=4 << 20)
    params = pltpu.CompilerParams(vmem_limit_bytes=24 << 20)
    at_vmem = pl.BlockSpec(memory_space=pltpu.VMEM)
    at_hbm = pl.BlockSpec(memory_space=pltpu.HBM)
    sems = pltpu.SemaphoreType.DMA
    work = row_count * channels
    held_dims = (groups, 3, long_rows, LANES)
    part_dims = (groups, 3, row_count, LANES)
    row_dims = (groups, row_count, LANES)
    kv_dims = (groups, 2, row_count, LANES)
    seg_dims = (groups, 2, modes, SUBS, LANES)

    held, cot_held, filt, rate, weight = pl.pallas_call(
        load_kernel,
        in_specs=[at_hbm] * 5,
        out_specs=[at_vmem] * 5,
        out_shape=[
            near(F32, *part_dims),
            near(F32, *row_dims),
            near(F32, 3, taps, channels),
            near(F32, modes, channels),
            near(F32, modes, channels),
        ],
        scratch_shapes=[pltpu.VMEM((4, row_count, channels), BF16), sems((4,)), sems((3,))],
        compiler_params=params,
        cost_estimate=cost(work * 2000, work * 8),
        name="load",
    )(*from_far(inputs, cotangent, short_filter, decay_rate, residue))
    prev = passed_along(inputs[:, row_count - HALO :, :], 1)
    state_rows = 2 * modes * groups // blocks
    first = lax.axis_index("ctx") * state_rows
    half = modes * groups

    def own_rows(values):
        start = lax.rem(first, half)
        if state_rows < groups:
            corner, taken = (start // groups, start % groups * LANES), (1, state_rows * LANES)
        else:
            corner, taken = (start // groups, 0), (state_rows // groups, channels)
        return lax.dynamic_slice(values, corner, taken).reshape(state_rows, LANES)

    prev, held, cot_held, own_rate, own_residue = lax.optimization_barrier(
        (prev, held, cot_held, own_rows(decay_rate), own_rows(residue))
    )
    gated, gradm, states = pl.pallas_call(
        mix_kernel,
        in_specs=[at_vmem] * 5,
        out_specs=[at_vmem] * 3,
        out_shape=[
            near(F32, *row_dims),
            near(F32, *row_dims),
            far(F32, 2 * modes, groups, LANES),
        ],
        scratch_shapes=[pltpu.VMEM((3, HALO, channels), F32)],
        compiler_params=params,
        cost_estimate=cost(work * 110, work * 24),
        name="mix",
    )(*from_near(held), prev, *from_near(cot_held, filt, rate))

    arrived = exchange(states.reshape(blocks, state_rows, LANES), "ctx")
    held, kv = pl.pallas_call(
        stage_kernel,
        in_specs=[at_hbm] * 2 + [at_vmem],
        out_specs=[at_hbm] * 2,
        out_shape=[far(F32, *held_dims), far(F32, *kv_dims)],
        scratch_shapes=[
            pltpu.VMEM(held_dims, F32),
            pltpu.VMEM(kv_dims, F32),
            pltpu.VMEM((3, taps, channels), F32),
            pltpu.VMEM((3, HALO, channels), F32),
            pltpu.VMEM((3, row_count, channels), BF16),
            sems((3,)),
            sems((1,)),
            sems((2, groups)),
        ],
        compiler_params=params,
        cost_estimate=cost(work * 2000, work * 18),
        name="stage",
    )(*from_far(inputs, short_filter), prev)
    def local_sums(span, gated, gradm, seg_states=None):
        seg = [] if seg_states is None else from_far(seg_states)
        return pl.pallas_call(
            functools.partial(local_kernel, span, len(seg)),
            in_specs=[at_vmem] * 4 + [at_hbm] * len(seg),
            out_specs=[at_vmem] * 2 + [at_hbm],
            out_shape=[near(F32, *row_dims), near(F32, *row_dims), far(F32, *seg_dims)],
            scratch_shapes=[pltpu.VMEM(seg_dims, F32), sems((1, groups))],
            input_output_aliases={0: 0, 1: 1, **({4: 2} if seg else {})},
            compiler_params=params,
            cost_estimate=cost(work * 16 * (span[1] - span[0]), work * 18),
            name="local",
        )(*from_near(gated, gradm, weight, rate), *seg)

    early_groups = groups // 8
    if early_groups:
        ahead, behind, seg_states = local_sums((0, early_groups), gated, gradm)
        arrived, held, kv, seg_states = lax.optimization_barrier((arrived, held, kv, seg_states))
    else:
        ahead, behind, seg_states = gated, gradm, None
        arrived, held, kv = lax.optimization_barrier((arrived, held, kv))

    entering = pl.pallas_call(
        functools.partial(chain_kernel, row_count, half),
        in_specs=[
            pl.BlockSpec(memory_space=pltpu.SMEM),
            at_vmem,
            at_vmem,
            at_vmem,
        ],
        out_specs=at_vmem,
        out_shape=shaped(F32, blocks, state_rows, LANES),
        compiler_params=small,
        cost_estimate=cost(blocks * state_rows * LANES * 2, blocks * state_rows * LANES * 8),
        name="chain",
    )(first[None], arrived, own_rate, own_residue)
    entering = exchange(entering, "ctx").reshape(2 * modes, groups, LANES)

    ahead, behind, seg_states = local_sums((early_groups, groups), ahead, behind, seg_states)
    entering, seg_states = lax.optimization_barrier((entering, seg_states))

    tp_count = lax.axis_size("tp")
    planes = blocks // LINES
    in_plane = LINES * tp_count
    share = -(-3 * taps * groups // in_plane)
    piece_rows = -(-(share + 1) // SUBS) * SUBS
    plane_members = [
        [(y * planes + z) * tp_count + m for y in range(LINES) for m in range(tp_count)]
        for z in range(planes)
    ]
    line_members = [[y * planes + z for z in range(planes)] for y in range(LINES)]
    *grad_mix, head, short_part = pl.pallas_call(
        functools.partial(grad_kernel, share),
        in_specs=[at_hbm] * 3 + [at_vmem] * 5,
        out_specs=[at_vmem] * 5,
        out_shape=[
            near(F32, *row_dims),
            near(F32, *row_dims),
            near(F32, *row_dims),
            shaped(BF16, 3, HALO, channels),
            far(F32, in_plane, piece_rows, LANES),
        ],
        scratch_shapes=[
            pltpu.VMEM(held_dims, F32),
            pltpu.VMEM(kv_dims, F32),
            pltpu.VMEM(seg_dims, F32),
            pltpu.VMEM((3 * taps, groups, LANES), F32),
            sems((3, groups)),
        ],
        input_output_aliases={3: 0, 4: 1, 5: 2},
        compiler_params=params,
        cost_estimate=cost(work * 110, work * 30),
        name="grad",
    )(
        *from_far(held, kv, seg_states), *from_near(ahead, behind, cot_held), entering, rate
    )

    gathered = exchange(short_part, ("ctx", "tp"), plane_members)
    late = passed_along(head, -1)
    own_sum = pl.pallas_call(
        functools.partial(line_kernel, share, tp_count),
        in_specs=[at_vmem],
        out_specs=at_vmem,
        out_shape=shaped(BF16, planes, tp_count * share, LANES),
        compiler_params=small,
        name="line",
    )(gathered)
    own_sum, late = lax.optimization_barrier((own_sum, late))
    all_sums = exchange(own_sum, "ctx", line_members)
    grad_inputs = pl.pallas_call(
        back_kernel,
        in_specs=[at_vmem] * 4 + [at_hbm],
        out_specs=at_hbm,
        out_shape=far(BF16, 3, row_count, channels),
        scratch_shapes=[
            pltpu.VMEM((3, HALO, channels), F32),
            pltpu.VMEM((row_count, channels), BF16),
            pltpu.VMEM((3, row_count, channels), BF16),
            pltpu.VMEM((3, taps, channels), F32),
            sems((3,)),
            sems((1,)),
        ],
        compiler_params=params,
        cost_estimate=cost(work * 48, work * 12),
        name="back",
    )(*from_near(*grad_mix), late, *from_far(short_filter))
    all_sums, grad_inputs = lax.optimization_barrier((all_sums, grad_inputs))
    all_sums = pl.pallas_call(
        functools.partial(plane_kernel, share),
        in_specs=[at_vmem],
        out_specs=at_vmem,
        out_shape=shaped(F32, in_plane, piece_rows, LANES),
        compiler_params=small,
        name="plane",
    )(all_sums)
    all_sums = exchange(all_sums, ("ctx", "tp"), plane_members)
    clip_limit = math.sqrt(3 * channels * tp_count * taps)
    grad_short = pl.pallas_call(
        functools.partial(scale_kernel, clip_limit, share),
        in_specs=[at_vmem],
        out_specs=at_vmem,
        out_shape=shaped(F32, 3, taps, channels),
        compiler_params=small,
        name="scale",
    )(all_sums)
    return (grad_inputs, grad_short)


def solution(mesh):
    return jax.shard_map(
        per_device,
        mesh=mesh,
        in_specs=(
            P(None, "ctx", "tp"),
            P("ctx", "tp"),
            P(None, None, "tp"),
            P(None, "tp"),
            P(None, "tp"),
        ),
        out_specs=(P(None, "ctx", "tp"), P(None, None, "tp")),
        check_vma=False,
    )
```

```python
import functools
import math

import jax
import jax.numpy as jnp
from jax import lax
from jax.experimental import pallas as pl
from jax.experimental.pallas import tpu as pltpu
from jax.sharding import PartitionSpec as P

LANES = 128
SUBS = 8
HALO = 8
CHUNK = 16
LINES = 4
F32 = jnp.float32
BF16 = jnp.bfloat16


def sub_index():
    return lax.broadcasted_iota(jnp.int32, (SUBS, LANES), 0)


def step_major(row_count, inverse):
    kept = lax.broadcasted_iota(jnp.int32, (row_count, row_count), 1 if inverse else 0)
    time = lax.broadcasted_iota(jnp.int32, (row_count, row_count), 0 if inverse else 1)
    source = (kept & (SUBS - 1)) * (row_count // SUBS) + (kept >> 3)
    return jnp.where(source == time, 1.0, 0.0).astype(BF16)


def spread(row):
    return jnp.broadcast_to(row, (SUBS, LANES))


def step_rows(first, count=1):
    return pl.ds(pl.multiple_of(first * SUBS, SUBS), count * SUBS)


def kept(value):
    return value.astype(BF16).astype(F32)


def added(terms):
    while len(terms) > 1:
        odd = terms[-1:] if len(terms) % 2 else []
        terms = [a + b for a, b in zip(terms[::2], terms[1::2])] + odd
    return terms[0]


def tapped(weights, rows):
    return added([w * r for w, r in zip(weights, rows)])


def each_group(groups, body):
    first, last = groups if isinstance(groups, tuple) else (0, groups)

    def step(group, carry):
        body(group)
        return carry

    lax.fori_loop(first, last, step, 0)


def slabs(sems, pairs):
    def of(group):
        return [
            pltpu.make_async_copy(source.at[group], target.at[group], sems.at[index, group])
            for index, (source, target) in enumerate(pairs)
        ]

    return of


def start_all(copies):
    for copy in copies:
        copy.start()


def wait_all(copies):
    for copy in copies:
        copy.wait()


def earlier_rows(held, first_row, early, group, part, lanes, lead):
    steps = (held.shape[2] - first_row) // SUBS
    made = []
    for step in range(lead):
        late = held[group, part, pl.ds(first_row + (steps - lead + step) * SUBS, SUBS), :]
        first = early[part, pl.ds(HALO - lead + step, 1), lanes]
        made.append(jnp.where(sub_index() == 0, spread(first), pltpu.roll(late, 1, 0)))
    return made


def short_weights(filt_ref, lanes):
    return [
        [spread(filt_ref[part, pl.ds(k, 1), lanes]) for k in range(filt_ref.shape[1])]
        for part in range(3)
    ]


def short_chunk(weights, window):
    taps = len(weights)
    return [tapped(weights, window[at : at + taps][::-1]) for at in range(CHUNK)]


def load_rows(sources, targets, wide, sems):
    row_count, channels = sources[0].shape
    copies = [
        pltpu.make_async_copy(source, wide.at[part], sems.at[part])
        for part, source in enumerate(sources)
    ]
    start_all(copies)
    perm = step_major(row_count, False)
    for part, copy in enumerate(copies):
        copy.wait()
        rows = jnp.dot(perm, wide[part], preferred_element_type=F32)
        for group in range(channels // LANES):
            slab = rows[:, group * LANES : (group + 1) * LANES]
            targets[part](group)[...] = slab


def own_rows(values, first, count):
    modes, channels = values.shape
    groups = channels // LANES
    wide = min(count, groups)
    at_mode = lax.broadcasted_iota(jnp.int32, (modes, wide * LANES), 0)
    start = lax.rem(first, modes * groups)
    mode, group = lax.div(start, groups), lax.rem(start, groups)
    lanes = pl.ds(pl.multiple_of(group * LANES, LANES), wide * LANES)
    rows = []
    for index in range(count // wide):
        picked = jnp.where(at_mode == mode + index, values[:, lanes], 0.0)
        row = jnp.sum(picked, axis=0, keepdims=True)
        rows += [row[:, at * LANES : (at + 1) * LANES] for at in range(wide)]
    return jnp.concatenate(rows, axis=0)


def load_kernel(
    x_ref, cot_ref, filt_ref, rate_ref, residue_ref,
    held_ref, cot_held_ref, filt_out, rate_out, residue_out,
    wide, sems, small_sems,
):
    sources = [filt_ref, rate_ref, residue_ref]
    targets = [filt_out, rate_out, residue_out]
    copies = [
        pltpu.make_async_copy(source, target, small_sems.at[index])
        for index, (source, target) in enumerate(zip(sources, targets))
    ]
    start_all(copies)
    load_rows(
        [x_ref.at[part] for part in range(3)] + [cot_ref],
        [lambda group, part=part: held_ref.at[group, part] for part in range(3)]
        + [lambda group: cot_held_ref.at[group]],
        wide,
        sems,
    )
    wait_all(copies)


def stage_kernel(
    x_ref, filt_in, prev_ref, held_out, kv_out,
    held, kv, filt_ref, early, wide, sems, filt_sem, out_sems,
):
    filt_copy = pltpu.make_async_copy(filt_in, filt_ref, filt_sem.at[0])
    filt_copy.start()
    groups, _, row_count, _ = kv_out.shape
    lead = filt_ref.shape[1] - 1
    below = pl.ds(lead * SUBS, row_count)
    load_rows(
        [x_ref.at[part] for part in range(3)],
        [lambda group, part=part: held.at[group, part, below, :] for part in range(3)],
        wide,
        sems,
    )
    early[...] = prev_ref[...].astype(F32)
    leaving = slabs(out_sems, [(held, held_out), (kv, kv_out)])
    filt_copy.wait()

    def one_group(group):
        lanes = pl.ds(pl.multiple_of(group * LANES, LANES), LANES)
        for part in range(3):
            rows = earlier_rows(held, lead * SUBS, early, group, part, lanes, lead)
            for step in range(lead):
                held[group, part, step_rows(step), :] = rows[step]
        weights = short_weights(filt_ref, lanes)

        def stage_chunk(index, carry):
            base = index * CHUNK
            for part in (1, 2):
                window = [held[group, part, step_rows(base + at), :] for at in range(CHUNK + lead)]
                rows = short_chunk(weights[part], window)
                for at in range(CHUNK):
                    kv[group, part - 1, step_rows(base + at), :] = rows[at]
            return carry

        lax.fori_loop(0, row_count // SUBS // CHUNK, stage_chunk, 0)
        start_all(leaving(group))

    each_group(groups, one_group)
    each_group(groups, lambda group: wait_all(leaving(group)))


def mix_kernel(
    held, prev_ref, cot_ref, filt_ref, rate_ref, gated, gradm, state_ref, early
):
    groups, row_count, _ = cot_ref.shape
    taps = filt_ref.shape[1]
    modes = rate_ref.shape[0]
    lead = taps - 1
    steps = row_count // SUBS
    early[...] = prev_ref[...].astype(F32)

    def one_group(group):
        lanes = pl.ds(pl.multiple_of(group * LANES, LANES), LANES)
        weights = short_weights(filt_ref, lanes)

        def mix_rows(base, window_of):
            key_rows = short_chunk(weights[1], window_of(1))
            value_rows = short_chunk(weights[2], window_of(2))
            for at in range(CHUNK):
                gated[group, step_rows(base + at), :] = kept(key_rows[at] * value_rows[at])
            query_rows = short_chunk(weights[0], window_of(0))
            for at in range(CHUNK):
                rows = step_rows(base + at)
                gradm[group, rows, :] = kept(cot_ref[group, rows, :] * query_rows[at])

        def inner(base, count):
            return lambda part: [
                held[group, part, step_rows(base + at), :] for at in range(count)
            ]

        def mix_chunk(index, carry):
            base = index * CHUNK
            mix_rows(base, inner(base - lead, CHUNK + lead))
            return carry

        mix_rows(
            0,
            lambda part: earlier_rows(held, 0, early, group, part, lanes, lead)
            + inner(0, CHUNK)(part),
        )
        lax.fori_loop(1, steps // CHUNK, mix_chunk, 0)
        decay = [spread(jnp.exp(-rate_ref[pl.ds(n, 1), lanes])) for n in range(modes)]

        def gather_step(step, carry):
            ends, starts = carry
            ahead = gated[group, step_rows(step), :]
            behind = gradm[group, step_rows(steps - 1 - step), :]
            return (
                [e * d + ahead for e, d in zip(ends, decay)],
                [s * d + behind for s, d in zip(starts, decay)],
            )

        zero = jnp.zeros((SUBS, LANES), F32)
        ends, starts = lax.fori_loop(
            0, steps, gather_step, ([zero] * modes, [zero] * modes), unroll=32
        )
        place = pl.ds(group, 1)
        seg = sub_index().astype(F32) * steps
        for n in range(modes):
            rate = spread(rate_ref[pl.ds(n, 1), lanes])
            to_start = jnp.exp(-rate * seg)
            to_end = jnp.exp(-rate * (steps * (SUBS - 1) - seg))
            state_ref[n, place, :] = jnp.sum(ends[n] * to_end, axis=0, keepdims=True)
            state_ref[modes + n, place, :] = jnp.sum(
                starts[n] * to_start, axis=0, keepdims=True
            )

    each_group(groups, one_group)


def chain_kernel(row_count, half, first_ref, arrived_ref, rate_ref, residue_ref, out_ref):
    blocks, state_rows, _ = arrived_ref.shape
    rate = own_rows(rate_ref, first_ref[0], state_rows)
    step_decay = jnp.exp(-rate * row_count)
    weight = own_rows(residue_ref, first_ref[0], state_rows) * jnp.exp(-rate)

    def run(order):
        def body(index, carry):
            block = order(index)
            out_ref[pl.ds(block, 1)] = (carry * weight)[None]
            return carry * step_decay + arrived_ref[pl.ds(block, 1)][0]

        lax.fori_loop(0, blocks, body, jnp.zeros(rate.shape, F32), unroll=32)

    @pl.when(first_ref[0] < half)
    def _():
        run(lambda index: index)

    @pl.when(first_ref[0] >= half)
    def _():
        run(lambda index: blocks - 1 - index)


def local_kernel(groups, given, gated, gradm, residue_ref, rate_ref, *refs):
    ahead, behind, seg_out, seg_states, sems = refs[given:]
    _, row_count, _ = gated.shape
    modes = rate_ref.shape[0]
    steps = row_count // SUBS
    leaving = slabs(sems, [(seg_states, seg_out)])

    def one_group(group):
        lanes = pl.ds(pl.multiple_of(group * LANES, LANES), LANES)
        weight = [spread(residue_ref[pl.ds(n, 1), lanes]) for n in range(modes)]
        rates = [rate_ref[pl.ds(n, 1), lanes] for n in range(modes)]
        decay = [spread(jnp.exp(-r)) for r in rates]
        zero = jnp.zeros((SUBS, LANES), F32)
        for source, target, backward in ((gated, ahead, False), (gradm, behind, True)):

            def scan_chunk(index, states):
                base = (steps // CHUNK - 1 - index if backward else index) * CHUNK
                values = [source[group, step_rows(base + at), :] for at in range(CHUNK)]
                made = [None] * CHUNK
                for at in range(CHUNK)[:: -1 if backward else 1]:
                    states = [s * d + values[at] for s, d in zip(states, decay)]
                    made[at] = tapped(weight, states)
                for at in range(CHUNK):
                    target[group, step_rows(base + at), :] = made[at]
                return states

            states = lax.fori_loop(0, steps // CHUNK, scan_chunk, [zero] * modes)
            sub = sub_index()
            for n in range(modes):
                span = spread(jnp.exp(-rates[n] * steps))
                total = states[n]
                for shift in (1, 2, 4):
                    if backward:
                        moved = jnp.where(
                            sub < SUBS - shift, pltpu.roll(total, SUBS - shift, 0), 0.0
                        )
                    else:
                        moved = jnp.where(sub >= shift, pltpu.roll(total, shift, 0), 0.0)
                    total = total + span * moved
                    span = span * span
                if backward:
                    enters = jnp.where(sub < SUBS - 1, pltpu.roll(total, SUBS - 1, 0), 0.0)
                else:
                    enters = jnp.where(sub >= 1, pltpu.roll(total, 1, 0), 0.0)
                seg_states[group, int(backward), n] = enters * weight[n] * decay[n]
        start_all(leaving(group))

    each_group(groups, one_group)
    each_group(groups, lambda group: wait_all(leaving(group)))


def grad_kernel(
    share, held_ref, kv_ref, seg_ref, ahead, behind, cot, enter_ref, rate_ref,
    query_mix, key_mix, value_mix, head_ref, short_ref,
    held, kv, seg_states, short, sems,
):
    groups, row_count, _ = cot.shape
    arriving = slabs(
        sems, [(seg_ref, seg_states), (held_ref, held), (kv_ref, kv)]
    )
    each_group(groups, lambda group: start_all(arriving(group)))
    modes = rate_ref.shape[0]
    steps = row_count // SUBS
    lead = held.shape[2] // SUBS - steps
    taps = lead + 1
    mix = (query_mix, key_mix, value_mix)
    short_ref[...] = jnp.zeros(short_ref.shape, F32)
    head_ref[...] = jnp.zeros(head_ref.shape, BF16)

    def one_group(group):
        lanes = pl.ds(pl.multiple_of(group * LANES, LANES), LANES)
        place = pl.ds(group, 1)
        rates = [spread(rate_ref[pl.ds(n, 1), lanes]) for n in range(modes)]
        decay = [jnp.exp(-r) for r in rates]
        seg = sub_index().astype(F32) * steps
        wait_all(arriving(group))
        for backward in (False, True):
            gap = steps * (SUBS - 1) - seg if backward else seg
            carried = []
            for n in range(modes):
                outer = spread(enter_ref[int(backward) * modes + n, place, :])
                inner = seg_states[group, int(backward), n]
                carried.append(inner + jnp.exp(-rates[n] * gap) * outer)
            parts = (1, 2) if backward else (0,)
            def grad_chunk(index, carry):
                carried, sums = carry
                base = (steps // CHUNK - 1 - index if backward else index) * CHUNK
                source = behind if backward else ahead
                long_rows = [None] * CHUNK
                for at in range(CHUNK)[:: -1 if backward else 1]:
                    long_rows[at] = source[group, step_rows(base + at), :] + added(carried)
                    carried = [c * d for c, d in zip(carried, decay)]
                new_sums = []
                for part, old in zip(parts, sums):
                    grads = []
                    for at in range(CHUNK):
                        rows = step_rows(base + at)
                        factor = cot[group, rows, :] if part == 0 else kv[group, 2 - part, rows, :]
                        grads.append(kept(long_rows[at] * factor))
                        mix[part][group, rows, :] = grads[at]
                    window = [
                        held[group, part, step_rows(base + at), :] for at in range(CHUNK + lead)
                    ]
                    new_sums.append(
                        [
                            old[k] + tapped(grads, window[lead - k : lead - k + CHUNK])
                            for k in range(taps)
                        ]
                    )
                return carried, new_sums

            zero = jnp.zeros((SUBS, LANES), F32)
            _, sums = lax.fori_loop(
                0, steps // CHUNK, grad_chunk, (carried, [[zero] * taps for _ in parts])
            )
            for part, taken in zip(parts, sums):
                for k in range(taps):
                    short[part * taps + k, place, :] = jnp.sum(taken[k], axis=0, keepdims=True)
                first = [mix[part][group, pl.ds(step * SUBS, 1), :] for step in range(lead)]
                first += [jnp.zeros((1, LANES), F32)] * (HALO - lead)
                head_ref[part, :, lanes] = jnp.concatenate(first, axis=0).astype(BF16)

    each_group(groups, one_group)
    for piece in range(short_ref.shape[0]):
        for slot in range(share):
            row, group = divmod(piece * share + slot, groups)
            if row < 3 * taps:
                short_ref[piece, slot : slot + 1, :] = short[row, group : group + 1, :]


def back_kernel(
    query_mix, key_mix, value_mix, next_ref, filt_ref, out_ref, late, made, wide, sems
):
    mix = (query_mix, key_mix, value_mix)
    taps = filt_ref.shape[1]
    row_count, channels = made.shape
    groups = channels // LANES
    steps = row_count // SUBS
    perm = step_major(row_count, True)
    late[...] = next_ref[...].astype(F32)
    copies = []
    for part in range(3):

        def one_group(group):
            lanes = pl.ds(pl.multiple_of(group * LANES, LANES), LANES)
            weights = [spread(filt_ref[part, pl.ds(k, 1), lanes]) for k in range(taps)]

            def back_rows(base, window):
                rows = [tapped(weights, window[at : at + taps]) for at in range(CHUNK)]
                made[step_rows(base, CHUNK), lanes] = jnp.concatenate(rows, axis=0).astype(BF16)

            def back_chunk(index, carry):
                base = index * CHUNK
                back_rows(
                    base,
                    [mix[part][group, step_rows(base + at), :] for at in range(CHUNK + taps - 1)],
                )
                return carry

            last = steps - CHUNK
            lax.fori_loop(0, last // CHUNK, back_chunk, 0)
            window = [mix[part][group, step_rows(last + at), :] for at in range(CHUNK)]
            for step in range(taps - 1):
                first = mix[part][group, step_rows(step), :]
                row = late[part, pl.ds(step, 1), lanes]
                window.append(
                    jnp.where(sub_index() == SUBS - 1, spread(row), pltpu.roll(first, SUBS - 1, 0))
                )
            back_rows(last, window)

        each_group(groups, one_group)
        wide[part] = jnp.dot(perm, made[...], preferred_element_type=F32).astype(BF16)
        copies.append(pltpu.make_async_copy(wide.at[part], out_ref.at[part], sems.at[part]))
        copies[-1].start()
    wait_all(copies)


def line_kernel(share, columns, part_ref, out_ref):
    lines = part_ref.shape[0] // columns
    totals = [
        added([part_ref[line * columns + column, :share, :] for line in range(lines)])
        for column in range(columns)
    ]
    totals = jnp.concatenate(totals, axis=0).astype(BF16)
    for plane in range(out_ref.shape[0]):
        out_ref[plane] = totals


def plane_kernel(share, part_ref, out_ref):
    planes, rows, _ = part_ref.shape
    piece_rows = out_ref.shape[1]
    totals = added([part_ref[plane].astype(F32) for plane in range(planes)])
    squares = jnp.sum(totals * totals)
    marks = jnp.full((piece_rows - share, LANES), squares, F32)
    columns = rows // share
    for column in range(columns):
        own = totals[column * share : (column + 1) * share]
        piece = jnp.concatenate([own, marks], axis=0)
        for line in range(out_ref.shape[0] // columns):
            out_ref[line * columns + column] = piece


def scale_kernel(clip_limit, share, sums_ref, out_ref):
    squares = added([sums_ref[piece, share : share + 1, :] for piece in range(sums_ref.shape[0])])
    factor = jnp.minimum(1.0, clip_limit / (jnp.sqrt(squares) + 1e-06))
    _, taps, channels = out_ref.shape
    groups = channels // LANES
    for part in range(3):
        for k in range(taps):
            for group in range(groups):
                piece, row = divmod((part * taps + k) * groups + group, share)
                out_ref[part, k : k + 1, pl.ds(group * LANES, LANES)] = (
                    sums_ref[piece, row : row + 1, :] * factor
                )


def passed_along(shard, by):
    length = lax.axis_size("ctx")
    pairs = [(i, i + by) for i in range(length) if 0 <= i + by < length]
    return lax.ppermute(shard, "ctx", pairs)


def exchange(blocks, axis, members=None):
    return lax.all_to_all(
        blocks, axis, split_axis=0, concat_axis=0, tiled=True, axis_index_groups=members
    )


def cost(flops, bytes_accessed):
    return pl.CostEstimate(flops=flops, bytes_accessed=bytes_accessed, transcendentals=0)


def per_device(inputs, cotangent, short_filter, residue, decay_rate):
    _, row_count, channels = inputs.shape
    taps = short_filter.shape[1]
    modes = residue.shape[0]
    blocks = lax.axis_size("ctx")
    groups = channels // LANES
    lead = taps - 1
    long_rows = row_count + lead * SUBS

    def shaped(dtype, *dims):
        return jax.ShapeDtypeStruct(dims, dtype)

    def near(dtype, *dims):
        return pltpu.VMEM(dims, dtype)

    def far(dtype, *dims):
        return pltpu.HBM(dims, dtype)

    def from_near(*values):
        return [pltpu.with_memory_space_constraint(v, pltpu.VMEM) for v in values]

    def from_far(*values):
        return [pltpu.with_memory_space_constraint(v, pltpu.HBM) for v in values]

    small = pltpu.CompilerParams(vmem_limit_bytes=4 << 20)
    params = pltpu.CompilerParams(vmem_limit_bytes=24 << 20)
    at_vmem = pl.BlockSpec(memory_space=pltpu.VMEM)
    at_hbm = pl.BlockSpec(memory_space=pltpu.HBM)
    sems = pltpu.SemaphoreType.DMA
    work = row_count * channels
    held_dims = (groups, 3, long_rows, LANES)
    part_dims = (groups, 3, row_count, LANES)
    row_dims = (groups, row_count, LANES)
    kv_dims = (groups, 2, row_count, LANES)
    seg_dims = (groups, 2, modes, SUBS, LANES)

    state_rows = 2 * modes * groups // blocks
    first = lax.axis_index("ctx") * state_rows
    half = modes * groups

    held, cot_held, filt, rate, weight = pl.pallas_call(
        load_kernel,
        in_specs=[at_hbm] * 5,
        out_specs=[at_vmem] * 5,
        out_shape=[
            near(F32, *part_dims),
            near(F32, *row_dims),
            near(F32, 3, taps, channels),
            near(F32, modes, channels),
            near(F32, modes, channels),
        ],
        scratch_shapes=[pltpu.VMEM((4, row_count, channels), BF16), sems((4,)), sems((3,))],
        compiler_params=params,
        cost_estimate=cost(work * 2000, work * 8),
        name="load",
    )(*from_far(inputs, cotangent, short_filter, decay_rate, residue))
    prev = passed_along(inputs[:, row_count - HALO :, :], 1)
    prev, held, cot_held = lax.optimization_barrier((prev, held, cot_held))
    gated, gradm, states = pl.pallas_call(
        mix_kernel,
        in_specs=[at_vmem] * 5,
        out_specs=[at_vmem] * 3,
        out_shape=[
            near(F32, *row_dims),
            near(F32, *row_dims),
            far(F32, 2 * modes, groups, LANES),
        ],
        scratch_shapes=[pltpu.VMEM((3, HALO, channels), F32)],
        compiler_params=params,
        cost_estimate=cost(work * 110, work * 24),
        name="mix",
    )(*from_near(held), prev, *from_near(cot_held, filt, rate))

    arrived = exchange(states.reshape(blocks, state_rows, LANES), "ctx")
    held, kv = pl.pallas_call(
        stage_kernel,
        in_specs=[at_hbm] * 2 + [at_vmem],
        out_specs=[at_hbm] * 2,
        out_shape=[far(F32, *held_dims), far(F32, *kv_dims)],
        scratch_shapes=[
            pltpu.VMEM(held_dims, F32),
            pltpu.VMEM(kv_dims, F32),
            pltpu.VMEM((3, taps, channels), F32),
            pltpu.VMEM((3, HALO, channels), F32),
            pltpu.VMEM((3, row_count, channels), BF16),
            sems((3,)),
            sems((1,)),
            sems((2, groups)),
        ],
        compiler_params=params,
        cost_estimate=cost(work * 2000, work * 18),
        name="stage",
    )(*from_far(inputs, short_filter), prev)
    def local_sums(span, gated, gradm, seg_states=None):
        seg = [] if seg_states is None else from_far(seg_states)
        return pl.pallas_call(
            functools.partial(local_kernel, span, len(seg)),
            in_specs=[at_vmem] * 4 + [at_hbm] * len(seg),
            out_specs=[at_vmem] * 2 + [at_hbm],
            out_shape=[near(F32, *row_dims), near(F32, *row_dims), far(F32, *seg_dims)],
            scratch_shapes=[pltpu.VMEM(seg_dims, F32), sems((1, groups))],
            input_output_aliases={0: 0, 1: 1, **({4: 2} if seg else {})},
            compiler_params=params,
            cost_estimate=cost(work * 16 * (span[1] - span[0]), work * 18),
            name="local",
        )(*from_near(gated, gradm, weight, rate), *seg)

    early_groups = groups // 8
    if early_groups:
        ahead, behind, seg_states = local_sums((0, early_groups), gated, gradm)
        arrived, held, kv, seg_states = lax.optimization_barrier((arrived, held, kv, seg_states))
    else:
        ahead, behind, seg_states = gated, gradm, None
        arrived, held, kv = lax.optimization_barrier((arrived, held, kv))

    entering = pl.pallas_call(
        functools.partial(chain_kernel, row_count, half),
        in_specs=[
            pl.BlockSpec(memory_space=pltpu.SMEM),
            at_vmem,
            at_vmem,
            at_vmem,
        ],
        out_specs=at_vmem,
        out_shape=shaped(F32, blocks, state_rows, LANES),
        compiler_params=small,
        cost_estimate=cost(blocks * state_rows * LANES * 2, blocks * state_rows * LANES * 8),
        name="chain",
    )(first[None], arrived, *from_near(rate, weight))
    entering = exchange(entering, "ctx").reshape(2 * modes, groups, LANES)

    ahead, behind, seg_states = local_sums((early_groups, groups), ahead, behind, seg_states)
    entering, seg_states = lax.optimization_barrier((entering, seg_states))

    tp_count = lax.axis_size("tp")
    planes = blocks // LINES
    in_plane = LINES * tp_count
    share = -(-3 * taps * groups // in_plane)
    piece_rows = -(-(share + 1) // SUBS) * SUBS
    plane_members = [
        [(y * planes + z) * tp_count + m for y in range(LINES) for m in range(tp_count)]
        for z in range(planes)
    ]
    line_members = [[y * planes + z for z in range(planes)] for y in range(LINES)]
    *grad_mix, head, short_part = pl.pallas_call(
        functools.partial(grad_kernel, share),
        in_specs=[at_hbm] * 3 + [at_vmem] * 5,
        out_specs=[at_vmem] * 5,
        out_shape=[
            near(F32, *row_dims),
            near(F32, *row_dims),
            near(F32, *row_dims),
            shaped(BF16, 3, HALO, channels),
            far(F32, in_plane, piece_rows, LANES),
        ],
        scratch_shapes=[
            pltpu.VMEM(held_dims, F32),
            pltpu.VMEM(kv_dims, F32),
            pltpu.VMEM(seg_dims, F32),
            pltpu.VMEM((3 * taps, groups, LANES), F32),
            sems((3, groups)),
        ],
        input_output_aliases={3: 0, 4: 1, 5: 2},
        compiler_params=params,
        cost_estimate=cost(work * 110, work * 30),
        name="grad",
    )(
        *from_far(held, kv, seg_states), *from_near(ahead, behind, cot_held), entering, rate
    )

    gathered = exchange(short_part, ("ctx", "tp"), plane_members)
    late = passed_along(head, -1)
    own_sum = pl.pallas_call(
        functools.partial(line_kernel, share, tp_count),
        in_specs=[at_vmem],
        out_specs=at_vmem,
        out_shape=shaped(BF16, planes, tp_count * share, LANES),
        compiler_params=small,
        name="line",
    )(gathered)
    all_sums = exchange(own_sum, "ctx", line_members)
    grad_inputs = pl.pallas_call(
        back_kernel,
        in_specs=[at_vmem] * 5,
        out_specs=at_hbm,
        out_shape=far(BF16, 3, row_count, channels),
        scratch_shapes=[
            pltpu.VMEM((3, HALO, channels), F32),
            pltpu.VMEM((row_count, channels), BF16),
            pltpu.VMEM((3, row_count, channels), BF16),
            sems((3,)),
        ],
        compiler_params=params,
        cost_estimate=cost(work * 48, work * 12),
        name="back",
    )(*from_near(*grad_mix), late, *from_near(filt))
    all_sums, grad_inputs = lax.optimization_barrier((all_sums, grad_inputs))
    all_sums = pl.pallas_call(
        functools.partial(plane_kernel, share),
        in_specs=[at_vmem],
        out_specs=at_vmem,
        out_shape=shaped(F32, in_plane, piece_rows, LANES),
        compiler_params=small,
        name="plane",
    )(all_sums)
    all_sums = exchange(all_sums, ("ctx", "tp"), plane_members)
    clip_limit = math.sqrt(3 * channels * tp_count * taps)
    grad_short = pl.pallas_call(
        functools.partial(scale_kernel, clip_limit, share),
        in_specs=[at_vmem],
        out_specs=at_vmem,
        out_shape=shaped(F32, 3, taps, channels),
        compiler_params=small,
        name="scale",
    )(all_sums)
    return (grad_inputs, grad_short)


def solution(mesh):
    return jax.shard_map(
        per_device,
        mesh=mesh,
        in_specs=(
            P(None, "ctx", "tp"),
            P("ctx", "tp"),
            P(None, None, "tp"),
            P(None, "tp"),
            P(None, "tp"),
        ),
        out_specs=(P(None, "ctx", "tp"), P(None, None, "tp")),
        check_vma=False,
    )
```

```python
import functools
import math

import jax
import jax.numpy as jnp
from jax import lax
from jax.experimental import pallas as pl
from jax.experimental.pallas import tpu as pltpu
from jax.sharding import PartitionSpec as P

LANES = 128
SUBS = 8
HALO = 8
CHUNK = 16
LINES = 4
F32 = jnp.float32
BF16 = jnp.bfloat16


def sub_index():
    return lax.broadcasted_iota(jnp.int32, (SUBS, LANES), 0)


def step_major(row_count, inverse):
    kept = lax.broadcasted_iota(jnp.int32, (row_count, row_count), 1 if inverse else 0)
    time = lax.broadcasted_iota(jnp.int32, (row_count, row_count), 0 if inverse else 1)
    source = (kept & (SUBS - 1)) * (row_count // SUBS) + (kept >> 3)
    return jnp.where(source == time, 1.0, 0.0).astype(BF16)


def spread(row):
    return jnp.broadcast_to(row, (SUBS, LANES))


def step_rows(first, count=1):
    return pl.ds(pl.multiple_of(first * SUBS, SUBS), count * SUBS)


def kept(value):
    return value.astype(BF16).astype(F32)


def added(terms):
    while len(terms) > 1:
        odd = terms[-1:] if len(terms) % 2 else []
        terms = [a + b for a, b in zip(terms[::2], terms[1::2])] + odd
    return terms[0]


def tapped(weights, rows):
    return added([w * r for w, r in zip(weights, rows)])


def each_group(groups, body):
    first, last = groups if isinstance(groups, tuple) else (0, groups)

    def step(group, carry):
        body(group)
        return carry

    lax.fori_loop(first, last, step, 0)


def slabs(sems, pairs):
    def of(group):
        return [
            pltpu.make_async_copy(source.at[group], target.at[group], sems.at[index, group])
            for index, (source, target) in enumerate(pairs)
        ]

    return of


def start_all(copies):
    for copy in copies:
        copy.start()


def wait_all(copies):
    for copy in copies:
        copy.wait()


def earlier_rows(held, first_row, early, group, part, lanes, lead):
    steps = (held.shape[2] - first_row) // SUBS
    made = []
    for step in range(lead):
        late = held[group, part, pl.ds(first_row + (steps - lead + step) * SUBS, SUBS), :]
        first = early[part, pl.ds(HALO - lead + step, 1), lanes]
        made.append(jnp.where(sub_index() == 0, spread(first), pltpu.roll(late, 1, 0)))
    return made


def short_weights(filt_ref, lanes):
    return [
        [spread(filt_ref[part, pl.ds(k, 1), lanes]) for k in range(filt_ref.shape[1])]
        for part in range(3)
    ]


def short_chunk(weights, window):
    taps = len(weights)
    return [tapped(weights, window[at : at + taps][::-1]) for at in range(CHUNK)]


def load_rows(sources, targets, wide, sems):
    row_count, channels = sources[0].shape
    copies = [
        pltpu.make_async_copy(source, wide.at[part], sems.at[part])
        for part, source in enumerate(sources)
    ]
    start_all(copies)
    perm = step_major(row_count, False)
    for part, copy in enumerate(copies):
        copy.wait()
        rows = jnp.dot(perm, wide[part], preferred_element_type=F32)
        for group in range(channels // LANES):
            slab = rows[:, group * LANES : (group + 1) * LANES]
            targets[part](group)[...] = slab


def own_rows(values, first, count):
    modes, channels = values.shape
    groups = channels // LANES
    wide = min(count, groups)
    at_mode = lax.broadcasted_iota(jnp.int32, (modes, wide * LANES), 0)
    start = lax.rem(first, modes * groups)
    mode, group = lax.div(start, groups), lax.rem(start, groups)
    lanes = pl.ds(pl.multiple_of(group * LANES, LANES), wide * LANES)
    rows = []
    for index in range(count // wide):
        picked = jnp.where(at_mode == mode + index, values[:, lanes], 0.0)
        row = jnp.sum(picked, axis=0, keepdims=True)
        rows += [row[:, at * LANES : (at + 1) * LANES] for at in range(wide)]
    return jnp.concatenate(rows, axis=0)


def load_kernel(
    x_ref, cot_ref, filt_ref, rate_ref, residue_ref,
    held_ref, cot_held_ref, filt_out, rate_out, residue_out,
    wide, sems, small_sems,
):
    sources = [filt_ref, rate_ref, residue_ref]
    targets = [filt_out, rate_out, residue_out]
    copies = [
        pltpu.make_async_copy(source, target, small_sems.at[index])
        for index, (source, target) in enumerate(zip(sources, targets))
    ]
    start_all(copies)
    load_rows(
        [x_ref.at[part] for part in range(3)] + [cot_ref],
        [lambda group, part=part: held_ref.at[group, part] for part in range(3)]
        + [lambda group: cot_held_ref.at[group]],
        wide,
        sems,
    )
    wait_all(copies)


def stage_kernel(
    x_ref, filt_in, prev_ref, held_out, kv_out,
    held, kv, filt_ref, early, wide, sems, filt_sem, out_sems,
):
    filt_copy = pltpu.make_async_copy(filt_in, filt_ref, filt_sem.at[0])
    filt_copy.start()
    groups, _, row_count, _ = kv_out.shape
    lead = filt_ref.shape[1] - 1
    below = pl.ds(lead * SUBS, row_count)
    load_rows(
        [x_ref.at[part] for part in range(3)],
        [lambda group, part=part: held.at[group, part, below, :] for part in range(3)],
        wide,
        sems,
    )
    early[...] = prev_ref[...].astype(F32)
    leaving = slabs(out_sems, [(held, held_out), (kv, kv_out)])
    filt_copy.wait()

    def one_group(group):
        lanes = pl.ds(pl.multiple_of(group * LANES, LANES), LANES)
        for part in range(3):
            rows = earlier_rows(held, lead * SUBS, early, group, part, lanes, lead)
            for step in range(lead):
                held[group, part, step_rows(step), :] = rows[step]
        weights = short_weights(filt_ref, lanes)

        def stage_chunk(index, carry):
            base = index * CHUNK
            for part in (1, 2):
                window = [held[group, part, step_rows(base + at), :] for at in range(CHUNK + lead)]
                rows = short_chunk(weights[part], window)
                for at in range(CHUNK):
                    kv[group, part - 1, step_rows(base + at), :] = rows[at]
            return carry

        lax.fori_loop(0, row_count // SUBS // CHUNK, stage_chunk, 0)
        start_all(leaving(group))

    each_group(groups, one_group)
    each_group(groups, lambda group: wait_all(leaving(group)))


def mix_kernel(
    held, prev_ref, cot_ref, filt_ref, rate_ref, gated, gradm, state_ref, early
):
    groups, row_count, _ = cot_ref.shape
    taps = filt_ref.shape[1]
    modes = rate_ref.shape[0]
    lead = taps - 1
    steps = row_count // SUBS
    early[...] = prev_ref[...].astype(F32)

    def one_group(group):
        lanes = pl.ds(pl.multiple_of(group * LANES, LANES), LANES)
        weights = short_weights(filt_ref, lanes)

        def mix_rows(base, window_of):
            key_rows = short_chunk(weights[1], window_of(1))
            value_rows = short_chunk(weights[2], window_of(2))
            for at in range(CHUNK):
                gated[group, step_rows(base + at), :] = kept(key_rows[at] * value_rows[at])
            query_rows = short_chunk(weights[0], window_of(0))
            for at in range(CHUNK):
                rows = step_rows(base + at)
                gradm[group, rows, :] = kept(cot_ref[group, rows, :] * query_rows[at])

        def inner(base, count):
            return lambda part: [
                held[group, part, step_rows(base + at), :] for at in range(count)
            ]

        def mix_chunk(index, carry):
            base = index * CHUNK
            mix_rows(base, inner(base - lead, CHUNK + lead))
            return carry

        mix_rows(
            0,
            lambda part: earlier_rows(held, 0, early, group, part, lanes, lead)
            + inner(0, CHUNK)(part),
        )
        lax.fori_loop(1, steps // CHUNK, mix_chunk, 0)
        decay = [spread(jnp.exp(-rate_ref[pl.ds(n, 1), lanes])) for n in range(modes)]

        def gather_step(step, carry):
            ends, starts = carry
            ahead = gated[group, step_rows(step), :]
            behind = gradm[group, step_rows(steps - 1 - step), :]
            return (
                [e * d + ahead for e, d in zip(ends, decay)],
                [s * d + behind for s, d in zip(starts, decay)],
            )

        zero = jnp.zeros((SUBS, LANES), F32)
        ends, starts = lax.fori_loop(
            0, steps, gather_step, ([zero] * modes, [zero] * modes), unroll=32
        )
        place = pl.ds(group, 1)
        seg = sub_index().astype(F32) * steps
        for n in range(modes):
            rate = spread(rate_ref[pl.ds(n, 1), lanes])
            to_start = jnp.exp(-rate * seg)
            to_end = jnp.exp(-rate * (steps * (SUBS - 1) - seg))
            state_ref[n, place, :] = jnp.sum(ends[n] * to_end, axis=0, keepdims=True)
            state_ref[modes + n, place, :] = jnp.sum(
                starts[n] * to_start, axis=0, keepdims=True
            )

    each_group(groups, one_group)


def chain_kernel(row_count, half, first_ref, arrived_ref, rate_ref, residue_ref, out_ref):
    blocks, state_rows, _ = arrived_ref.shape
    rate = own_rows(rate_ref, first_ref[0], state_rows)
    step_decay = jnp.exp(-rate * row_count)
    weight = own_rows(residue_ref, first_ref[0], state_rows) * jnp.exp(-rate)

    def run(order):
        def body(index, carry):
            block = order(index)
            out_ref[pl.ds(block, 1)] = (carry * weight)[None]
            return carry * step_decay + arrived_ref[pl.ds(block, 1)][0]

        lax.fori_loop(0, blocks, body, jnp.zeros(rate.shape, F32), unroll=32)

    @pl.when(first_ref[0] < half)
    def _():
        run(lambda index: index)

    @pl.when(first_ref[0] >= half)
    def _():
        run(lambda index: blocks - 1 - index)


def local_kernel(groups, given, gated, gradm, residue_ref, rate_ref, *refs):
    ahead, behind, seg_out, seg_states, sems = refs[given:]
    _, row_count, _ = gated.shape
    modes = rate_ref.shape[0]
    steps = row_count // SUBS
    leaving = slabs(sems, [(seg_states, seg_out)])

    def one_group(group):
        lanes = pl.ds(pl.multiple_of(group * LANES, LANES), LANES)
        weight = [spread(residue_ref[pl.ds(n, 1), lanes]) for n in range(modes)]
        rates = [rate_ref[pl.ds(n, 1), lanes] for n in range(modes)]
        decay = [spread(jnp.exp(-r)) for r in rates]
        zero = jnp.zeros((SUBS, LANES), F32)
        for source, target, backward in ((gated, ahead, False), (gradm, behind, True)):

            def scan_chunk(index, states):
                base = (steps // CHUNK - 1 - index if backward else index) * CHUNK
                values = [source[group, step_rows(base + at), :] for at in range(CHUNK)]
                made = [None] * CHUNK
                for at in range(CHUNK)[:: -1 if backward else 1]:
                    states = [s * d + values[at] for s, d in zip(states, decay)]
                    made[at] = tapped(weight, states)
                for at in range(CHUNK):
                    target[group, step_rows(base + at), :] = made[at]
                return states

            states = lax.fori_loop(0, steps // CHUNK, scan_chunk, [zero] * modes)
            sub = sub_index()
            for n in range(modes):
                span = spread(jnp.exp(-rates[n] * steps))
                total = states[n]
                for shift in (1, 2, 4):
                    if backward:
                        moved = jnp.where(
                            sub < SUBS - shift, pltpu.roll(total, SUBS - shift, 0), 0.0
                        )
                    else:
                        moved = jnp.where(sub >= shift, pltpu.roll(total, shift, 0), 0.0)
                    total = total + span * moved
                    span = span * span
                if backward:
                    enters = jnp.where(sub < SUBS - 1, pltpu.roll(total, SUBS - 1, 0), 0.0)
                else:
                    enters = jnp.where(sub >= 1, pltpu.roll(total, 1, 0), 0.0)
                seg_states[group, int(backward), n] = enters * weight[n] * decay[n]
        start_all(leaving(group))

    each_group(groups, one_group)
    each_group(groups, lambda group: wait_all(leaving(group)))


def grad_kernel(
    share, held_ref, kv_ref, seg_ref, ahead, behind, cot, enter_ref, rate_ref,
    query_mix, key_mix, value_mix, head_ref, short_ref,
    held, kv, seg_states, short, sems,
):
    groups, row_count, _ = cot.shape
    arriving = slabs(
        sems, [(seg_ref, seg_states), (held_ref, held), (kv_ref, kv)]
    )
    each_group(groups, lambda group: start_all(arriving(group)))
    modes = rate_ref.shape[0]
    steps = row_count // SUBS
    lead = held.shape[2] // SUBS - steps
    taps = lead + 1
    mix = (query_mix, key_mix, value_mix)
    short_ref[...] = jnp.zeros(short_ref.shape, F32)
    head_ref[...] = jnp.zeros(head_ref.shape, BF16)

    def one_group(group):
        lanes = pl.ds(pl.multiple_of(group * LANES, LANES), LANES)
        place = pl.ds(group, 1)
        rates = [spread(rate_ref[pl.ds(n, 1), lanes]) for n in range(modes)]
        decay = [jnp.exp(-r) for r in rates]
        seg = sub_index().astype(F32) * steps
        wait_all(arriving(group))
        for backward in (False, True):
            gap = steps * (SUBS - 1) - seg if backward else seg
            carried = []
            for n in range(modes):
                outer = spread(enter_ref[int(backward) * modes + n, place, :])
                inner = seg_states[group, int(backward), n]
                carried.append(inner + jnp.exp(-rates[n] * gap) * outer)
            parts = (1, 2) if backward else (0,)
            def grad_chunk(index, carry):
                carried, sums = carry
                base = (steps // CHUNK - 1 - index if backward else index) * CHUNK
                source = behind if backward else ahead
                long_rows = [None] * CHUNK
                for at in range(CHUNK)[:: -1 if backward else 1]:
                    long_rows[at] = source[group, step_rows(base + at), :] + added(carried)
                    carried = [c * d for c, d in zip(carried, decay)]
                new_sums = []
                for part, old in zip(parts, sums):
                    grads = []
                    for at in range(CHUNK):
                        rows = step_rows(base + at)
                        factor = cot[group, rows, :] if part == 0 else kv[group, 2 - part, rows, :]
                        grads.append(kept(long_rows[at] * factor))
                        mix[part][group, rows, :] = grads[at]
                    window = [
                        held[group, part, step_rows(base + at), :] for at in range(CHUNK + lead)
                    ]
                    new_sums.append(
                        [
                            old[k] + tapped(grads, window[lead - k : lead - k + CHUNK])
                            for k in range(taps)
                        ]
                    )
                return carried, new_sums

            zero = jnp.zeros((SUBS, LANES), F32)
            _, sums = lax.fori_loop(
                0, steps // CHUNK, grad_chunk, (carried, [[zero] * taps for _ in parts])
            )
            for part, taken in zip(parts, sums):
                for k in range(taps):
                    short[part * taps + k, place, :] = jnp.sum(taken[k], axis=0, keepdims=True)
                first = [mix[part][group, pl.ds(step * SUBS, 1), :] for step in range(lead)]
                first += [jnp.zeros((1, LANES), F32)] * (HALO - lead)
                head_ref[part, :, lanes] = jnp.concatenate(first, axis=0).astype(BF16)

    each_group(groups, one_group)
    for piece in range(short_ref.shape[0]):
        for slot in range(share):
            row, group = divmod(piece * share + slot, groups)
            if row < 3 * taps:
                short_ref[piece, slot : slot + 1, :] = short[row, group : group + 1, :]


def back_kernel(
    query_mix, key_mix, value_mix, filt_ref, out_ref, edge_ref, made, wide, sems
):
    mix = (query_mix, key_mix, value_mix)
    taps = filt_ref.shape[1]
    row_count, channels = made.shape
    groups = channels // LANES
    steps = row_count // SUBS
    perm = step_major(row_count, True)
    copies = []
    for part in range(3):

        def one_group(group):
            lanes = pl.ds(pl.multiple_of(group * LANES, LANES), LANES)
            weights = [spread(filt_ref[part, pl.ds(k, 1), lanes]) for k in range(taps)]

            def back_rows(base, window):
                rows = [tapped(weights, window[at : at + taps]) for at in range(CHUNK)]
                made[step_rows(base, CHUNK), lanes] = jnp.concatenate(rows, axis=0).astype(BF16)

            def back_chunk(index, carry):
                base = index * CHUNK
                back_rows(
                    base,
                    [mix[part][group, step_rows(base + at), :] for at in range(CHUNK + taps - 1)],
                )
                return carry

            last = steps - CHUNK
            lax.fori_loop(0, last // CHUNK, back_chunk, 0)
            window = [mix[part][group, step_rows(last + at), :] for at in range(CHUNK)]
            for step in range(taps - 1):
                first = mix[part][group, step_rows(step), :]
                window.append(
                    jnp.where(sub_index() == SUBS - 1, 0.0, pltpu.roll(first, SUBS - 1, 0))
                )
            back_rows(last, window)
            edge = [
                mix[part][group, pl.ds((steps - HALO + row) * SUBS + SUBS - 1, 1), :]
                for row in range(HALO)
            ]
            edge_ref[part, :, lanes] = jnp.concatenate(edge, axis=0)

        each_group(groups, one_group)
        wide[part] = jnp.dot(perm, made[...], preferred_element_type=F32).astype(BF16)
        copies.append(pltpu.make_async_copy(wide.at[part], out_ref.at[part], sems.at[part]))
        copies[-1].start()
    wait_all(copies)


def edge_kernel(out_in, edge_ref, next_ref, filt_ref, out_ref, rows, made, sems):
    del out_in
    taps = filt_ref.shape[1]
    last = out_ref.shape[1] - HALO
    copies = []
    for part in range(3):
        rows[part, pl.ds(0, HALO), :] = edge_ref[part]
        rows[part, pl.ds(HALO, HALO), :] = next_ref[part].astype(F32)
        terms = [
            filt_ref[part, pl.ds(k, 1), :] * rows[part, pl.ds(k, HALO), :] for k in range(taps)
        ]
        made[part] = added(terms).astype(BF16)
        copies.append(
            pltpu.make_async_copy(
                made.at[part], out_ref.at[part, pl.ds(last, HALO), :], sems.at[part]
            )
        )
        copies[-1].start()
    wait_all(copies)


def line_kernel(share, columns, part_ref, out_ref):
    lines = part_ref.shape[0] // columns
    totals = [
        added([part_ref[line * columns + column, :share, :] for line in range(lines)])
        for column in range(columns)
    ]
    totals = jnp.concatenate(totals, axis=0).astype(BF16)
    for plane in range(out_ref.shape[0]):
        out_ref[plane] = totals


def plane_kernel(share, part_ref, out_ref):
    planes, rows, _ = part_ref.shape
    piece_rows = out_ref.shape[1]
    totals = added([part_ref[plane].astype(F32) for plane in range(planes)])
    squares = jnp.sum(totals * totals)
    marks = jnp.full((piece_rows - share, LANES), squares, F32)
    columns = rows // share
    for column in range(columns):
        own = totals[column * share : (column + 1) * share]
        piece = jnp.concatenate([own, marks], axis=0)
        for line in range(out_ref.shape[0] // columns):
            out_ref[line * columns + column] = piece


def scale_kernel(clip_limit, share, sums_ref, out_ref):
    squares = added([sums_ref[piece, share : share + 1, :] for piece in range(sums_ref.shape[0])])
    factor = jnp.minimum(1.0, clip_limit / (jnp.sqrt(squares) + 1e-06))
    _, taps, channels = out_ref.shape
    groups = channels // LANES
    for part in range(3):
        for k in range(taps):
            for group in range(groups):
                piece, row = divmod((part * taps + k) * groups + group, share)
                out_ref[part, k : k + 1, pl.ds(group * LANES, LANES)] = (
                    sums_ref[piece, row : row + 1, :] * factor
                )


def passed_along(shard, by):
    length = lax.axis_size("ctx")
    pairs = [(i, i + by) for i in range(length) if 0 <= i + by < length]
    return lax.ppermute(shard, "ctx", pairs)


def exchange(blocks, axis, members=None):
    return lax.all_to_all(
        blocks, axis, split_axis=0, concat_axis=0, tiled=True, axis_index_groups=members
    )


def cost(flops, bytes_accessed):
    return pl.CostEstimate(flops=flops, bytes_accessed=bytes_accessed, transcendentals=0)


def per_device(inputs, cotangent, short_filter, residue, decay_rate):
    _, row_count, channels = inputs.shape
    taps = short_filter.shape[1]
    modes = residue.shape[0]
    blocks = lax.axis_size("ctx")
    groups = channels // LANES
    lead = taps - 1
    long_rows = row_count + lead * SUBS

    def shaped(dtype, *dims):
        return jax.ShapeDtypeStruct(dims, dtype)

    def near(dtype, *dims):
        return pltpu.VMEM(dims, dtype)

    def far(dtype, *dims):
        return pltpu.HBM(dims, dtype)

    def from_near(*values):
        return [pltpu.with_memory_space_constraint(v, pltpu.VMEM) for v in values]

    def from_far(*values):
        return [pltpu.with_memory_space_constraint(v, pltpu.HBM) for v in values]

    small = pltpu.CompilerParams(vmem_limit_bytes=4 << 20)
    params = pltpu.CompilerParams(vmem_limit_bytes=24 << 20)
    at_vmem = pl.BlockSpec(memory_space=pltpu.VMEM)
    at_hbm = pl.BlockSpec(memory_space=pltpu.HBM)
    sems = pltpu.SemaphoreType.DMA
    work = row_count * channels
    held_dims = (groups, 3, long_rows, LANES)
    part_dims = (groups, 3, row_count, LANES)
    row_dims = (groups, row_count, LANES)
    kv_dims = (groups, 2, row_count, LANES)
    seg_dims = (groups, 2, modes, SUBS, LANES)

    state_rows = 2 * modes * groups // blocks
    first = lax.axis_index("ctx") * state_rows
    half = modes * groups

    held, cot_held, filt, rate, weight = pl.pallas_call(
        load_kernel,
        in_specs=[at_hbm] * 5,
        out_specs=[at_vmem] * 5,
        out_shape=[
            near(F32, *part_dims),
            near(F32, *row_dims),
            near(F32, 3, taps, channels),
            near(F32, modes, channels),
            near(F32, modes, channels),
        ],
        scratch_shapes=[pltpu.VMEM((4, row_count, channels), BF16), sems((4,)), sems((3,))],
        compiler_params=params,
        cost_estimate=cost(work * 2000, work * 8),
        name="load",
    )(*from_far(inputs, cotangent, short_filter, decay_rate, residue))
    prev = passed_along(inputs[:, row_count - HALO :, :], 1)
    prev, held, cot_held = lax.optimization_barrier((prev, held, cot_held))
    gated, gradm, states = pl.pallas_call(
        mix_kernel,
        in_specs=[at_vmem] * 5,
        out_specs=[at_vmem] * 3,
        out_shape=[
            near(F32, *row_dims),
            near(F32, *row_dims),
            far(F32, 2 * modes, groups, LANES),
        ],
        scratch_shapes=[pltpu.VMEM((3, HALO, channels), F32)],
        compiler_params=params,
        cost_estimate=cost(work * 110, work * 24),
        name="mix",
    )(*from_near(held), prev, *from_near(cot_held, filt, rate))

    arrived = exchange(states.reshape(blocks, state_rows, LANES), "ctx")
    held, kv = pl.pallas_call(
        stage_kernel,
        in_specs=[at_hbm] * 2 + [at_vmem],
        out_specs=[at_hbm] * 2,
        out_shape=[far(F32, *held_dims), far(F32, *kv_dims)],
        scratch_shapes=[
            pltpu.VMEM(held_dims, F32),
            pltpu.VMEM(kv_dims, F32),
            pltpu.VMEM((3, taps, channels), F32),
            pltpu.VMEM((3, HALO, channels), F32),
            pltpu.VMEM((3, row_count, channels), BF16),
            sems((3,)),
            sems((1,)),
            sems((2, groups)),
        ],
        compiler_params=params,
        cost_estimate=cost(work * 2000, work * 18),
        name="stage",
    )(*from_far(inputs, short_filter), prev)
    def local_sums(span, gated, gradm, seg_states=None):
        seg = [] if seg_states is None else from_far(seg_states)
        return pl.pallas_call(
            functools.partial(local_kernel, span, len(seg)),
            in_specs=[at_vmem] * 4 + [at_hbm] * len(seg),
            out_specs=[at_vmem] * 2 + [at_hbm],
            out_shape=[near(F32, *row_dims), near(F32, *row_dims), far(F32, *seg_dims)],
            scratch_shapes=[pltpu.VMEM(seg_dims, F32), sems((1, groups))],
            input_output_aliases={0: 0, 1: 1, **({4: 2} if seg else {})},
            compiler_params=params,
            cost_estimate=cost(work * 16 * (span[1] - span[0]), work * 18),
            name="local",
        )(*from_near(gated, gradm, weight, rate), *seg)

    early_groups = groups // 8
    if early_groups:
        ahead, behind, seg_states = local_sums((0, early_groups), gated, gradm)
        arrived, held, kv, seg_states = lax.optimization_barrier((arrived, held, kv, seg_states))
    else:
        ahead, behind, seg_states = gated, gradm, None
        arrived, held, kv = lax.optimization_barrier((arrived, held, kv))

    entering = pl.pallas_call(
        functools.partial(chain_kernel, row_count, half),
        in_specs=[
            pl.BlockSpec(memory_space=pltpu.SMEM),
            at_vmem,
            at_vmem,
            at_vmem,
        ],
        out_specs=at_vmem,
        out_shape=shaped(F32, blocks, state_rows, LANES),
        compiler_params=small,
        cost_estimate=cost(blocks * state_rows * LANES * 2, blocks * state_rows * LANES * 8),
        name="chain",
    )(first[None], arrived, *from_near(rate, weight))
    entering = exchange(entering, "ctx").reshape(2 * modes, groups, LANES)

    ahead, behind, seg_states = local_sums((early_groups, groups), ahead, behind, seg_states)
    entering, seg_states = lax.optimization_barrier((entering, seg_states))

    tp_count = lax.axis_size("tp")
    planes = blocks // LINES
    in_plane = LINES * tp_count
    share = -(-3 * taps * groups // in_plane)
    piece_rows = -(-(share + 1) // SUBS) * SUBS
    plane_members = [
        [(y * planes + z) * tp_count + m for y in range(LINES) for m in range(tp_count)]
        for z in range(planes)
    ]
    line_members = [[y * planes + z for z in range(planes)] for y in range(LINES)]
    *grad_mix, head, short_part = pl.pallas_call(
        functools.partial(grad_kernel, share),
        in_specs=[at_hbm] * 3 + [at_vmem] * 5,
        out_specs=[at_vmem] * 5,
        out_shape=[
            near(F32, *row_dims),
            near(F32, *row_dims),
            near(F32, *row_dims),
            shaped(BF16, 3, HALO, channels),
            far(F32, in_plane, piece_rows, LANES),
        ],
        scratch_shapes=[
            pltpu.VMEM(held_dims, F32),
            pltpu.VMEM(kv_dims, F32),
            pltpu.VMEM(seg_dims, F32),
            pltpu.VMEM((3 * taps, groups, LANES), F32),
            sems((3, groups)),
        ],
        input_output_aliases={3: 0, 4: 1, 5: 2},
        compiler_params=params,
        cost_estimate=cost(work * 110, work * 30),
        name="grad",
    )(
        *from_far(held, kv, seg_states), *from_near(ahead, behind, cot_held), entering, rate
    )

    gathered = exchange(short_part, ("ctx", "tp"), plane_members)
    late = passed_along(head, -1)
    own_sum = pl.pallas_call(
        functools.partial(line_kernel, share, tp_count),
        in_specs=[at_vmem],
        out_specs=at_vmem,
        out_shape=far(BF16, planes, tp_count * share, LANES),
        compiler_params=small,
        name="line",
    )(gathered)
    all_sums = exchange(own_sum, "ctx", line_members)
    grad_inputs, edge = pl.pallas_call(
        back_kernel,
        in_specs=[at_vmem] * 4,
        out_specs=[at_hbm, at_vmem],
        out_shape=[far(BF16, 3, row_count, channels), far(F32, 3, HALO, channels)],
        scratch_shapes=[
            pltpu.VMEM((row_count, channels), BF16),
            pltpu.VMEM((3, row_count, channels), BF16),
            sems((3,)),
        ],
        compiler_params=params,
        cost_estimate=cost(work * 48, work * 12),
        name="back",
    )(*from_near(*grad_mix, filt))
    all_sums, grad_inputs, late = lax.optimization_barrier((all_sums, grad_inputs, late))
    all_sums = pl.pallas_call(
        functools.partial(plane_kernel, share),
        in_specs=[at_vmem],
        out_specs=at_vmem,
        out_shape=shaped(F32, in_plane, piece_rows, LANES),
        compiler_params=small,
        name="plane",
    )(all_sums)
    all_sums = exchange(all_sums, ("ctx", "tp"), plane_members)
    grad_inputs = pl.pallas_call(
        edge_kernel,
        in_specs=[at_hbm] + [at_vmem] * 3,
        out_specs=at_hbm,
        out_shape=far(BF16, 3, row_count, channels),
        scratch_shapes=[
            pltpu.VMEM((3, 2 * HALO, channels), F32),
            pltpu.VMEM((3, HALO, channels), BF16),
            sems((3,)),
        ],
        input_output_aliases={0: 0},
        compiler_params=small,
        cost_estimate=cost(work, work),
        name="edge",
    )(*from_far(grad_inputs), edge, late, *from_near(filt))
    all_sums, grad_inputs = lax.optimization_barrier((all_sums, grad_inputs))
    clip_limit = math.sqrt(3 * channels * tp_count * taps)
    grad_short = pl.pallas_call(
        functools.partial(scale_kernel, clip_limit, share),
        in_specs=[at_vmem],
        out_specs=at_vmem,
        out_shape=shaped(F32, 3, taps, channels),
        compiler_params=small,
        name="scale",
    )(all_sums)
    return (grad_inputs, grad_short)


def solution(mesh):
    return jax.shard_map(
        per_device,
        mesh=mesh,
        in_specs=(
            P(None, "ctx", "tp"),
            P("ctx", "tp"),
            P(None, None, "tp"),
            P(None, "tp"),
            P(None, "tp"),
        ),
        out_specs=(P(None, "ctx", "tp"), P(None, None, "tp")),
        check_vma=False,
    )
```

```python
import functools
import math

import jax
import jax.numpy as jnp
from jax import lax
from jax.experimental import pallas as pl
from jax.experimental.pallas import tpu as pltpu
from jax.sharding import PartitionSpec as P

LANES = 128
SUBS = 8
HALO = 8
CHUNK = 16
LINES = 4
F32 = jnp.float32
BF16 = jnp.bfloat16


def sub_index():
    return lax.broadcasted_iota(jnp.int32, (SUBS, LANES), 0)


def step_major(row_count, inverse):
    kept = lax.broadcasted_iota(jnp.int32, (row_count, row_count), 1 if inverse else 0)
    time = lax.broadcasted_iota(jnp.int32, (row_count, row_count), 0 if inverse else 1)
    source = (kept & (SUBS - 1)) * (row_count // SUBS) + (kept >> 3)
    return jnp.where(source == time, 1.0, 0.0).astype(BF16)


def spread(row):
    return jnp.broadcast_to(row, (SUBS, LANES))


def step_rows(first, count=1):
    return pl.ds(pl.multiple_of(first * SUBS, SUBS), count * SUBS)


def kept(value):
    return value.astype(BF16).astype(F32)


def added(terms):
    while len(terms) > 1:
        odd = terms[-1:] if len(terms) % 2 else []
        terms = [a + b for a, b in zip(terms[::2], terms[1::2])] + odd
    return terms[0]


def tapped(weights, rows):
    return added([w * r for w, r in zip(weights, rows)])


def each_group(groups, body):
    first, last = groups if isinstance(groups, tuple) else (0, groups)

    def step(group, carry):
        body(group)
        return carry

    lax.fori_loop(first, last, step, 0)


def slabs(sems, pairs):
    def of(group):
        return [
            pltpu.make_async_copy(source.at[group], target.at[group], sems.at[index, group])
            for index, (source, target) in enumerate(pairs)
        ]

    return of


def start_all(copies):
    for copy in copies:
        copy.start()


def wait_all(copies):
    for copy in copies:
        copy.wait()


def earlier_rows(held, first_row, early, group, part, lanes, lead):
    steps = (held.shape[2] - first_row) // SUBS
    made = []
    for step in range(lead):
        late = held[group, part, pl.ds(first_row + (steps - lead + step) * SUBS, SUBS), :]
        first = early[part, pl.ds(HALO - lead + step, 1), lanes]
        made.append(jnp.where(sub_index() == 0, spread(first), pltpu.roll(late, 1, 0)))
    return made


def short_weights(filt_ref, lanes):
    return [
        [spread(filt_ref[part, pl.ds(k, 1), lanes]) for k in range(filt_ref.shape[1])]
        for part in range(3)
    ]


def short_chunk(weights, window):
    taps = len(weights)
    return [tapped(weights, window[at : at + taps][::-1]) for at in range(CHUNK)]


def load_rows(sources, targets, wide, sems):
    row_count, channels = sources[0].shape
    copies = [
        pltpu.make_async_copy(source, wide.at[part], sems.at[part])
        for part, source in enumerate(sources)
    ]
    start_all(copies)
    perm = step_major(row_count, False)
    for part, copy in enumerate(copies):
        copy.wait()
        rows = jnp.dot(perm, wide[part], preferred_element_type=F32)
        for group in range(channels // LANES):
            slab = rows[:, group * LANES : (group + 1) * LANES]
            targets[part](group)[...] = slab


def own_rows(values, first, count):
    modes, channels = values.shape
    groups = channels // LANES
    wide = min(count, groups)
    at_mode = lax.broadcasted_iota(jnp.int32, (modes, wide * LANES), 0)
    start = lax.rem(first, modes * groups)
    mode, group = lax.div(start, groups), lax.rem(start, groups)
    lanes = pl.ds(pl.multiple_of(group * LANES, LANES), wide * LANES)
    rows = []
    for index in range(count // wide):
        picked = jnp.where(at_mode == mode + index, values[:, lanes], 0.0)
        row = jnp.sum(picked, axis=0, keepdims=True)
        rows += [row[:, at * LANES : (at + 1) * LANES] for at in range(wide)]
    return jnp.concatenate(rows, axis=0)


def load_kernel(
    x_ref, cot_ref, filt_ref, rate_ref, residue_ref,
    held_ref, cot_held_ref, filt_out, rate_out, residue_out,
    wide, sems, small_sems,
):
    sources = [filt_ref, rate_ref, residue_ref]
    targets = [filt_out, rate_out, residue_out]
    copies = [
        pltpu.make_async_copy(source, target, small_sems.at[index])
        for index, (source, target) in enumerate(zip(sources, targets))
    ]
    start_all(copies)
    load_rows(
        [x_ref.at[part] for part in range(3)] + [cot_ref],
        [lambda group, part=part: held_ref.at[group, part] for part in range(3)]
        + [lambda group: cot_held_ref.at[group]],
        wide,
        sems,
    )
    wait_all(copies)


def stage_kernel(
    x_ref, filt_in, prev_ref, held_out, kv_out,
    held, kv, filt_ref, early, wide, sems, filt_sem, out_sems,
):
    filt_copy = pltpu.make_async_copy(filt_in, filt_ref, filt_sem.at[0])
    filt_copy.start()
    groups, _, row_count, _ = kv_out.shape
    lead = filt_ref.shape[1] - 1
    below = pl.ds(lead * SUBS, row_count)
    load_rows(
        [x_ref.at[part] for part in range(3)],
        [lambda group, part=part: held.at[group, part, below, :] for part in range(3)],
        wide,
        sems,
    )
    early[...] = prev_ref[...].astype(F32)
    leaving = slabs(out_sems, [(held, held_out), (kv, kv_out)])
    filt_copy.wait()

    def one_group(group):
        lanes = pl.ds(pl.multiple_of(group * LANES, LANES), LANES)
        for part in range(3):
            rows = earlier_rows(held, lead * SUBS, early, group, part, lanes, lead)
            for step in range(lead):
                held[group, part, step_rows(step), :] = rows[step]
        weights = short_weights(filt_ref, lanes)

        def stage_chunk(index, carry):
            base = index * CHUNK
            for part in (1, 2):
                window = [held[group, part, step_rows(base + at), :] for at in range(CHUNK + lead)]
                rows = short_chunk(weights[part], window)
                for at in range(CHUNK):
                    kv[group, part - 1, step_rows(base + at), :] = rows[at]
            return carry

        lax.fori_loop(0, row_count // SUBS // CHUNK, stage_chunk, 0)
        start_all(leaving(group))

    each_group(groups, one_group)
    each_group(groups, lambda group: wait_all(leaving(group)))


def mix_kernel(
    held, prev_ref, cot_ref, filt_ref, rate_ref, gated, gradm, state_ref, early
):
    groups, row_count, _ = cot_ref.shape
    taps = filt_ref.shape[1]
    modes = rate_ref.shape[0]
    lead = taps - 1
    steps = row_count // SUBS
    early[...] = prev_ref[...].astype(F32)

    def one_group(group):
        lanes = pl.ds(pl.multiple_of(group * LANES, LANES), LANES)
        weights = short_weights(filt_ref, lanes)

        def mix_rows(base, window_of):
            key_rows = short_chunk(weights[1], window_of(1))
            value_rows = short_chunk(weights[2], window_of(2))
            for at in range(CHUNK):
                gated[group, step_rows(base + at), :] = kept(key_rows[at] * value_rows[at])
            query_rows = short_chunk(weights[0], window_of(0))
            for at in range(CHUNK):
                rows = step_rows(base + at)
                gradm[group, rows, :] = kept(cot_ref[group, rows, :] * query_rows[at])

        def inner(base, count):
            return lambda part: [
                held[group, part, step_rows(base + at), :] for at in range(count)
            ]

        def mix_chunk(index, carry):
            base = index * CHUNK
            mix_rows(base, inner(base - lead, CHUNK + lead))
            return carry

        mix_rows(
            0,
            lambda part: earlier_rows(held, 0, early, group, part, lanes, lead)
            + inner(0, CHUNK)(part),
        )
        lax.fori_loop(1, steps // CHUNK, mix_chunk, 0)
        decay = [spread(jnp.exp(-rate_ref[pl.ds(n, 1), lanes])) for n in range(modes)]

        def gather_step(step, carry):
            ends, starts = carry
            ahead = gated[group, step_rows(step), :]
            behind = gradm[group, step_rows(steps - 1 - step), :]
            return (
                [e * d + ahead for e, d in zip(ends, decay)],
                [s * d + behind for s, d in zip(starts, decay)],
            )

        zero = jnp.zeros((SUBS, LANES), F32)
        ends, starts = lax.fori_loop(
            0, steps, gather_step, ([zero] * modes, [zero] * modes), unroll=32
        )
        place = pl.ds(group, 1)
        seg = sub_index().astype(F32) * steps
        for n in range(modes):
            rate = spread(rate_ref[pl.ds(n, 1), lanes])
            to_start = jnp.exp(-rate * seg)
            to_end = jnp.exp(-rate * (steps * (SUBS - 1) - seg))
            state_ref[n, place, :] = jnp.sum(ends[n] * to_end, axis=0, keepdims=True)
            state_ref[modes + n, place, :] = jnp.sum(
                starts[n] * to_start, axis=0, keepdims=True
            )

    each_group(groups, one_group)


def chain_kernel(row_count, half, first_ref, arrived_ref, rate_ref, residue_ref, out_ref):
    blocks, state_rows, _ = arrived_ref.shape
    rate = own_rows(rate_ref, first_ref[0], state_rows)
    step_decay = jnp.exp(-rate * row_count)
    weight = own_rows(residue_ref, first_ref[0], state_rows) * jnp.exp(-rate)

    def run(order):
        def body(index, carry):
            block = order(index)
            out_ref[pl.ds(block, 1)] = (carry * weight)[None]
            return carry * step_decay + arrived_ref[pl.ds(block, 1)][0]

        lax.fori_loop(0, blocks, body, jnp.zeros(rate.shape, F32), unroll=32)

    @pl.when(first_ref[0] < half)
    def _():
        run(lambda index: index)

    @pl.when(first_ref[0] >= half)
    def _():
        run(lambda index: blocks - 1 - index)


def local_kernel(groups, given, gated, gradm, residue_ref, rate_ref, *refs):
    ahead, behind, seg_out, seg_states, sems = refs[given:]
    _, row_count, _ = gated.shape
    modes = rate_ref.shape[0]
    steps = row_count // SUBS
    leaving = slabs(sems, [(seg_states, seg_out)])

    def one_group(group):
        lanes = pl.ds(pl.multiple_of(group * LANES, LANES), LANES)
        weight = [spread(residue_ref[pl.ds(n, 1), lanes]) for n in range(modes)]
        rates = [rate_ref[pl.ds(n, 1), lanes] for n in range(modes)]
        decay = [spread(jnp.exp(-r)) for r in rates]
        zero = jnp.zeros((SUBS, LANES), F32)
        for source, target, backward in ((gated, ahead, False), (gradm, behind, True)):

            def scan_chunk(index, states):
                base = (steps // CHUNK - 1 - index if backward else index) * CHUNK
                values = [source[group, step_rows(base + at), :] for at in range(CHUNK)]
                made = [None] * CHUNK
                for at in range(CHUNK)[:: -1 if backward else 1]:
                    states = [s * d + values[at] for s, d in zip(states, decay)]
                    made[at] = tapped(weight, states)
                for at in range(CHUNK):
                    target[group, step_rows(base + at), :] = made[at]
                return states

            states = lax.fori_loop(0, steps // CHUNK, scan_chunk, [zero] * modes)
            sub = sub_index()
            for n in range(modes):
                span = spread(jnp.exp(-rates[n] * steps))
                total = states[n]
                for shift in (1, 2, 4):
                    if backward:
                        moved = jnp.where(
                            sub < SUBS - shift, pltpu.roll(total, SUBS - shift, 0), 0.0
                        )
                    else:
                        moved = jnp.where(sub >= shift, pltpu.roll(total, shift, 0), 0.0)
                    total = total + span * moved
                    span = span * span
                if backward:
                    enters = jnp.where(sub < SUBS - 1, pltpu.roll(total, SUBS - 1, 0), 0.0)
                else:
                    enters = jnp.where(sub >= 1, pltpu.roll(total, 1, 0), 0.0)
                seg_states[group, int(backward), n] = enters * weight[n] * decay[n]
        start_all(leaving(group))

    each_group(groups, one_group)
    each_group(groups, lambda group: wait_all(leaving(group)))


def grad_kernel(
    share, held_ref, kv_ref, seg_ref, ahead, behind, cot, enter_ref, rate_ref,
    query_mix, key_mix, value_mix, head_ref, short_ref,
    held, kv, seg_states, short, sems,
):
    groups, row_count, _ = cot.shape
    arriving = slabs(
        sems, [(seg_ref, seg_states), (held_ref, held), (kv_ref, kv)]
    )
    each_group(groups, lambda group: start_all(arriving(group)))
    modes = rate_ref.shape[0]
    steps = row_count // SUBS
    lead = held.shape[2] // SUBS - steps
    taps = lead + 1
    mix = (query_mix, key_mix, value_mix)
    short_ref[...] = jnp.zeros(short_ref.shape, F32)
    head_ref[...] = jnp.zeros(head_ref.shape, BF16)

    def one_group(group):
        lanes = pl.ds(pl.multiple_of(group * LANES, LANES), LANES)
        place = pl.ds(group, 1)
        rates = [spread(rate_ref[pl.ds(n, 1), lanes]) for n in range(modes)]
        decay = [jnp.exp(-r) for r in rates]
        seg = sub_index().astype(F32) * steps
        wait_all(arriving(group))
        for backward in (False, True):
            gap = steps * (SUBS - 1) - seg if backward else seg
            carried = []
            for n in range(modes):
                outer = spread(enter_ref[int(backward) * modes + n, place, :])
                inner = seg_states[group, int(backward), n]
                carried.append(inner + jnp.exp(-rates[n] * gap) * outer)
            parts = (1, 2) if backward else (0,)
            def grad_chunk(index, carry):
                carried, sums = carry
                base = (steps // CHUNK - 1 - index if backward else index) * CHUNK
                source = behind if backward else ahead
                long_rows = [None] * CHUNK
                for at in range(CHUNK)[:: -1 if backward else 1]:
                    long_rows[at] = source[group, step_rows(base + at), :] + added(carried)
                    carried = [c * d for c, d in zip(carried, decay)]
                new_sums = []
                for part, old in zip(parts, sums):
                    grads = []
                    for at in range(CHUNK):
                        rows = step_rows(base + at)
                        factor = cot[group, rows, :] if part == 0 else kv[group, 2 - part, rows, :]
                        grads.append(kept(long_rows[at] * factor))
                        mix[part][group, rows, :] = grads[at]
                    window = [
                        held[group, part, step_rows(base + at), :] for at in range(CHUNK + lead)
                    ]
                    new_sums.append(
                        [
                            old[k] + tapped(grads, window[lead - k : lead - k + CHUNK])
                            for k in range(taps)
                        ]
                    )
                return carried, new_sums

            zero = jnp.zeros((SUBS, LANES), F32)
            _, sums = lax.fori_loop(
                0, steps // CHUNK, grad_chunk, (carried, [[zero] * taps for _ in parts])
            )
            for part, taken in zip(parts, sums):
                for k in range(taps):
                    short[part * taps + k, place, :] = jnp.sum(taken[k], axis=0, keepdims=True)
                first = [mix[part][group, pl.ds(step * SUBS, 1), :] for step in range(lead)]
                first += [jnp.zeros((1, LANES), F32)] * (HALO - lead)
                head_ref[part, :, lanes] = jnp.concatenate(first, axis=0).astype(BF16)

    each_group(groups, one_group)
    for piece in range(short_ref.shape[0]):
        for slot in range(share):
            row, group = divmod(piece * share + slot, groups)
            if row < 3 * taps:
                short_ref[piece, slot : slot + 1, :] = short[row, group : group + 1, :]


def back_kernel(
    query_mix, key_mix, value_mix, next_ref, filt_ref, out_ref, late, made, wide, sems
):
    mix = (query_mix, key_mix, value_mix)
    taps = filt_ref.shape[1]
    row_count, channels = made.shape
    groups = channels // LANES
    steps = row_count // SUBS
    perm = step_major(row_count, True)
    late[...] = next_ref[...].astype(F32)
    copies = []
    for part in range(3):

        def one_group(group):
            lanes = pl.ds(pl.multiple_of(group * LANES, LANES), LANES)
            weights = [spread(filt_ref[part, pl.ds(k, 1), lanes]) for k in range(taps)]

            def back_rows(base, window):
                rows = [tapped(weights, window[at : at + taps]) for at in range(CHUNK)]
                made[step_rows(base, CHUNK), lanes] = jnp.concatenate(rows, axis=0).astype(BF16)

            def back_chunk(index, carry):
                base = index * CHUNK
                back_rows(
                    base,
                    [mix[part][group, step_rows(base + at), :] for at in range(CHUNK + taps - 1)],
                )
                return carry

            last = steps - CHUNK
            lax.fori_loop(0, last // CHUNK, back_chunk, 0)
            window = [mix[part][group, step_rows(last + at), :] for at in range(CHUNK)]
            for step in range(taps - 1):
                first = mix[part][group, step_rows(step), :]
                row = late[part, pl.ds(step, 1), lanes]
                window.append(
                    jnp.where(sub_index() == SUBS - 1, spread(row), pltpu.roll(first, SUBS - 1, 0))
                )
            back_rows(last, window)

        each_group(groups, one_group)
        wide[part] = jnp.dot(perm, made[...], preferred_element_type=F32).astype(BF16)
        copies.append(pltpu.make_async_copy(wide.at[part], out_ref.at[part], sems.at[part]))
        copies[-1].start()
    wait_all(copies)


def line_kernel(share, columns, part_ref, out_ref):
    lines = part_ref.shape[0] // columns
    totals = [
        added([part_ref[line * columns + column, :share, :] for line in range(lines)])
        for column in range(columns)
    ]
    totals = jnp.concatenate(totals, axis=0).astype(BF16)
    for plane in range(out_ref.shape[0]):
        out_ref[plane] = totals


def plane_kernel(share, part_ref, out_ref):
    planes, rows, _ = part_ref.shape
    piece_rows = out_ref.shape[1]
    totals = added([part_ref[plane].astype(F32) for plane in range(planes)])
    squares = jnp.sum(totals * totals)
    marks = jnp.full((piece_rows - share, LANES), squares, F32)
    columns = rows // share
    for column in range(columns):
        own = totals[column * share : (column + 1) * share]
        piece = jnp.concatenate([own, marks], axis=0)
        for line in range(out_ref.shape[0] // columns):
            out_ref[line * columns + column] = piece


def scale_kernel(clip_limit, share, sums_ref, out_ref):
    squares = added([sums_ref[piece, share : share + 1, :] for piece in range(sums_ref.shape[0])])
    factor = jnp.minimum(1.0, clip_limit / (jnp.sqrt(squares) + 1e-06))
    _, taps, channels = out_ref.shape
    groups = channels // LANES
    for part in range(3):
        for k in range(taps):
            for group in range(groups):
                piece, row = divmod((part * taps + k) * groups + group, share)
                out_ref[part, k : k + 1, pl.ds(group * LANES, LANES)] = (
                    sums_ref[piece, row : row + 1, :] * factor
                )


def passed_along(shard, by):
    length = lax.axis_size("ctx")
    pairs = [(i, i + by) for i in range(length) if 0 <= i + by < length]
    return lax.ppermute(shard, "ctx", pairs)


def exchange(blocks, axis, members=None):
    return lax.all_to_all(
        blocks, axis, split_axis=0, concat_axis=0, tiled=True, axis_index_groups=members
    )


def cost(flops, bytes_accessed):
    return pl.CostEstimate(flops=flops, bytes_accessed=bytes_accessed, transcendentals=0)


def per_device(inputs, cotangent, short_filter, residue, decay_rate):
    _, row_count, channels = inputs.shape
    taps = short_filter.shape[1]
    modes = residue.shape[0]
    blocks = lax.axis_size("ctx")
    groups = channels // LANES
    lead = taps - 1
    long_rows = row_count + lead * SUBS

    def shaped(dtype, *dims):
        return jax.ShapeDtypeStruct(dims, dtype)

    def near(dtype, *dims):
        return pltpu.VMEM(dims, dtype)

    def far(dtype, *dims):
        return pltpu.HBM(dims, dtype)

    def from_near(*values):
        return [pltpu.with_memory_space_constraint(v, pltpu.VMEM) for v in values]

    def from_far(*values):
        return [pltpu.with_memory_space_constraint(v, pltpu.HBM) for v in values]

    small = pltpu.CompilerParams(vmem_limit_bytes=4 << 20)
    params = pltpu.CompilerParams(vmem_limit_bytes=24 << 20)
    at_vmem = pl.BlockSpec(memory_space=pltpu.VMEM)
    at_hbm = pl.BlockSpec(memory_space=pltpu.HBM)
    sems = pltpu.SemaphoreType.DMA
    work = row_count * channels
    held_dims = (groups, 3, long_rows, LANES)
    part_dims = (groups, 3, row_count, LANES)
    row_dims = (groups, row_count, LANES)
    kv_dims = (groups, 2, row_count, LANES)
    seg_dims = (groups, 2, modes, SUBS, LANES)

    state_rows = 2 * modes * groups // blocks
    first = lax.axis_index("ctx") * state_rows
    half = modes * groups

    held, cot_held, filt, rate, weight = pl.pallas_call(
        load_kernel,
        in_specs=[at_hbm] * 5,
        out_specs=[at_vmem] * 5,
        out_shape=[
            near(F32, *part_dims),
            near(F32, *row_dims),
            near(F32, 3, taps, channels),
            near(F32, modes, channels),
            near(F32, modes, channels),
        ],
        scratch_shapes=[pltpu.VMEM((4, row_count, channels), BF16), sems((4,)), sems((3,))],
        compiler_params=params,
        cost_estimate=cost(work * 2000, work * 8),
        name="load",
    )(*from_far(inputs, cotangent, short_filter, decay_rate, residue))
    prev = passed_along(inputs[:, row_count - HALO :, :], 1)
    prev, held, cot_held = lax.optimization_barrier((prev, held, cot_held))
    gated, gradm, states = pl.pallas_call(
        mix_kernel,
        in_specs=[at_vmem] * 5,
        out_specs=[at_vmem] * 3,
        out_shape=[
            near(F32, *row_dims),
            near(F32, *row_dims),
            far(F32, 2 * modes, groups, LANES),
        ],
        scratch_shapes=[pltpu.VMEM((3, HALO, channels), F32)],
        compiler_params=params,
        cost_estimate=cost(work * 110, work * 24),
        name="mix",
    )(*from_near(held), prev, *from_near(cot_held, filt, rate))

    arrived = exchange(states.reshape(blocks, state_rows, LANES), "ctx")
    held, kv = pl.pallas_call(
        stage_kernel,
        in_specs=[at_hbm] * 2 + [at_vmem],
        out_specs=[at_hbm] * 2,
        out_shape=[far(F32, *held_dims), far(F32, *kv_dims)],
        scratch_shapes=[
            pltpu.VMEM(held_dims, F32),
            pltpu.VMEM(kv_dims, F32),
            pltpu.VMEM((3, taps, channels), F32),
            pltpu.VMEM((3, HALO, channels), F32),
            pltpu.VMEM((3, row_count, channels), BF16),
            sems((3,)),
            sems((1,)),
            sems((2, groups)),
        ],
        compiler_params=params,
        cost_estimate=cost(work * 2000, work * 18),
        name="stage",
    )(*from_far(inputs, short_filter), prev)
    def local_sums(span, gated, gradm, seg_states=None):
        seg = [] if seg_states is None else from_far(seg_states)
        return pl.pallas_call(
            functools.partial(local_kernel, span, len(seg)),
            in_specs=[at_vmem] * 4 + [at_hbm] * len(seg),
            out_specs=[at_vmem] * 2 + [at_hbm],
            out_shape=[near(F32, *row_dims), near(F32, *row_dims), far(F32, *seg_dims)],
            scratch_shapes=[pltpu.VMEM(seg_dims, F32), sems((1, groups))],
            input_output_aliases={0: 0, 1: 1, **({4: 2} if seg else {})},
            compiler_params=params,
            cost_estimate=cost(work * 16 * (span[1] - span[0]), work * 18),
            name="local",
        )(*from_near(gated, gradm, weight, rate), *seg)

    early_groups = groups // 8
    if early_groups:
        ahead, behind, seg_states = local_sums((0, early_groups), gated, gradm)
        arrived, held, kv, seg_states = lax.optimization_barrier((arrived, held, kv, seg_states))
    else:
        ahead, behind, seg_states = gated, gradm, None
        arrived, held, kv = lax.optimization_barrier((arrived, held, kv))

    entering = pl.pallas_call(
        functools.partial(chain_kernel, row_count, half),
        in_specs=[
            pl.BlockSpec(memory_space=pltpu.SMEM),
            at_vmem,
            at_vmem,
            at_vmem,
        ],
        out_specs=at_vmem,
        out_shape=shaped(F32, blocks, state_rows, LANES),
        compiler_params=small,
        cost_estimate=cost(blocks * state_rows * LANES * 2, blocks * state_rows * LANES * 8),
        name="chain",
    )(first[None], arrived, *from_near(rate, weight))
    entering = exchange(entering, "ctx").reshape(2 * modes, groups, LANES)

    ahead, behind, seg_states = local_sums((early_groups, groups), ahead, behind, seg_states)
    entering, seg_states = lax.optimization_barrier((entering, seg_states))

    tp_count = lax.axis_size("tp")
    planes = blocks // LINES
    in_plane = LINES * tp_count
    share = -(-3 * taps * groups // in_plane)
    piece_rows = -(-(share + 1) // SUBS) * SUBS
    plane_members = [
        [(y * planes + z) * tp_count + m for y in range(LINES) for m in range(tp_count)]
        for z in range(planes)
    ]
    line_members = [[y * planes + z for z in range(planes)] for y in range(LINES)]
    *grad_mix, head, short_part = pl.pallas_call(
        functools.partial(grad_kernel, share),
        in_specs=[at_hbm] * 3 + [at_vmem] * 5,
        out_specs=[at_vmem] * 5,
        out_shape=[
            near(F32, *row_dims),
            near(F32, *row_dims),
            near(F32, *row_dims),
            shaped(BF16, 3, HALO, channels),
            far(F32, in_plane, piece_rows, LANES),
        ],
        scratch_shapes=[
            pltpu.VMEM(held_dims, F32),
            pltpu.VMEM(kv_dims, F32),
            pltpu.VMEM(seg_dims, F32),
            pltpu.VMEM((3 * taps, groups, LANES), F32),
            sems((3, groups)),
        ],
        input_output_aliases={3: 0, 4: 1, 5: 2},
        compiler_params=params,
        cost_estimate=cost(work * 110, work * 30),
        name="grad",
    )(
        *from_far(held, kv, seg_states), *from_near(ahead, behind, cot_held), entering, rate
    )

    gathered = exchange(short_part, ("ctx", "tp"), plane_members)
    late = passed_along(head, -1)
    own_sum = pl.pallas_call(
        functools.partial(line_kernel, share, tp_count),
        in_specs=[at_vmem],
        out_specs=at_vmem,
        out_shape=shaped(BF16, planes, tp_count * share, LANES),
        compiler_params=small,
        name="line",
    )(gathered)
    own_sum, late = lax.optimization_barrier((own_sum, late))
    all_sums = exchange(own_sum, "ctx", line_members)
    grad_inputs = pl.pallas_call(
        back_kernel,
        in_specs=[at_vmem] * 5,
        out_specs=at_hbm,
        out_shape=far(BF16, 3, row_count, channels),
        scratch_shapes=[
            pltpu.VMEM((3, HALO, channels), F32),
            pltpu.VMEM((row_count, channels), BF16),
            pltpu.VMEM((3, row_count, channels), BF16),
            sems((3,)),
        ],
        compiler_params=params,
        cost_estimate=cost(work * 48, work * 12),
        name="back",
    )(*from_near(*grad_mix), late, *from_near(filt))
    all_sums, grad_inputs = lax.optimization_barrier((all_sums, grad_inputs))
    all_sums = pl.pallas_call(
        functools.partial(plane_kernel, share),
        in_specs=[at_vmem],
        out_specs=at_vmem,
        out_shape=shaped(F32, in_plane, piece_rows, LANES),
        compiler_params=small,
        name="plane",
    )(all_sums)
    all_sums = exchange(all_sums, ("ctx", "tp"), plane_members)
    clip_limit = math.sqrt(3 * channels * tp_count * taps)
    grad_short = pl.pallas_call(
        functools.partial(scale_kernel, clip_limit, share),
        in_specs=[at_vmem],
        out_specs=at_vmem,
        out_shape=shaped(F32, 3, taps, channels),
        compiler_params=small,
        name="scale",
    )(all_sums)
    return (grad_inputs, grad_short)


def solution(mesh):
    return jax.shard_map(
        per_device,
        mesh=mesh,
        in_specs=(
            P(None, "ctx", "tp"),
            P("ctx", "tp"),
            P(None, None, "tp"),
            P(None, "tp"),
            P(None, "tp"),
        ),
        out_specs=(P(None, "ctx", "tp"), P(None, None, "tp")),
        check_vma=False,
    )
```
